32 devices in a mesh: dp: 4 (over z), ctx: 4 (over x, core), expert: 2 (over y).
Axes of the slice: x: 2, y: 2, z: 4, core: 2. Of those that a mesh axis runs over, the one named last changes fastest.
Arguments:
- x_prompt: bfloat16 [8, 1024, 1536], P(('dp', 'expert'), 'ctx'), may hold values from -6 to 6
- x_cont: bfloat16 [8, 4, 256, 1536], P(('dp', 'expert'), 'ctx'), may hold values from -6 to 6
- norm1_gain: bfloat16 [1536], replicated, may hold values from 0.099609375 to 1.8984375
- w_query: bfloat16 [1536, 1536], replicated, may hold values from -0.625 to 0.625
- key_weight: bfloat16 [1536, 512], replicated, may hold values from -0.625 to 0.625
- value_weight: bfloat16 [1536, 512], replicated, may hold values from -0.15625 to 0.15625
- w_out: bfloat16 [1536, 1536], replicated, may hold values from -3 to 3
- norm2_gain: bfloat16 [1536], replicated, may hold values from 0.099609375 to 1.8984375
- w_router: bfloat16 [1536, 40], replicated, may hold values from -0.078125 to 0.078125
- w_gate_up: bfloat16 [40, 1536, 1024], P('expert'), may hold values from -0.15625 to 0.15625
- w_down: bfloat16 [40, 512, 1536], P('expert'), may hold values from -6 to 6
- routes_prompt: int32 [8, 1024, 8], P(('dp', 'expert'), 'ctx'), may hold values from 0 to 39, all different within a row
- routes_cont: int32 [8, 4, 256, 8], P(('dp', 'expert'), 'ctx'), may hold values from 0 to 39, all different within a row
- slot_order: int32 [8, 4, 512], P(('dp', 'expert'), 'ctx'), may hold values from 0 to 511, each once within a row
- dy_prompt: bfloat16 [8, 1024, 1536], P(('dp', 'expert'), 'ctx'), may hold values from -6 to 6
- dy_cont: bfloat16 [8, 4, 256, 1536], P(('dp', 'expert'), 'ctx'), may hold values from -6 to 6
Outputs:
- y_prompt: bfloat16 [8, 1024, 1536], P(('dp', 'expert'), 'ctx')
- y_cont: bfloat16 [8, 4, 256, 1536], P(('dp', 'expert'), 'ctx')
- dx_prompt: float32 [8, 1024, 1536], P(('dp', 'expert'), 'ctx')
- dx_cont: float32 [8, 4, 256, 1536], P(('dp', 'expert'), 'ctx')
- grad_norm1: float32 [1536], P(('dp', 'ctx'))
- grad_query: float32 [1536, 1536], P(('dp', 'ctx'))
- grad_key: float32 [1536, 512], P(('dp', 'ctx'))
- grad_value: float32 [1536, 512], P(('dp', 'ctx'))
- grad_out: float32 [1536, 1536], P(('dp', 'ctx'))
- grad_norm2: float32 [1536], P(('dp', 'ctx'))
- grad_router: float32 [1536, 40], P(('dp', 'ctx'))
- grad_gate_up: float32 [40, 1536, 1024], P('expert', ('dp', 'ctx'))
- grad_down: float32 [40, 512, 1536], P('expert', ('dp', 'ctx'))
The draws below stay inside these ranges and needn't reach their ends.
Inputs may be any that keep to these rules, and one draw needn't show every extreme that they name: `routes_prompt`: each token names 8 different experts. `routes_cont`: each token names 8 different experts. slot_order[s, c] lists each of the block's 512 tokens once.
All inputs are finite; a program needn't handle non-finite values.
Results may differ from the reference program's by a relative error of at most 0.025.
Values may be sent and summed in bfloat16 or wider, within the bound.
No kernel may reach another device: no remote copies, remote signals or barrier semaphores. Data moves between devices by JAX's collectives and lax.ppermute only.
A program may use at most 448 MiB of HBM per device.

```python
from functools import partial
import jax
import jax.numpy as jnp
import numpy as np
from jax import lax

MODEL_WIDTH = 1536
QUERY_HEADS = 24
KEY_VALUE_HEADS = 8
HEAD_SIZE = 64
FF = 512
EXPERTS = 40
TOPK = 8
PROMPT = 1024
CONT_LEN = 256
CONT_DEV = 1
SHARDS = 8
CONT_N = 4
TOK_DEV = 512
CAP = 103
N_CTX = 4


def block_levels(key, shape, cuts, least, largest):
    gain = 1.0
    for axis_at, parts in cuts:
        steps = jax.random.uniform(jax.random.fold_in(jax.random.fold_in(key, 6), axis_at), (parts,), jnp.float32, least / len(cuts), largest / len(cuts))
        gain = gain * jnp.repeat(jnp.exp(steps), shape[axis_at] // parts).reshape((-1,) + (1,) * (len(shape) - 1 - axis_at))
    return gain


def different_ones(key, rows, count, top, lift):
    order = jax.random.permutation(jax.random.fold_in(key, 1), count)
    boost = order
    for power in range(3):
        boost = boost * boost // count
    boost = boost * lift // count
    lots = jax.random.randint(jax.random.fold_in(key, 2), (rows, count), 0, 4096) + boost
    fixed_rows = jax.random.permutation(jax.random.fold_in(key, 3), rows)[jnp.arange(count) % rows]
    lots = jnp.where(jnp.arange(rows)[:, None] == fixed_rows[None, :], 1 << 14, lots)
    merit = lots * count + jnp.arange(count)
    return lax.top_k(merit.astype(jnp.int32), top)[1].astype(jnp.int32)


def scatter_about(rng, dims, scale, most, split=(), held_as=jnp.bfloat16):
    array = scale * jax.random.normal(rng, dims, jnp.float32)
    if split:
        array = array * block_levels(rng, dims, split, -0.22, 0.18)
    return jnp.clip(array, -most, most).astype(held_as)


def setup_inputs(seed: int = 0) -> dict:
    splits = jax.random.split(jax.random.key(seed), 17)
    return {
        "x_prompt": scatter_about(splits[0], (SHARDS, PROMPT, MODEL_WIDTH), 1.0, 6.0, ((0, 8), (1, 4))),
        "x_cont": scatter_about(splits[1], (SHARDS, CONT_N, CONT_LEN, MODEL_WIDTH), 1.0, 6.0, ((0, 8), (1, 4))),
        "norm1_gain": jnp.clip(1.0 + 0.18 * jax.random.normal(splits[2], (MODEL_WIDTH,), jnp.float32), 0.099609375, 1.8984375).astype(jnp.bfloat16),
        "w_query": scatter_about(splits[3], (MODEL_WIDTH, QUERY_HEADS * HEAD_SIZE), (MODEL_WIDTH // 16) ** -0.5, 0.625),
        "key_weight": scatter_about(splits[4], (MODEL_WIDTH, KEY_VALUE_HEADS * HEAD_SIZE), (MODEL_WIDTH // 16) ** -0.5, 0.625),
        "value_weight": scatter_about(splits[5], (MODEL_WIDTH, KEY_VALUE_HEADS * HEAD_SIZE), MODEL_WIDTH ** -0.5, 0.15625),
        "w_out": scatter_about(splits[6], (QUERY_HEADS * HEAD_SIZE, MODEL_WIDTH), (max(MODEL_WIDTH // 384, 1)) ** -0.5, 3.0),
        "norm2_gain": jnp.clip(1.0 + 0.18 * jax.random.normal(splits[7], (MODEL_WIDTH,), jnp.float32), 0.099609375, 1.8984375).astype(jnp.bfloat16),
        "w_router": scatter_about(splits[8], (MODEL_WIDTH, EXPERTS), (4 * MODEL_WIDTH) ** -0.5, 0.078125),
        "w_gate_up": scatter_about(splits[9], (EXPERTS, MODEL_WIDTH, 2 * FF), MODEL_WIDTH ** -0.5, 0.15625, ((0, 2),)),
        "w_down": scatter_about(splits[10], (EXPERTS, FF, MODEL_WIDTH), (max(FF // 512, 1)) ** -0.5, 6.0, ((0, 2),)),
        "routes_prompt": different_ones(splits[11], SHARDS * PROMPT, EXPERTS, TOPK, 1638).reshape((SHARDS, PROMPT, TOPK)),
        "routes_cont": different_ones(splits[12], SHARDS * CONT_N * CONT_LEN, EXPERTS, TOPK, 1638).reshape((SHARDS, CONT_N, CONT_LEN, TOPK)),
        "slot_order": jax.vmap(lambda own: jax.random.permutation(own, TOK_DEV))(jax.random.split(splits[13], SHARDS * N_CTX)).reshape((SHARDS, N_CTX, TOK_DEV)).astype(jnp.int32),
        "dy_prompt": scatter_about(splits[14], (SHARDS, PROMPT, MODEL_WIDTH), 1.0, 6.0, ((0, 8), (1, 4))),
        "dy_cont": scatter_about(splits[15], (SHARDS, CONT_N, CONT_LEN, MODEL_WIDTH), 1.0, 6.0, ((0, 8), (1, 4))),
    }


EPS = 1e-06
RESID = 0.22
ATT_SCALE = 0.015625
THETA = 10000.0
NEG = -1e+30
HIGHEST = lax.Precision.HIGHEST

@jax.custom_vjp
def reduced_precision(v):
    return lax.optimization_barrier(v.astype(jnp.bfloat16)).astype(jnp.float32)

@jax.custom_vjp
def low_back(v):
    return v

def low_keep(v):
    return (reduced_precision(v), None)

def low_pass(kept, grad):
    return (grad,)

def back_keep(v):
    return (v, None)

def back_low(kept, grad):
    return (reduced_precision(grad),)
reduced_precision.defvjp(low_keep, low_pass)
low_back.defvjp(back_keep, back_low)

def exact_dot(left, right):
    return jnp.dot(left, right, precision=HIGHEST)

def rope_tables(positions, head_dim):
    half_dim = head_dim // 2
    frequency = THETA ** (-(jnp.arange(half_dim, dtype=jnp.float32) * 2.0 / head_dim))
    angles = positions[:, None] * frequency[None, :]
    cosine_lookup = jnp.concatenate([jnp.cos(angles), jnp.cos(angles)], axis=-1)
    sine_lookup = jnp.concatenate([jnp.sin(angles), jnp.sin(angles)], axis=-1)
    return (cosine_lookup, sine_lookup)

def apply_rotary(values, cosine_lookup, sine_lookup, sign):
    half_dim = values.shape[-1] // 2
    turned = jnp.concatenate([-values[..., half_dim:], values[..., :half_dim]], axis=-1)
    return values * cosine_lookup[:, None, :] + sign * turned * sine_lookup[:, None, :]

def rms_scale(values):
    return lax.rsqrt(lax.optimization_barrier(jnp.mean(values * values, axis=-1, keepdims=True)) + EPS)

def slot_tables(routes, visit_order, experts, capacity):
    count_of_tokens, top_count = routes.shape
    ordered = routes[visit_order]
    hit_table = (ordered[:, :, None] == jnp.arange(experts, dtype=jnp.int32)[None, None, :]).astype(jnp.int32)
    counts = lax.optimization_barrier(jnp.sum(hit_table, axis=1, dtype=jnp.int32))
    before = jnp.cumsum(counts, axis=0, dtype=jnp.int32) - counts
    slot_rank = lax.optimization_barrier(jnp.sum(hit_table * before[:, None, :], axis=2, dtype=jnp.int32))
    slot_total = experts * capacity
    flat_ordered = jnp.where(slot_rank < capacity, ordered * capacity + slot_rank, slot_total).astype(jnp.int32)
    flat = jnp.zeros((count_of_tokens, top_count), jnp.int32).at[visit_order].set(flat_ordered)
    owners = jnp.repeat(visit_order, top_count).astype(jnp.int32)
    token_slot = jnp.full((slot_total + 1,), count_of_tokens, jnp.int32).at[flat_ordered.reshape(-1)].set(owners)[:slot_total]
    return (flat, token_slot)

def take_rows(row_table, row_index):
    return row_table[row_index]

def attend_group(allowed, pieces):
    query_row_block, key_row_block, value_row_block = pieces
    scores = low_back(jnp.einsum('trd,kd->trk', query_row_block, key_row_block, precision=HIGHEST) * ATT_SCALE)
    scores = jnp.where(allowed[:, None, :], scores, NEG)
    weights = reduced_precision(jax.nn.softmax(scores, axis=-1))
    return jnp.einsum('trk,kd->trd', weights, value_row_block, precision=HIGHEST)

def layer(params, prompt_rows, cont_rows, flat, token_slot, routes, context):
    gain_one, w_query, key_weight, value_weight, w_out, gain_two, w_router, w_gate_up, w_down = params
    cosine_lookup, sine_lookup, allowed, block_rows, inverse_rows = context
    model_width = prompt_rows.shape[-1]
    tokens = jnp.concatenate([prompt_rows, cont_rows.reshape(-1, model_width)], axis=0)
    count_of_tokens = tokens.shape[0]
    normed_one = reduced_precision(tokens * rms_scale(tokens) * gain_one)
    q_lin = low_back(exact_dot(normed_one, w_query))
    key_linear = low_back(exact_dot(normed_one, key_weight))
    value_linear = low_back(exact_dot(normed_one, value_weight))
    query_row_block = reduced_precision(apply_rotary(q_lin.reshape(count_of_tokens, QUERY_HEADS, HEAD_SIZE), cosine_lookup, sine_lookup, 1.0))
    key_row_block = reduced_precision(apply_rotary(key_linear.reshape(count_of_tokens, KEY_VALUE_HEADS, HEAD_SIZE), cosine_lookup, sine_lookup, 1.0))
    value_row_block = reduced_precision(value_linear).reshape(count_of_tokens, KEY_VALUE_HEADS, HEAD_SIZE)
    queries_per_group = QUERY_HEADS // KEY_VALUE_HEADS
    grouped_query = query_row_block.reshape(count_of_tokens, KEY_VALUE_HEADS, queries_per_group, HEAD_SIZE).transpose(1, 0, 2, 3)
    attended = lax.map(jax.checkpoint(partial(attend_group, allowed)), (grouped_query, key_row_block.transpose(1, 0, 2), value_row_block.transpose(1, 0, 2)))
    merged = attended.transpose(1, 0, 2, 3).reshape(count_of_tokens, QUERY_HEADS * HEAD_SIZE)
    merged = low_back(reduced_precision(merged))
    branch = low_back(exact_dot(merged, w_out))
    resid = tokens + RESID * branch
    normed_two = reduced_precision(resid * rms_scale(resid) * gain_two)
    logits = low_back(exact_dot(normed_two, w_router))
    gates = jax.nn.softmax(jnp.take_along_axis(logits, routes, axis=-1), axis=-1)
    blocked = normed_two[block_rows]
    padded = jnp.concatenate([blocked, jnp.zeros((N_CTX, 1, model_width), jnp.float32)], axis=1)
    inputs = low_back(jax.vmap(take_rows)(padded, token_slot)).reshape(N_CTX, EXPERTS, CAP, model_width)
    both = low_back(jnp.einsum('becd,edf->becf', inputs, w_gate_up, precision=HIGHEST))
    hidden = reduced_precision(jax.nn.silu(both[..., :FF]) * both[..., FF:])
    expert_out = low_back(reduced_precision(jnp.einsum('becf,efd->becd', hidden, w_down, precision=HIGHEST)))
    flat_out = jnp.concatenate([expert_out.reshape(N_CTX, EXPERTS * CAP, model_width), jnp.zeros((N_CTX, 1, model_width), jnp.float32)], axis=1)
    pairs = jax.vmap(take_rows)(flat_out, flat)
    gates_blocked = gates[block_rows]
    mixed = jnp.einsum('btk,btkd->btd', gates_blocked, pairs, precision=HIGHEST).reshape(-1, model_width)[inverse_rows]
    output = resid + RESID * mixed
    return (output[:PROMPT], output[PROMPT:].reshape(CONT_N, CONT_LEN, model_width))

def reference(x_prompt, x_cont, norm1_gain, w_query, key_weight, value_weight, w_out, norm2_gain, w_router, w_gate_up, w_down, routes_prompt, routes_cont, slot_order, dy_prompt, dy_cont):
    params = tuple((member.astype(jnp.float32) for member in (norm1_gain, w_query, key_weight, value_weight, w_out, norm2_gain, w_router, w_gate_up, w_down)))
    shard_tokens = PROMPT + CONT_N * CONT_LEN
    index_all = np.arange(shard_tokens)
    in_cont = index_all >= PROMPT
    offset = index_all - PROMPT
    positions = np.where(in_cont, PROMPT + offset % CONT_LEN, index_all)
    cont_ids = np.where(in_cont, offset // CONT_LEN, -1)
    seen = positions[None, :] <= positions[:, None]
    allowed = (cont_ids[None, :] < 0) & ((cont_ids[:, None] >= 0) | seen) | (cont_ids[None, :] >= 0) & (cont_ids[None, :] == cont_ids[:, None]) & seen
    cosine_lookup, sine_lookup = rope_tables(jnp.asarray(positions).astype(jnp.float32), HEAD_SIZE)
    prompt_part = PROMPT // N_CTX
    cont_part = CONT_DEV * CONT_LEN
    block_list = [np.concatenate([ctx_pos * prompt_part + np.arange(prompt_part), PROMPT + ctx_pos * cont_part + np.arange(cont_part)]) for ctx_pos in range(N_CTX)]
    block_rows = np.stack(block_list).astype(np.int32)
    inverse_rows = np.argsort(block_rows.reshape(-1)).astype(np.int32)
    context = (cosine_lookup, sine_lookup, jnp.asarray(allowed), jnp.asarray(block_rows), jnp.asarray(inverse_rows))
    block_index = jnp.asarray(block_rows)

    def one_shard(totals, inputs):
        prompt_in, cont_in, prompt_routes, cont_routes, visit_order, prompt_grad, cont_grad = inputs
        routes = jnp.concatenate([prompt_routes, cont_routes.reshape(-1, TOPK)], axis=0)
        routes_blocked = routes[block_index]
        flat, token_slot = jax.vmap(partial(slot_tables, experts=EXPERTS, capacity=CAP))(routes_blocked, visit_order)

        def forward(weights, prompt_rows, cont_rows):
            return layer(weights, prompt_rows, cont_rows, flat, token_slot, routes, context)
        outputs, pullback = jax.vjp(forward, params, prompt_in.astype(jnp.float32), cont_in.astype(jnp.float32))
        grads, d_prompt, d_cont = pullback((prompt_grad.astype(jnp.float32), cont_grad.astype(jnp.float32)))
        totals = jax.tree.map(jnp.add, totals, grads)
        return (totals, (outputs[0].astype(jnp.bfloat16), outputs[1].astype(jnp.bfloat16), d_prompt, d_cont))
    zeros = tuple((jnp.zeros_like(member) for member in params))
    totals, stacked = lax.scan(one_shard, zeros, (x_prompt, x_cont, routes_prompt, routes_cont, slot_order, dy_prompt, dy_cont))
    return (stacked[0], stacked[1], stacked[2], stacked[3], totals[0], totals[1], totals[2], totals[3], totals[4], totals[5], totals[6], totals[7], totals[8])
```

```python
from functools import partial

import jax
import jax.numpy as jnp
from jax import lax
from jax.experimental import pallas as pl
from jax.experimental.pallas import tpu as pltpu
from jax.sharding import PartitionSpec as P

QUERY_HEADS = 24
KEY_VALUE_HEADS = 8
HEAD_SIZE = 64


EPS = 1e-06
RESID = 0.22
ATT_SCALE = 0.015625
THETA = 10000.0
NEG = -1e30


def rope_tables(positions, head_dim):
    half_dim = head_dim // 2
    frequency = THETA ** (-(jnp.arange(half_dim, dtype=jnp.float32) * 2.0 / head_dim))
    angles = positions[:, None] * frequency[None, :]
    cosine_lookup = jnp.concatenate([jnp.cos(angles), jnp.cos(angles)], axis=-1)
    sine_lookup = jnp.concatenate([jnp.sin(angles), jnp.sin(angles)], axis=-1)
    return (cosine_lookup, sine_lookup)


def apply_rotary(values, cosine_lookup, sine_lookup, sign):
    half_dim = values.shape[-1] // 2
    turned = jnp.concatenate([-values[..., half_dim:], values[..., :half_dim]], axis=-1)
    return values * cosine_lookup[:, None, :] + sign * turned * sine_lookup[:, None, :]


def rms_forward(values, norm_gain):
    inverse = lax.rsqrt(jnp.mean(values * values, axis=-1, keepdims=True) + EPS)
    return (values * inverse * norm_gain, inverse)


def rms_backward(values, inverse, norm_gain, upstream):
    normed = values * inverse
    weighted = upstream * norm_gain
    projected = jnp.mean(weighted * normed, axis=-1, keepdims=True)
    return (inverse * (weighted - normed * projected), jnp.sum(upstream * normed, axis=0))


def slot_codes(routes, visit_order, experts, capacity):
    count = routes.shape[0]
    ids = jnp.arange(count, dtype=jnp.int32)
    visit = jnp.arange(count, dtype=jnp.float32)
    place = (visit_order[:, None] == ids[None, :]).astype(jnp.float32)
    place_row = jnp.sum(place * visit[:, None], axis=0)
    place_col = jnp.sum((visit_order[None, :] == ids[:, None]).astype(jnp.float32) * visit[None, :], axis=1)
    earlier = (place_col[:, None] < place_row[None, :]).astype(jnp.bfloat16)
    named = jnp.any(
        routes.T[None, :, :] == jnp.arange(experts, dtype=jnp.int32)[:, None, None], axis=1
    )
    rank = jnp.dot(named.astype(jnp.bfloat16), earlier, preferred_element_type=jnp.float32)
    return jnp.where(named, jnp.where(rank < capacity, rank, -1.0), -2.0)


def selection(codes, own, slots):
    tokens = codes.shape[-1]
    slot_index = lax.broadcasted_iota(jnp.int32, (slots, tokens), 0).astype(jnp.float32)
    picks = [
        jnp.where(codes[e : e + 1, :] == slot_index, 1.0, 0.0).astype(jnp.bfloat16)
        for e in range(own)
    ]
    return jnp.concatenate(picks, axis=0)


def dispatch_body(own, slots, codes_ref, rows_ref, out_ref):
    pick = selection(codes_ref[0], own, slots)
    moved = jnp.dot(pick, rows_ref[0], preferred_element_type=jnp.float32).astype(jnp.bfloat16)
    for e in range(own):
        out_ref[e] = moved[e * slots : (e + 1) * slots]


def dispatch(codes, rows, own, slots):
    blocks, tokens, width = rows.shape
    return pl.pallas_call(
        partial(dispatch_body, own, slots),
        grid=(blocks,),
        in_specs=[
            pl.BlockSpec((1, codes.shape[1], tokens), lambda b: (b, 0, 0)),
            pl.BlockSpec((1, tokens, width), lambda b: (b, 0, 0)),
        ],
        out_specs=pl.BlockSpec((own, slots, width), lambda b: (0, b, 0)),
        out_shape=jax.ShapeDtypeStruct((own, blocks * slots, width), jnp.bfloat16),
        cost_estimate=pl.CostEstimate(
            flops=2 * blocks * own * slots * tokens * width,
            transcendentals=0,
            bytes_accessed=2 * blocks * (tokens + own * slots) * width,
        ),
        name="dispatch",
    )(codes, rows)


def combine_body(own, slots, codes_ref, rows_ref, out_ref):
    pick = selection(codes_ref[0], own, slots)
    rows = rows_ref[...].reshape(own * slots, rows_ref.shape[-1])
    out_ref[0] = lax.dot_general(
        pick, rows, (((0,), (0,)), ((), ())), preferred_element_type=jnp.float32
    ).astype(out_ref.dtype)


def combine(codes, rows, own, slots):
    blocks, tokens = codes.shape[0], codes.shape[2]
    width = rows.shape[-1]
    return pl.pallas_call(
        partial(combine_body, own, slots),
        grid=(blocks,),
        in_specs=[
            pl.BlockSpec((1, codes.shape[1], tokens), lambda b: (b, 0, 0)),
            pl.BlockSpec((own, slots, width), lambda b: (0, b, 0)),
        ],
        out_specs=pl.BlockSpec((1, tokens, width), lambda b: (b, 0, 0)),
        out_shape=jax.ShapeDtypeStruct((blocks, tokens, width), jnp.bfloat16),
        cost_estimate=pl.CostEstimate(
            flops=2 * blocks * own * slots * tokens * width,
            transcendentals=0,
            bytes_accessed=2 * blocks * (tokens + own * slots) * width,
        ),
        name="combine",
    )(codes, rows)


def attend_forward(allowed, pieces):
    query_row_block, key_row_block, value_row_block = pieces
    scores = (
        jnp.einsum(
            "trd,kd->trk", query_row_block, key_row_block, preferred_element_type=jnp.float32
        )
        * ATT_SCALE
    )
    scores = jnp.where(allowed[:, None, :], scores, NEG)
    highest = jnp.max(scores, axis=-1, keepdims=True)
    lifted = jnp.exp(scores - highest)
    summed = jnp.sum(lifted, axis=-1, keepdims=True)
    weights = (lifted / summed).astype(jnp.bfloat16)
    result = jnp.einsum("trk,kd->trd", weights, value_row_block, preferred_element_type=jnp.float32)
    return (result, highest[..., 0] + jnp.log(summed[..., 0]))


def attend_backward(allowed, pieces):
    query_row_block, key_row_block, value_row_block, d_out, out_rows, log_total = pieces
    scores = (
        jnp.einsum(
            "trd,kd->trk", query_row_block, key_row_block, preferred_element_type=jnp.float32
        )
        * ATT_SCALE
    )
    scores = jnp.where(allowed[:, None, :], scores, NEG)
    weights = jnp.exp(scores - log_total[..., None])
    d_weights = jnp.einsum(
        "trd,kd->trk", d_out, value_row_block, preferred_element_type=jnp.float32
    )
    centre = jnp.sum(d_out.astype(jnp.float32) * out_rows, axis=-1, keepdims=True)
    d_scores = (weights * (d_weights - centre)).astype(jnp.bfloat16)
    d_query = (
        jnp.einsum("trk,kd->trd", d_scores, key_row_block, preferred_element_type=jnp.float32)
        * ATT_SCALE
    )
    d_key = (
        jnp.einsum("trk,trd->kd", d_scores, query_row_block, preferred_element_type=jnp.float32)
        * ATT_SCALE
    )
    d_value = jnp.einsum(
        "trk,trd->kd", weights.astype(jnp.bfloat16), d_out, preferred_element_type=jnp.float32
    )
    return (d_query, d_key, d_value)


def reduce_experts(grad, split):
    if split == 1:
        return lax.psum_scatter(
            grad, ("dp", "ctx"), scatter_dimension=1, tiled=True
        ).astype(jnp.float32)
    part = lax.psum_scatter(grad, "dp", scatter_dimension=1, tiled=True)
    return lax.all_to_all(part, "ctx", split_axis=1, concat_axis=0, tiled=True).astype(jnp.float32)


def per_device(
    x_prompt,
    x_cont,
    norm1_gain,
    w_query,
    key_weight,
    value_weight,
    w_out,
    norm2_gain,
    w_router,
    w_gate_up,
    w_down,
    routes_prompt,
    routes_cont,
    slot_order,
    dy_prompt,
    dy_cont,
):
    model_width = x_prompt.shape[2]
    prompt_rows = x_prompt.shape[1]
    cont_count = x_cont.shape[1]
    cont_len = x_cont.shape[2]
    cont_rows = cont_count * cont_len
    count_of_tokens = prompt_rows + cont_rows
    queries_per_group = QUERY_HEADS // KEY_VALUE_HEADS
    key_value_width = KEY_VALUE_HEADS * HEAD_SIZE
    local_experts = w_gate_up.shape[0]
    expert_groups = lax.axis_size("expert")
    expert_total = local_experts * expert_groups
    top_count = routes_prompt.shape[2]
    capacity = (count_of_tokens * top_count + expert_total - 1) // expert_total
    hidden_units = w_down.shape[1]
    prompt_total = prompt_rows * lax.axis_size("ctx")
    count_of_keys = prompt_total + cont_rows
    split = lax.axis_size("ctx") if local_experts % lax.axis_size("ctx") == 0 else 1
    own = local_experts // split
    blocks = split * expert_groups
    slots = -(-capacity // 8) * 8
    group = ("ctx", "expert") if split > 1 else ("expert",)
    block_index = lax.axis_index(group)
    own_offset = lax.axis_index("ctx") * own if split > 1 else 0
    first_expert = lax.axis_index("expert") * local_experts + own_offset
    gate_up_own = w_gate_up
    down_own = w_down
    if split > 1:
        gate_up_own = lax.dynamic_slice_in_dim(w_gate_up, own_offset, own, axis=0)
        down_own = lax.dynamic_slice_in_dim(w_down, own_offset, own, axis=0)
    routes = jnp.concatenate(
        [routes_prompt[0], routes_cont[0].reshape(cont_rows, top_count)], axis=0
    )
    codes_all = lax.all_gather(
        slot_codes(routes, slot_order[0, 0], expert_total, capacity), group, axis=0, tiled=False
    )
    own_codes = lax.dynamic_slice_in_dim(codes_all, first_expert, own, axis=1)
    own_codes = jnp.pad(own_codes, ((0, 0), (0, -own % 8), (0, 0)), constant_values=-2.0)
    upstream_low = jnp.concatenate([dy_prompt[0], dy_cont[0].reshape(cont_rows, model_width)], axis=0)
    upstream = upstream_low.astype(jnp.float32)
    upstream_all = lax.all_gather(upstream_low, group, axis=0, tiled=False)
    d_slot_rows = dispatch(own_codes, upstream_all, own, slots)
    d_plain = jnp.einsum("ecd,efd->ecf", d_slot_rows, down_own, preferred_element_type=jnp.float32)
    gain_one = norm1_gain.astype(jnp.float32)
    gain_two = norm2_gain.astype(jnp.float32)
    tokens = jnp.concatenate(
        [x_prompt[0], x_cont[0].reshape(cont_rows, model_width)], axis=0
    ).astype(jnp.float32)
    normed_one, scale_one = rms_forward(tokens, gain_one)
    h1_low = normed_one.astype(jnp.bfloat16)
    q_lin = jnp.dot(h1_low, w_query, preferred_element_type=jnp.float32)
    key_linear = jnp.dot(h1_low, key_weight, preferred_element_type=jnp.float32)
    value_linear = jnp.dot(h1_low, value_weight, preferred_element_type=jnp.float32)
    row_index = jnp.arange(count_of_tokens, dtype=jnp.int32)
    in_cont = row_index >= prompt_rows
    cont_offset = row_index - prompt_rows
    ctx_index = lax.axis_index("ctx")
    query_pos = jnp.where(
        in_cont, prompt_total + cont_offset % cont_len, ctx_index * prompt_rows + row_index
    )
    query_cont = jnp.where(in_cont, cont_offset // cont_len, -1)
    cosine_lookup, sine_lookup = rope_tables(query_pos.astype(jnp.float32), HEAD_SIZE)
    query_row_block = apply_rotary(
        q_lin.reshape(count_of_tokens, QUERY_HEADS, HEAD_SIZE), cosine_lookup, sine_lookup, 1.0
    ).astype(jnp.bfloat16)
    key_row_block = (
        apply_rotary(
            key_linear.reshape(count_of_tokens, KEY_VALUE_HEADS, HEAD_SIZE),
            cosine_lookup,
            sine_lookup,
            1.0,
        )
        .astype(jnp.bfloat16)
        .reshape(count_of_tokens, key_value_width)
    )
    value_row_block = value_linear.astype(jnp.bfloat16)
    prompt_kv = lax.all_gather(
        jnp.stack([key_row_block[:prompt_rows], value_row_block[:prompt_rows]]),
        "ctx",
        axis=1,
        tiled=True,
    )
    every_key_row = jnp.concatenate([prompt_kv[0], key_row_block[prompt_rows:]], axis=0)
    every_value_row = jnp.concatenate([prompt_kv[1], value_row_block[prompt_rows:]], axis=0)
    key_index = jnp.arange(count_of_keys, dtype=jnp.int32)
    key_in_cont = key_index >= prompt_total
    key_offset = key_index - prompt_total
    key_pos = jnp.where(key_in_cont, prompt_total + key_offset % cont_len, key_index)
    key_cont = jnp.where(key_in_cont, key_offset // cont_len, -1)
    seen = key_pos[None, :] <= query_pos[:, None]
    allowed = (key_cont[None, :] < 0) & ((query_cont[:, None] >= 0) | seen) | (
        key_cont[None, :] >= 0
    ) & (key_cont[None, :] == query_cont[:, None]) & seen
    grouped_query = query_row_block.reshape(
        count_of_tokens, KEY_VALUE_HEADS, queries_per_group, HEAD_SIZE
    ).transpose(1, 0, 2, 3)
    grouped_key = every_key_row.reshape(count_of_keys, KEY_VALUE_HEADS, HEAD_SIZE).transpose(
        1, 0, 2
    )
    grouped_value = every_value_row.reshape(count_of_keys, KEY_VALUE_HEADS, HEAD_SIZE).transpose(
        1, 0, 2
    )
    attended, log_total = lax.map(
        partial(attend_forward, allowed), (grouped_query, grouped_key, grouped_value)
    )
    merged_low = (
        attended.transpose(1, 0, 2, 3)
        .reshape(count_of_tokens, QUERY_HEADS * HEAD_SIZE)
        .astype(jnp.bfloat16)
    )
    branch = jnp.dot(merged_low, w_out, preferred_element_type=jnp.float32)
    resid = tokens + RESID * branch
    normed_two, scale_two = rms_forward(resid, gain_two)
    h2_low = normed_two.astype(jnp.bfloat16)
    rows_all = lax.all_gather(h2_low, group, axis=0, tiled=False)
    slot_rows = dispatch(own_codes, rows_all, own, slots)
    logits = jnp.einsum("btd,de->bet", rows_all, w_router, preferred_element_type=jnp.float32)
    named = codes_all > -1.5
    logits = jnp.where(named, logits, NEG)
    lifted = jnp.where(named, jnp.exp(logits - jnp.max(logits, axis=1, keepdims=True)), 0.0)
    gates_all = lifted / jnp.sum(lifted, axis=1, keepdims=True)
    own_gates = lax.dynamic_slice_in_dim(gates_all, first_expert, own, axis=1)
    gates = lax.dynamic_index_in_dim(gates_all, block_index, 0, keepdims=False)
    slot_index = jnp.arange(slots, dtype=jnp.int32).astype(jnp.float32)
    picked = own_codes[:, :own, None, :] == slot_index[None, None, :, None]
    slot_gate = jnp.sum(jnp.where(picked, own_gates[:, :, None, :], 0.0), axis=-1)
    slot_gate = slot_gate.transpose(1, 0, 2).reshape(own, blocks * slots)
    both = jnp.einsum("ecd,edf->ecf", slot_rows, gate_up_own, preferred_element_type=jnp.float32)
    gate_part = both[..., :hidden_units]
    up_part = both[..., hidden_units:]
    weight = RESID * slot_gate[:, :, None]
    logistic = jax.nn.sigmoid(gate_part)
    silu = gate_part * logistic
    hidden = silu * up_part
    d_slot_gate = RESID * jnp.sum(hidden * d_plain, axis=-1)
    weighted = (weight * hidden).astype(jnp.bfloat16)
    d_hidden = weight * d_plain
    d_gate = d_hidden * up_part * logistic * (1.0 + gate_part * (1.0 - logistic))
    d_both = jnp.concatenate([d_gate, d_hidden * silu], axis=-1).astype(jnp.bfloat16)
    d_slots = jnp.einsum(
        "ecf,edf->ecd", d_both, gate_up_own, preferred_element_type=jnp.float32
    ).astype(jnp.bfloat16)
    d_rows = lax.psum_scatter(combine(own_codes, d_slots, own, slots), group, scatter_dimension=0)
    d_gates_own = jnp.sum(
        jnp.where(
            picked,
            d_slot_gate.reshape(own, blocks, slots).transpose(1, 0, 2)[..., None],
            0.0,
        ),
        axis=2,
    )
    d_gates = lax.psum_scatter(
        lax.dynamic_update_slice_in_dim(
            jnp.zeros((blocks, expert_total, count_of_tokens), jnp.float32),
            d_gates_own,
            first_expert,
            axis=1,
        ),
        group,
        scatter_dimension=0,
    )
    d_logits = (
        gates * (d_gates - jnp.sum(gates * d_gates, axis=0, keepdims=True))
    ).astype(jnp.bfloat16)
    grad_router = jnp.einsum("td,et->de", h2_low, d_logits, preferred_element_type=jnp.float32)
    d_normed_two = d_rows.astype(jnp.float32) + jnp.einsum(
        "et,de->td", d_logits, w_router, preferred_element_type=jnp.float32
    )
    grad_down = jnp.einsum(
        "ecf,ecd->efd", weighted, d_slot_rows, preferred_element_type=jnp.float32
    ).astype(jnp.bfloat16)
    grad_gate_up = jnp.einsum(
        "ecd,ecf->edf", slot_rows, d_both, preferred_element_type=jnp.float32
    ).astype(jnp.bfloat16)
    grad_down = reduce_experts(grad_down, split)
    grad_gate_up = reduce_experts(grad_gate_up, split)
    expert_out = jnp.einsum(
        "ecf,efd->ecd", weighted, down_own, preferred_element_type=jnp.float32
    ).astype(jnp.bfloat16)
    mixed = lax.psum_scatter(
        combine(own_codes, expert_out, own, slots), group, scatter_dimension=0
    ).astype(jnp.float32)
    output = resid + mixed
    y_prompt = output[:prompt_rows].astype(jnp.bfloat16)[None]
    y_cont = output[prompt_rows:].reshape(1, cont_count, cont_len, model_width).astype(jnp.bfloat16)
    d_resid_norm, grad_norm2 = rms_backward(resid, scale_two, gain_two, d_normed_two)
    d_resid = upstream + d_resid_norm
    d_branch = (RESID * d_resid).astype(jnp.bfloat16)
    grad_out = jnp.einsum("tq,td->qd", merged_low, d_branch, preferred_element_type=jnp.float32)
    merged_gradient = jnp.einsum(
        "td,qd->tq", d_branch, w_out, preferred_element_type=jnp.float32
    ).astype(jnp.bfloat16)
    grouped_output_gradient = merged_gradient.reshape(
        count_of_tokens, KEY_VALUE_HEADS, queries_per_group, HEAD_SIZE
    ).transpose(1, 0, 2, 3)
    d_q, d_k, d_v = lax.map(
        partial(attend_backward, allowed),
        (grouped_query, grouped_key, grouped_value, grouped_output_gradient, attended, log_total),
    )
    d_query = d_q.transpose(1, 0, 2, 3).reshape(count_of_tokens, QUERY_HEADS, HEAD_SIZE)
    d_key_all = d_k.transpose(1, 0, 2).reshape(count_of_keys, key_value_width)
    d_value_all = d_v.transpose(1, 0, 2).reshape(count_of_keys, key_value_width)
    summed = lax.psum_scatter(
        jnp.stack([d_key_all[:prompt_total], d_value_all[:prompt_total]]).astype(jnp.bfloat16),
        "ctx",
        scatter_dimension=1,
        tiled=True,
    ).astype(jnp.float32)
    d_key = jnp.concatenate([summed[0], d_key_all[prompt_total:]], axis=0).reshape(
        count_of_tokens, KEY_VALUE_HEADS, HEAD_SIZE
    )
    d_value_low = jnp.concatenate([summed[1], d_value_all[prompt_total:]], axis=0).astype(
        jnp.bfloat16
    )
    d_query_low = (
        apply_rotary(d_query, cosine_lookup, sine_lookup, -1.0)
        .reshape(count_of_tokens, QUERY_HEADS * HEAD_SIZE)
        .astype(jnp.bfloat16)
    )
    d_key_low = (
        apply_rotary(d_key, cosine_lookup, sine_lookup, -1.0)
        .reshape(count_of_tokens, key_value_width)
        .astype(jnp.bfloat16)
    )
    grad_query = jnp.einsum("td,tq->dq", h1_low, d_query_low, preferred_element_type=jnp.float32)
    grad_key = jnp.einsum("td,tq->dq", h1_low, d_key_low, preferred_element_type=jnp.float32)
    grad_value = jnp.einsum("td,tq->dq", h1_low, d_value_low, preferred_element_type=jnp.float32)
    d_normed_one = jnp.einsum("tq,dq->td", d_query_low, w_query, preferred_element_type=jnp.float32)
    d_normed_one = d_normed_one + jnp.einsum(
        "tq,dq->td", d_key_low, key_weight, preferred_element_type=jnp.float32
    )
    d_normed_one = d_normed_one + jnp.einsum(
        "tq,dq->td", d_value_low, value_weight, preferred_element_type=jnp.float32
    )
    d_tokens_norm, grad_norm1 = rms_backward(tokens, scale_one, gain_one, d_normed_one)
    d_tokens = d_resid + d_tokens_norm
    dx_prompt = d_tokens[:prompt_rows][None]
    dx_cont = d_tokens[prompt_rows:].reshape(1, cont_count, cont_len, model_width)
    wide = jnp.concatenate([grad_query, grad_key, grad_value, grad_out], axis=1)
    small = jnp.concatenate([grad_router, grad_norm1[:, None], grad_norm2[:, None]], axis=1)
    small = jnp.pad(small, ((0, 0), (0, -small.shape[1] % 128)))
    dense = jnp.concatenate([wide, small], axis=1).astype(jnp.bfloat16)
    dense = lax.psum_scatter(dense, ("dp", "ctx"), scatter_dimension=0, tiled=True)
    dense = lax.psum(dense, "expert").astype(jnp.float32)
    heads_width = QUERY_HEADS * HEAD_SIZE
    edge = heads_width + 2 * key_value_width
    tail = edge + w_out.shape[1]
    return (
        y_prompt,
        y_cont,
        dx_prompt,
        dx_cont,
        dense[:, tail + expert_total],
        dense[:, :heads_width],
        dense[:, heads_width : heads_width + key_value_width],
        dense[:, heads_width + key_value_width : edge],
        dense[:, edge:tail],
        dense[:, tail + expert_total + 1],
        dense[:, tail : tail + expert_total],
        grad_gate_up,
        grad_down,
    )


def solution(mesh):
    return jax.shard_map(
        per_device,
        mesh=mesh,
        in_specs=(
            P(("dp", "expert"), "ctx", None),
            P(("dp", "expert"), "ctx", None, None),
            P(),
            P(),
            P(),
            P(),
            P(),
            P(),
            P(),
            P("expert", None, None),
            P("expert", None, None),
            P(("dp", "expert"), "ctx", None),
            P(("dp", "expert"), "ctx", None, None),
            P(("dp", "expert"), "ctx", None),
            P(("dp", "expert"), "ctx", None),
            P(("dp", "expert"), "ctx", None, None),
        ),
        out_specs=(
            P(("dp", "expert"), "ctx", None),
            P(("dp", "expert"), "ctx", None, None),
            P(("dp", "expert"), "ctx", None),
            P(("dp", "expert"), "ctx", None, None),
            P(("dp", "ctx")),
            P(("dp", "ctx"), None),
            P(("dp", "ctx"), None),
            P(("dp", "ctx"), None),
            P(("dp", "ctx"), None),
            P(("dp", "ctx")),
            P(("dp", "ctx"), None),
            P("expert", ("dp", "ctx"), None),
            P("expert", ("dp", "ctx"), None),
        ),
        check_vma=False,
    )
```

```python
from functools import partial

import jax
import jax.numpy as jnp
from jax import lax
from jax.experimental import pallas as pl
from jax.experimental.pallas import tpu as pltpu
from jax.sharding import PartitionSpec as P

QUERY_HEADS = 24
KEY_VALUE_HEADS = 8
HEAD_SIZE = 64


EPS = 1e-06
RESID = 0.22
ATT_SCALE = 0.015625
THETA = 10000.0
NEG = -1e30


def rope_tables(positions, head_dim):
    half_dim = head_dim // 2
    frequency = THETA ** (-(jnp.arange(half_dim, dtype=jnp.float32) * 2.0 / head_dim))
    angles = positions[:, None] * frequency[None, :]
    cosine_lookup = jnp.concatenate([jnp.cos(angles), jnp.cos(angles)], axis=-1)
    sine_lookup = jnp.concatenate([jnp.sin(angles), jnp.sin(angles)], axis=-1)
    return (cosine_lookup, sine_lookup)


def signed_tables(positions, width):
    cosine_lookup, sine_lookup = rope_tables(positions, HEAD_SIZE)
    half_dim = HEAD_SIZE // 2
    sine_lookup = jnp.concatenate([-sine_lookup[:, :half_dim], sine_lookup[:, half_dim:]], axis=-1)
    copies = width // HEAD_SIZE
    return (jnp.tile(cosine_lookup, (1, copies)), jnp.tile(sine_lookup, (1, copies)))


def rms_forward(values, norm_gain):
    inverse = lax.rsqrt(jnp.mean(values * values, axis=-1, keepdims=True) + EPS)
    return (values * inverse * norm_gain, inverse)


def rms_backward(values, inverse, norm_gain, upstream):
    normed = values * inverse
    weighted = upstream * norm_gain
    projected = jnp.mean(weighted * normed, axis=-1, keepdims=True)
    return (inverse * (weighted - normed * projected), jnp.sum(upstream * normed, axis=0))


def slot_codes(routes, visit_order, experts, capacity):
    count = routes.shape[0]
    ids = jnp.arange(count, dtype=jnp.int32)
    visit = jnp.arange(count, dtype=jnp.float32)
    place = (visit_order[:, None] == ids[None, :]).astype(jnp.float32)
    place_row = jnp.sum(place * visit[:, None], axis=0)
    place_col = jnp.sum((visit_order[None, :] == ids[:, None]).astype(jnp.float32) * visit[None, :], axis=1)
    earlier = (place_col[:, None] < place_row[None, :]).astype(jnp.bfloat16)
    named = jnp.any(
        routes.T[None, :, :] == jnp.arange(experts, dtype=jnp.int32)[:, None, None], axis=1
    )
    rank = jnp.dot(named.astype(jnp.bfloat16), earlier, preferred_element_type=jnp.float32)
    return jnp.where(named, jnp.where(rank < capacity, rank, -1.0), -2.0)


def selection(codes, own, slots):
    tokens = codes.shape[-1]
    slot_index = lax.broadcasted_iota(jnp.int32, (slots, tokens), 0).astype(jnp.float32)
    picks = [
        jnp.where(codes[e : e + 1, :] == slot_index, 1.0, 0.0).astype(jnp.bfloat16)
        for e in range(own)
    ]
    return jnp.concatenate(picks, axis=0)


def dispatch_body(own, slots, codes_ref, rows_ref, out_ref):
    pick = selection(codes_ref[0], own, slots)
    moved = jnp.dot(pick, rows_ref[0], preferred_element_type=jnp.float32).astype(jnp.bfloat16)
    for e in range(own):
        out_ref[e] = moved[e * slots : (e + 1) * slots]


def dispatch(codes, rows, own, slots):
    blocks, tokens, width = rows.shape
    return pl.pallas_call(
        partial(dispatch_body, own, slots),
        grid=(blocks,),
        in_specs=[
            pl.BlockSpec((1, codes.shape[1], tokens), lambda b: (b, 0, 0)),
            pl.BlockSpec((1, tokens, width), lambda b: (b, 0, 0)),
        ],
        out_specs=pl.BlockSpec((own, slots, width), lambda b: (0, b, 0)),
        out_shape=jax.ShapeDtypeStruct((own, blocks * slots, width), jnp.bfloat16),
        cost_estimate=pl.CostEstimate(
            flops=2 * blocks * own * slots * tokens * width,
            transcendentals=0,
            bytes_accessed=2 * blocks * (tokens + own * slots) * width,
        ),
        name="dispatch",
    )(codes, rows)


def combine_body(own, slots, at_ref, codes_ref, rows_ref, out_ref):
    pick = selection(codes_ref[0], own, slots)
    rows = rows_ref[...].reshape(own * slots, rows_ref.shape[-1])
    out_ref[0] = lax.dot_general(
        pick, rows, (((0,), (0,)), ((), ())), preferred_element_type=jnp.float32
    ).astype(out_ref.dtype)


def combine(at, codes, rows, own, slots):
    count, tokens = at.shape[0], codes.shape[2]
    width = rows.shape[-1]
    return pl.pallas_call(
        partial(combine_body, own, slots),
        grid_spec=pltpu.PrefetchScalarGridSpec(
            num_scalar_prefetch=1,
            grid=(count,),
            in_specs=[
                pl.BlockSpec((1, codes.shape[1], tokens), lambda b, at: (at[b], 0, 0)),
                pl.BlockSpec((own, slots, width), lambda b, at: (0, at[b], 0)),
            ],
            out_specs=pl.BlockSpec((1, tokens, width), lambda b, at: (b, 0, 0)),
        ),
        out_shape=jax.ShapeDtypeStruct((count, tokens, width), jnp.bfloat16),
        cost_estimate=pl.CostEstimate(
            flops=2 * count * own * slots * tokens * width,
            transcendentals=0,
            bytes_accessed=2 * count * (tokens + own * slots) * width,
        ),
        name="combine",
    )(at, codes, rows)


def swap(values, axis, bit):
    size = lax.axis_size(axis)
    return lax.ppermute(values, axis, [(i, i ^ bit) for i in range(size)])


def added(left, right):
    return (left.astype(jnp.float32) + right.astype(jnp.float32)).astype(jnp.bfloat16)


def start_scatter(codes, rows, own, slots, group):
    blocks = codes.shape[0]
    if group != ("ctx", "expert") or lax.axis_size("ctx") != 4 or lax.axis_size("expert") != 2:
        every = jnp.arange(blocks, dtype=jnp.int32)
        return lax.psum_scatter(
            combine(every, codes, rows, own, slots), group, scatter_dimension=0
        )
    here = lax.axis_index(group).astype(jnp.int32)
    far = here ^ jnp.array([2, 3, 6, 7], jnp.int32)
    near = here ^ jnp.array([0, 1, 4, 5], jnp.int32)
    sent = swap(combine(far, codes, rows, own, slots), "ctx", 1)
    return added(combine(near, codes, rows, own, slots), sent)


def finish_scatter(part, middle=None, later=None, work=None):
    if part.ndim == 2:
        return part.astype(jnp.float32), None if work is None else work(later)
    half = part.shape[-1] // 2
    left, right = part[:, :, :half], part[:, :, half:]
    left_sent = swap(left[2:], "ctx", 2)
    right_sent = swap(jnp.stack([right[1], right[3]]), "expert", 1)
    if work is not None:
        left_sent, right_sent, _, later = lax.optimization_barrier(
            (left_sent, right_sent, middle, later)
        )
    left_on = swap(added(left[1], left_sent[1]), "expert", 1)
    right_on = swap(added(right[2], right_sent[1]), "ctx", 2)
    made = None
    if work is not None:
        left_on, right_on, made = lax.optimization_barrier((left_on, right_on, work(later)))
    wide = lambda *pieces: sum(piece.astype(jnp.float32) for piece in pieces)
    whole = jnp.concatenate(
        [wide(left[0], left_sent[0], left_on), wide(right[0], right_sent[0], right_on)], axis=1
    )
    return whole, made


def lane_half(shape):
    return lax.broadcasted_iota(jnp.int32, shape, 1) // HEAD_SIZE


def turn(values, cosine, sine):
    half_dim = HEAD_SIZE // 2
    width = values.shape[1]
    lane = lax.broadcasted_iota(jnp.int32, values.shape, 1) % HEAD_SIZE
    partner = jnp.where(
        lane < half_dim,
        pltpu.roll(values, width - half_dim, 1),
        pltpu.roll(values, half_dim, 1),
    )
    return values * cosine + partner * sine


def to_key_half(values, swap, key_half):
    moved = jnp.where(swap, pltpu.roll(values, HEAD_SIZE, 1), values)
    return jnp.where(lane_half(values.shape) == key_half, moved, 0.0)


def head_place(group):
    head = pl.program_id(0)
    key_half = (head // group) % 2
    return head, key_half, (head % 2) != key_half


def attend_forward_body(
    group, prompt_rows, cont_len, pos_ref, q_ref, cos_ref, sin_ref, kp_ref, vp_ref, kc_ref, vc_ref,
    qr_ref, out_ref, log_ref,
):
    head, key_half, swap = head_place(group)
    rotated = turn(q_ref[...], cos_ref[...], sin_ref[...]).astype(jnp.bfloat16)
    qr_ref[...] = rotated
    query = to_key_half(rotated.astype(jnp.float32), swap, key_half) * ATT_SCALE
    query = query.astype(jnp.bfloat16)
    nt = (((1,), (1,)), ((), ()))

    def finish(parts, rows):
        highest = parts[0][0].max(axis=1, keepdims=True)
        for scores, _ in parts[1:]:
            highest = jnp.maximum(highest, scores.max(axis=1, keepdims=True))
        lifted = [jnp.exp(scores - highest) for scores, _ in parts]
        total = lifted[0].sum(axis=1, keepdims=True)
        for piece in lifted[1:]:
            total = total + piece.sum(axis=1, keepdims=True)
        inverse = 1.0 / total
        result = None
        for piece, (_, value) in zip(lifted, parts):
            term = jnp.dot(
                (piece * inverse).astype(jnp.bfloat16), value, preferred_element_type=jnp.float32
            )
            result = term if result is None else result + term
        log_total = jnp.broadcast_to(highest + jnp.log(total), (total.shape[0], 128))
        log_ref[0, :, rows] = jnp.transpose(log_total)[:8]
        keep = jnp.where(lane_half(result.shape) == key_half, result, 0.0)
        keep = jnp.where(swap, pltpu.roll(keep, HEAD_SIZE, 1), keep).astype(jnp.bfloat16)

        @pl.when(head % 2 == 0)
        def _():
            out_ref[rows, :] = keep

        @pl.when(head % 2 == 1)
        def _():
            out_ref[rows, :] = out_ref[rows, :] + keep

    total_rows = q_ref.shape[0]
    first = lax.dot_general(
        query[:prompt_rows], kp_ref[...], nt, preferred_element_type=jnp.float32
    )
    row = lax.broadcasted_iota(jnp.int32, first.shape, 0) + pos_ref[0]
    first = jnp.where(lax.broadcasted_iota(jnp.int32, first.shape, 1) <= row, first, NEG)
    finish([(first, vp_ref[...])], pl.ds(0, prompt_rows))
    lower = query[prompt_rows:]
    wide = lax.dot_general(lower, kp_ref[...], nt, preferred_element_type=jnp.float32)
    near = lax.dot_general(lower, kc_ref[...], nt, preferred_element_type=jnp.float32)
    row = lax.broadcasted_iota(jnp.int32, near.shape, 0)
    col = lax.broadcasted_iota(jnp.int32, near.shape, 1)
    near = jnp.where((col <= row) & (col // cont_len == row // cont_len), near, NEG)
    finish([(wide, vp_ref[...]), (near, vc_ref[...])], pl.ds(prompt_rows, total_rows - prompt_rows))


def attend_forward(q_lin, key_prompt, value_prompt, key_cont, value_cont, cosine, sine, start, rows, cont_len):
    tokens, width = q_lin.shape
    heads = width // HEAD_SIZE
    group = heads // (key_prompt.shape[1] // HEAD_SIZE)
    keys, near = key_prompt.shape[0], key_cont.shape[0]
    tile = lambda h, *_: (0, h // 2)
    key_tile = lambda h, *_: (0, h // (2 * group))
    same = lambda h, *_: (0, 0)
    return pl.pallas_call(
        partial(attend_forward_body, group, rows, cont_len),
        grid_spec=pltpu.PrefetchScalarGridSpec(
            num_scalar_prefetch=1,
            grid=(heads,),
            in_specs=[
                pl.BlockSpec((tokens, 128), tile),
                pl.BlockSpec((tokens, 128), same),
                pl.BlockSpec((tokens, 128), same),
                pl.BlockSpec((keys, 128), key_tile),
                pl.BlockSpec((keys, 128), key_tile),
                pl.BlockSpec((near, 128), key_tile),
                pl.BlockSpec((near, 128), key_tile),
            ],
            out_specs=[
                pl.BlockSpec((tokens, 128), tile),
                pl.BlockSpec((tokens, 128), tile),
                pl.BlockSpec((1, 8, tokens), lambda h, *_: (h, 0, 0)),
            ],
        ),
        out_shape=[
            jax.ShapeDtypeStruct((tokens, width), jnp.bfloat16),
            jax.ShapeDtypeStruct((tokens, width), jnp.bfloat16),
            jax.ShapeDtypeStruct((heads, 8, tokens), jnp.float32),
        ],
        cost_estimate=pl.CostEstimate(
            flops=4 * heads * tokens * (keys + near) * 128,
            transcendentals=heads * tokens * (keys + near),
            bytes_accessed=8 * tokens * width,
        ),
        name="attend_forward",
    )(start, q_lin, cosine, sine, key_prompt, value_prompt, key_cont, value_cont)


def attend_backward_body(
    group, prompt_rows, cont_len, chunk, pos_ref, q_ref, do_ref, out_ref, log_ref, cos_ref, sin_ref,
    kcos_ref, ksin_ref, kp_ref, vp_ref, kc_ref, vc_ref,
    dq_ref, dkp_ref, dvp_ref, dkc_ref, dvc_ref, dk_acc, dv_acc,
):
    head, key_half, swap = head_place(group)
    tokens = q_ref.shape[0]
    keys = kp_ref.shape[0]
    near = kc_ref.shape[0]
    nt = (((1,), (1,)), ((), ()))
    tn = (((0,), (0,)), ((), ()))

    @pl.when(head % (2 * group) == 0)
    def _():
        dk_acc[...] = jnp.zeros_like(dk_acc)
        dv_acc[...] = jnp.zeros_like(dv_acc)

    query = to_key_half(q_ref[...].astype(jnp.float32), swap, key_half) * ATT_SCALE
    query = query.astype(jnp.bfloat16)
    d_out = to_key_half(do_ref[...].astype(jnp.float32), swap, key_half)
    result = to_key_half(out_ref[...].astype(jnp.float32), swap, key_half)
    centre = jnp.transpose(
        jnp.broadcast_to(jnp.sum(d_out * result, axis=1, keepdims=True), (tokens, 128))
    )[:1]
    d_out = d_out.astype(jnp.bfloat16)
    log_total = log_ref[0][:1]
    row = lax.broadcasted_iota(jnp.int32, (1, tokens), 1)
    limit = jnp.where(row < prompt_rows, row + pos_ref[0], keys)

    def step(key, value, query, d_out, log_total, centre, allowed, at, count):
        scores = lax.dot_general(key, query, nt, preferred_element_type=jnp.float32)
        scores = jnp.where(allowed(scores.shape), scores, NEG)
        weights = jnp.exp(scores - log_total)
        d_weights = lax.dot_general(value, d_out, nt, preferred_element_type=jnp.float32)
        d_scores = (weights * (d_weights - centre)).astype(jnp.bfloat16)
        dv_acc[at : at + count] += jnp.dot(
            weights.astype(jnp.bfloat16), d_out, preferred_element_type=jnp.float32
        )
        dk_acc[at : at + count] += jnp.dot(d_scores, query, preferred_element_type=jnp.float32)
        return lax.dot_general(d_scores, key, tn, preferred_element_type=jnp.float32)

    d_query = jnp.zeros((tokens, 128), jnp.float32)
    for at in range(0, keys, chunk):

        def seen(shape, at=at):
            return lax.broadcasted_iota(jnp.int32, shape, 0) + at <= limit

        d_query = d_query + step(
            kp_ref[at : at + chunk], vp_ref[at : at + chunk], query, d_out, log_total, centre, seen,
            at, chunk,
        )

    def nearby(shape):
        key_at = lax.broadcasted_iota(jnp.int32, shape, 0)
        query_at = lax.broadcasted_iota(jnp.int32, shape, 1)
        return (key_at <= query_at) & (key_at // cont_len == query_at // cont_len)

    tail = step(
        kc_ref[...], vc_ref[...], query[prompt_rows:], d_out[prompt_rows:],
        log_total[:, prompt_rows:], centre[:, prompt_rows:], nearby, keys, near,
    )
    d_query = jnp.concatenate([d_query[:prompt_rows], d_query[prompt_rows:] + tail], axis=0)
    d_query = jnp.where(lane_half(d_query.shape) == key_half, d_query * ATT_SCALE, 0.0)
    d_query = jnp.where(swap, pltpu.roll(d_query, HEAD_SIZE, 1), d_query)
    d_query = turn(d_query, cos_ref[...], -sin_ref[...]).astype(jnp.bfloat16)

    @pl.when(head % 2 == 0)
    def _():
        dq_ref[...] = d_query

    @pl.when(head % 2 == 1)
    def _():
        dq_ref[...] = dq_ref[...] + d_query

    @pl.when(head % (2 * group) == 2 * group - 1)
    def _():
        dk = turn(dk_acc[...], kcos_ref[...], -ksin_ref[...]).astype(jnp.bfloat16)
        dv = dv_acc[...].astype(jnp.bfloat16)
        dkp_ref[...] = dk[:keys]
        dkc_ref[...] = dk[keys:]
        dvp_ref[...] = dv[:keys]
        dvc_ref[...] = dv[keys:]


def attend_backward(
    query, d_out, result, log_total, key_prompt, value_prompt, key_cont, value_cont, cosine, sine,
    key_cosine, key_sine, start, rows, cont_len,
):
    tokens, width = query.shape
    heads = width // HEAD_SIZE
    key_width = key_prompt.shape[1]
    group = heads // (key_width // HEAD_SIZE)
    keys, near = key_prompt.shape[0], key_cont.shape[0]
    chunk = min(256, keys)
    tile = lambda h, *_: (0, h // 2)
    key_tile = lambda h, *_: (0, h // (2 * group))
    same = lambda h, *_: (0, 0)
    return pl.pallas_call(
        partial(attend_backward_body, group, rows, cont_len, chunk),
        grid_spec=pltpu.PrefetchScalarGridSpec(
            num_scalar_prefetch=1,
            grid=(heads,),
            in_specs=[
                pl.BlockSpec((tokens, 128), tile),
                pl.BlockSpec((tokens, 128), tile),
                pl.BlockSpec((tokens, 128), tile),
                pl.BlockSpec((1, 8, tokens), lambda h, *_: (h, 0, 0)),
                pl.BlockSpec((tokens, 128), same),
                pl.BlockSpec((tokens, 128), same),
                pl.BlockSpec((keys + near, 128), same),
                pl.BlockSpec((keys + near, 128), same),
                pl.BlockSpec((keys, 128), key_tile),
                pl.BlockSpec((keys, 128), key_tile),
                pl.BlockSpec((near, 128), key_tile),
                pl.BlockSpec((near, 128), key_tile),
            ],
            out_specs=[
                pl.BlockSpec((tokens, 128), tile),
                pl.BlockSpec((keys, 128), key_tile),
                pl.BlockSpec((keys, 128), key_tile),
                pl.BlockSpec((near, 128), key_tile),
                pl.BlockSpec((near, 128), key_tile),
            ],
            scratch_shapes=[
                pltpu.VMEM((keys + near, 128), jnp.float32),
                pltpu.VMEM((keys + near, 128), jnp.float32),
            ],
        ),
        out_shape=[
            jax.ShapeDtypeStruct((tokens, width), jnp.bfloat16),
            jax.ShapeDtypeStruct((keys, key_width), jnp.bfloat16),
            jax.ShapeDtypeStruct((keys, key_width), jnp.bfloat16),
            jax.ShapeDtypeStruct((near, key_width), jnp.bfloat16),
            jax.ShapeDtypeStruct((near, key_width), jnp.bfloat16),
        ],
        cost_estimate=pl.CostEstimate(
            flops=10 * heads * tokens * (keys + near) * 128,
            transcendentals=heads * tokens * (keys + near),
            bytes_accessed=8 * tokens * width,
        ),
        name="attend_backward",
    )(
        start, query, d_out, result, log_total, cosine, sine, key_cosine, key_sine, key_prompt,
        value_prompt, key_cont, value_cont,
    )


def reduce_experts(grad, split):
    if split == 1:
        return lax.psum_scatter(
            grad, ("dp", "ctx"), scatter_dimension=1, tiled=True
        ).astype(jnp.float32)
    part = lax.psum_scatter(grad, "dp", scatter_dimension=1, tiled=True)
    return lax.all_to_all(part, "ctx", split_axis=1, concat_axis=0, tiled=True).astype(jnp.float32)


def scatter_keys(d_key, d_value, rows):
    size = lax.axis_size("ctx")
    here = lax.axis_index("ctx")

    def share(owner):
        return jnp.concatenate(
            [
                lax.dynamic_slice_in_dim(d_key, owner * rows, rows, axis=0),
                lax.dynamic_slice_in_dim(d_value, owner * rows, rows, axis=0),
            ],
            axis=1,
        )

    total = share(here).astype(jnp.float32)
    for hop in range(1, size):
        moved = lax.ppermute(
            share((here + hop) % size), "ctx", [(i, (i + hop) % size) for i in range(size)]
        )
        total = total + moved.astype(jnp.float32)
    total = total.astype(jnp.bfloat16)
    return (total[:, : d_key.shape[1]], total[:, d_key.shape[1] :])


def per_device(
    x_prompt,
    x_cont,
    norm1_gain,
    w_query,
    key_weight,
    value_weight,
    w_out,
    norm2_gain,
    w_router,
    w_gate_up,
    w_down,
    routes_prompt,
    routes_cont,
    slot_order,
    dy_prompt,
    dy_cont,
):
    model_width = x_prompt.shape[2]
    prompt_rows = x_prompt.shape[1]
    cont_count = x_cont.shape[1]
    cont_len = x_cont.shape[2]
    cont_rows = cont_count * cont_len
    count_of_tokens = prompt_rows + cont_rows
    key_value_width = KEY_VALUE_HEADS * HEAD_SIZE
    local_experts = w_gate_up.shape[0]
    expert_groups = lax.axis_size("expert")
    expert_total = local_experts * expert_groups
    top_count = routes_prompt.shape[2]
    capacity = (count_of_tokens * top_count + expert_total - 1) // expert_total
    hidden_units = w_down.shape[1]
    prompt_total = prompt_rows * lax.axis_size("ctx")
    count_of_keys = prompt_total + cont_rows
    split = lax.axis_size("ctx") if local_experts % lax.axis_size("ctx") == 0 else 1
    own = local_experts // split
    blocks = split * expert_groups
    slots = -(-capacity // 8) * 8
    group = ("ctx", "expert") if split > 1 else ("expert",)
    block_index = lax.axis_index(group)
    own_offset = lax.axis_index("ctx") * own if split > 1 else 0
    first_expert = lax.axis_index("expert") * local_experts + own_offset
    gate_up_own = w_gate_up
    down_own = w_down
    if split > 1:
        gate_up_own = lax.dynamic_slice_in_dim(w_gate_up, own_offset, own, axis=0)
        down_own = lax.dynamic_slice_in_dim(w_down, own_offset, own, axis=0)
    routes = jnp.concatenate(
        [routes_prompt[0], routes_cont[0].reshape(cont_rows, top_count)], axis=0
    )
    codes_all = lax.all_gather(
        slot_codes(routes, slot_order[0, 0], expert_total, capacity), group, axis=0, tiled=False
    )
    own_codes = lax.dynamic_slice_in_dim(codes_all, first_expert, own, axis=1)
    own_codes = jnp.pad(own_codes, ((0, 0), (0, -own % 8), (0, 0)), constant_values=-2.0)
    upstream_low = jnp.concatenate([dy_prompt[0], dy_cont[0].reshape(cont_rows, model_width)], axis=0)
    upstream = upstream_low.astype(jnp.float32)
    upstream_all = lax.all_gather(upstream_low, group, axis=0, tiled=False)
    d_slot_rows = dispatch(own_codes, upstream_all, own, slots)
    d_plain = jnp.einsum("ecd,efd->ecf", d_slot_rows, down_own, preferred_element_type=jnp.float32)
    gain_one = norm1_gain.astype(jnp.float32)
    gain_two = norm2_gain.astype(jnp.float32)
    tokens = jnp.concatenate(
        [x_prompt[0], x_cont[0].reshape(cont_rows, model_width)], axis=0
    ).astype(jnp.float32)
    normed_one, scale_one = rms_forward(tokens, gain_one)
    h1_low = normed_one.astype(jnp.bfloat16)
    q_lin = jnp.dot(h1_low, w_query, preferred_element_type=jnp.float32)
    key_linear = jnp.dot(h1_low, key_weight, preferred_element_type=jnp.float32)
    value_linear = jnp.dot(h1_low, value_weight, preferred_element_type=jnp.float32)
    row_index = jnp.arange(count_of_tokens, dtype=jnp.int32)
    cont_offset = row_index - prompt_rows
    start = lax.axis_index("ctx") * prompt_rows
    query_pos = jnp.where(
        cont_offset >= 0, prompt_total + cont_offset % cont_len, start + row_index
    )
    key_index = jnp.arange(count_of_keys, dtype=jnp.int32)
    key_pos = jnp.where(
        key_index >= prompt_total, prompt_total + (key_index - prompt_total) % cont_len, key_index
    )
    start = start.astype(jnp.int32)[None]
    cosine, sine = signed_tables(query_pos.astype(jnp.float32), 128)
    key_cosine, key_sine = signed_tables(key_pos.astype(jnp.float32), 128)
    wide_cosine, wide_sine = signed_tables(query_pos.astype(jnp.float32), key_value_width)
    half_dim = HEAD_SIZE // 2
    lane = jnp.arange(key_value_width, dtype=jnp.int32) % HEAD_SIZE
    partner = jnp.where(
        lane < half_dim, jnp.roll(key_linear, -half_dim, axis=1), jnp.roll(key_linear, half_dim, axis=1)
    )
    key_row_block = (key_linear * wide_cosine + partner * wide_sine).astype(jnp.bfloat16)
    value_row_block = value_linear.astype(jnp.bfloat16)
    prompt_kv = lax.all_gather(
        jnp.stack([key_row_block[:prompt_rows], value_row_block[:prompt_rows]]),
        "ctx",
        axis=1,
        tiled=True,
    )
    keys_values = (
        prompt_kv[0], prompt_kv[1], key_row_block[prompt_rows:], value_row_block[prompt_rows:]
    )
    query_row_block, merged_low, log_total = attend_forward(
        q_lin, *keys_values, cosine, sine, start, prompt_rows, cont_len
    )
    branch = jnp.dot(merged_low, w_out, preferred_element_type=jnp.float32)
    resid = tokens + RESID * branch
    normed_two, scale_two = rms_forward(resid, gain_two)
    h2_low = normed_two.astype(jnp.bfloat16)
    rows_all = lax.all_gather(h2_low, group, axis=0, tiled=False)
    rows_all, d_plain = lax.optimization_barrier((rows_all, d_plain))
    slot_rows = dispatch(own_codes, rows_all, own, slots)
    logits = jnp.einsum("btd,de->bet", rows_all, w_router, preferred_element_type=jnp.float32)
    named = codes_all > -1.5
    logits = jnp.where(named, logits, NEG)
    lifted = jnp.where(named, jnp.exp(logits - jnp.max(logits, axis=1, keepdims=True)), 0.0)
    gates_all = lifted / jnp.sum(lifted, axis=1, keepdims=True)
    own_gates = lax.dynamic_slice_in_dim(gates_all, first_expert, own, axis=1)
    gates = lax.dynamic_index_in_dim(gates_all, block_index, 0, keepdims=False)
    slot_index = jnp.arange(slots, dtype=jnp.int32).astype(jnp.float32)
    picked = own_codes[:, :own, None, :] == slot_index[None, None, :, None]
    slot_gate = jnp.sum(jnp.where(picked, own_gates[:, :, None, :], 0.0), axis=-1)
    slot_gate = slot_gate.transpose(1, 0, 2).reshape(own, blocks * slots)
    both = jnp.einsum("ecd,edf->ecf", slot_rows, gate_up_own, preferred_element_type=jnp.float32)
    gate_part = both[..., :hidden_units]
    up_part = both[..., hidden_units:]
    weight = RESID * slot_gate[:, :, None]
    logistic = jax.nn.sigmoid(gate_part)
    silu = gate_part * logistic
    hidden = silu * up_part
    d_slot_gate = RESID * jnp.sum(hidden * d_plain, axis=-1)
    weighted = (weight * hidden).astype(jnp.bfloat16)
    d_hidden = weight * d_plain
    d_gate = d_hidden * up_part * logistic * (1.0 + gate_part * (1.0 - logistic))
    d_both = jnp.concatenate([d_gate, d_hidden * silu], axis=-1).astype(jnp.bfloat16)
    grad_down = jnp.einsum(
        "ecf,ecd->efd", weighted, d_slot_rows, preferred_element_type=jnp.float32
    ).astype(jnp.bfloat16)
    d_both, grad_down = lax.optimization_barrier((d_both, grad_down))
    grad_down = reduce_experts(grad_down, split)
    d_slots = jnp.einsum(
        "ecf,edf->ecd", d_both, gate_up_own, preferred_element_type=jnp.float32
    ).astype(jnp.bfloat16)
    d_rows_parts, weighted, slot_rows = lax.optimization_barrier(
        (start_scatter(own_codes, d_slots, own, slots, group), weighted, slot_rows)
    )
    grad_gate_up = jnp.einsum(
        "ecd,ecf->edf", slot_rows, d_both, preferred_element_type=jnp.float32
    ).astype(jnp.bfloat16)

    def forward_rows(weighted):
        expert_out = jnp.einsum(
            "ecf,efd->ecd", weighted, down_own, preferred_element_type=jnp.float32
        ).astype(jnp.bfloat16)
        return start_scatter(own_codes, expert_out, own, slots, group)

    d_rows, mixed_part = finish_scatter(d_rows_parts, grad_gate_up, weighted, forward_rows)
    d_gates_own = jnp.sum(
        jnp.where(
            picked,
            d_slot_gate.reshape(own, blocks, slots).transpose(1, 0, 2)[..., None],
            0.0,
        ),
        axis=2,
    )
    d_gates = lax.psum_scatter(
        lax.dynamic_update_slice_in_dim(
            jnp.zeros((blocks, expert_total, count_of_tokens), jnp.float32),
            d_gates_own,
            first_expert,
            axis=1,
        ),
        group,
        scatter_dimension=0,
    )
    grad_gate_up = reduce_experts(grad_gate_up, split)
    d_logits = (
        gates * (d_gates - jnp.sum(gates * d_gates, axis=0, keepdims=True))
    ).astype(jnp.bfloat16)
    grad_router = jnp.einsum("td,et->de", h2_low, d_logits, preferred_element_type=jnp.float32)
    d_normed_two = d_rows + jnp.einsum(
        "et,de->td", d_logits, w_router, preferred_element_type=jnp.float32
    )
    d_resid_norm, grad_norm2 = rms_backward(resid, scale_two, gain_two, d_normed_two)
    d_resid = upstream + d_resid_norm
    d_branch = (RESID * d_resid).astype(jnp.bfloat16)
    grad_out = jnp.einsum("tq,td->qd", merged_low, d_branch, preferred_element_type=jnp.float32)
    merged_gradient = jnp.einsum(
        "td,qd->tq", d_branch, w_out, preferred_element_type=jnp.float32
    ).astype(jnp.bfloat16)
    mixed_part, merged_gradient = lax.optimization_barrier((mixed_part, merged_gradient))
    d_query_low, d_key_prompt, d_value_prompt, d_key_cont, d_value_cont = attend_backward(
        query_row_block, merged_gradient, merged_low, log_total, *keys_values, cosine, sine,
        key_cosine, key_sine, start, prompt_rows, cont_len,
    )
    mixed, d_key_prompt = finish_scatter(mixed_part, d_key_prompt, d_key_prompt, lambda v: v)
    output = resid + mixed
    y_prompt = output[:prompt_rows].astype(jnp.bfloat16)[None]
    y_cont = output[prompt_rows:].reshape(1, cont_count, cont_len, model_width).astype(jnp.bfloat16)
    d_key_prompt, d_value_prompt = scatter_keys(d_key_prompt, d_value_prompt, prompt_rows)
    d_key_low = jnp.concatenate([d_key_prompt, d_key_cont], axis=0)
    d_value_low = jnp.concatenate([d_value_prompt, d_value_cont], axis=0)
    grad_query = jnp.einsum("td,tq->dq", h1_low, d_query_low, preferred_element_type=jnp.float32)
    grad_key = jnp.einsum("td,tq->dq", h1_low, d_key_low, preferred_element_type=jnp.float32)
    grad_value = jnp.einsum("td,tq->dq", h1_low, d_value_low, preferred_element_type=jnp.float32)
    d_normed_one = jnp.einsum("tq,dq->td", d_query_low, w_query, preferred_element_type=jnp.float32)
    d_normed_one = d_normed_one + jnp.einsum(
        "tq,dq->td", d_key_low, key_weight, preferred_element_type=jnp.float32
    )
    d_normed_one = d_normed_one + jnp.einsum(
        "tq,dq->td", d_value_low, value_weight, preferred_element_type=jnp.float32
    )
    d_tokens_norm, grad_norm1 = rms_backward(tokens, scale_one, gain_one, d_normed_one)
    d_tokens = d_resid + d_tokens_norm
    dx_prompt = d_tokens[:prompt_rows][None]
    dx_cont = d_tokens[prompt_rows:].reshape(1, cont_count, cont_len, model_width)
    wide = jnp.concatenate([grad_query, grad_key, grad_value, grad_out], axis=1)
    small = jnp.concatenate([grad_router, grad_norm1[:, None], grad_norm2[:, None]], axis=1)
    small = jnp.pad(small, ((0, 0), (0, -small.shape[1] % 128)))
    dense = jnp.concatenate([wide, small], axis=1).astype(jnp.bfloat16)
    dense = lax.psum_scatter(dense, ("dp", "ctx"), scatter_dimension=0, tiled=True)
    dense = lax.psum(dense, "expert").astype(jnp.float32)
    heads_width = QUERY_HEADS * HEAD_SIZE
    edge = heads_width + 2 * key_value_width
    tail = edge + w_out.shape[1]
    return (
        y_prompt,
        y_cont,
        dx_prompt,
        dx_cont,
        dense[:, tail + expert_total],
        dense[:, :heads_width],
        dense[:, heads_width : heads_width + key_value_width],
        dense[:, heads_width + key_value_width : edge],
        dense[:, edge:tail],
        dense[:, tail + expert_total + 1],
        dense[:, tail : tail + expert_total],
        grad_gate_up,
        grad_down,
    )


def solution(mesh):
    return jax.shard_map(
        per_device,
        mesh=mesh,
        in_specs=(
            P(("dp", "expert"), "ctx", None),
            P(("dp", "expert"), "ctx", None, None),
            P(),
            P(),
            P(),
            P(),
            P(),
            P(),
            P(),
            P("expert", None, None),
            P("expert", None, None),
            P(("dp", "expert"), "ctx", None),
            P(("dp", "expert"), "ctx", None, None),
            P(("dp", "expert"), "ctx", None),
            P(("dp", "expert"), "ctx", None),
            P(("dp", "expert"), "ctx", None, None),
        ),
        out_specs=(
            P(("dp", "expert"), "ctx", None),
            P(("dp", "expert"), "ctx", None, None),
            P(("dp", "expert"), "ctx", None),
            P(("dp", "expert"), "ctx", None, None),
            P(("dp", "ctx")),
            P(("dp", "ctx"), None),
            P(("dp", "ctx"), None),
            P(("dp", "ctx"), None),
            P(("dp", "ctx"), None),
            P(("dp", "ctx")),
            P(("dp", "ctx"), None),
            P("expert", ("dp", "ctx"), None),
            P("expert", ("dp", "ctx"), None),
        ),
        check_vma=False,
    )
```

```python
from functools import partial

import jax
import jax.numpy as jnp
from jax import lax
from jax.experimental import pallas as pl
from jax.experimental.pallas import tpu as pltpu
from jax.sharding import PartitionSpec as P

QUERY_HEADS = 24
KEY_VALUE_HEADS = 8
HEAD_SIZE = 64


EPS = 1e-06
RESID = 0.22
ATT_SCALE = 0.015625
THETA = 10000.0
NEG = -1e30


def rope_tables(positions, head_dim):
    half_dim = head_dim // 2
    frequency = THETA ** (-(jnp.arange(half_dim, dtype=jnp.float32) * 2.0 / head_dim))
    angles = positions[:, None] * frequency[None, :]
    cosine_lookup = jnp.concatenate([jnp.cos(angles), jnp.cos(angles)], axis=-1)
    sine_lookup = jnp.concatenate([jnp.sin(angles), jnp.sin(angles)], axis=-1)
    return (cosine_lookup, sine_lookup)


def signed_tables(positions, width):
    cosine_lookup, sine_lookup = rope_tables(positions, HEAD_SIZE)
    half_dim = HEAD_SIZE // 2
    sine_lookup = jnp.concatenate([-sine_lookup[:, :half_dim], sine_lookup[:, half_dim:]], axis=-1)
    copies = width // HEAD_SIZE
    return (jnp.tile(cosine_lookup, (1, copies)), jnp.tile(sine_lookup, (1, copies)))


def rms_forward(values, norm_gain):
    inverse = lax.rsqrt(jnp.mean(values * values, axis=-1, keepdims=True) + EPS)
    return (values * inverse * norm_gain, inverse)


def rms_backward(values, inverse, norm_gain, upstream):
    normed = values * inverse
    weighted = upstream * norm_gain
    projected = jnp.mean(weighted * normed, axis=-1, keepdims=True)
    return (inverse * (weighted - normed * projected), jnp.sum(upstream * normed, axis=0))


def slot_codes(routes, visit_order, experts, capacity):
    count = routes.shape[0]
    ids = jnp.arange(count, dtype=jnp.int32)
    visit = jnp.arange(count, dtype=jnp.float32)
    place = (visit_order[:, None] == ids[None, :]).astype(jnp.float32)
    place_row = jnp.sum(place * visit[:, None], axis=0)
    place_col = jnp.sum((visit_order[None, :] == ids[:, None]).astype(jnp.float32) * visit[None, :], axis=1)
    earlier = (place_col[:, None] < place_row[None, :]).astype(jnp.bfloat16)
    named = jnp.any(
        routes.T[None, :, :] == jnp.arange(experts, dtype=jnp.int32)[:, None, None], axis=1
    )
    rank = jnp.dot(named.astype(jnp.bfloat16), earlier, preferred_element_type=jnp.float32)
    return jnp.where(named, jnp.where(rank < capacity, rank, -1.0), -2.0)


def selection(codes, own, slots):
    tokens = codes.shape[-1]
    slot_index = lax.broadcasted_iota(jnp.int32, (slots, tokens), 0).astype(jnp.float32)
    picks = [
        jnp.where(codes[e : e + 1, :] == slot_index, 1.0, 0.0).astype(jnp.bfloat16)
        for e in range(own)
    ]
    return jnp.concatenate(picks, axis=0)


def dispatch_body(own, slots, codes_ref, rows_ref, out_ref):
    pick = selection(codes_ref[0], own, slots)
    moved = jnp.dot(pick, rows_ref[0], preferred_element_type=jnp.float32).astype(jnp.bfloat16)
    for e in range(own):
        out_ref[e] = moved[e * slots : (e + 1) * slots]


def dispatch(codes, rows, own, slots):
    blocks, tokens, width = rows.shape
    return pl.pallas_call(
        partial(dispatch_body, own, slots),
        grid=(blocks,),
        in_specs=[
            pl.BlockSpec((1, codes.shape[1], tokens), lambda b: (b, 0, 0)),
            pl.BlockSpec((1, tokens, width), lambda b: (b, 0, 0)),
        ],
        out_specs=pl.BlockSpec((own, slots, width), lambda b: (0, b, 0)),
        out_shape=jax.ShapeDtypeStruct((own, blocks * slots, width), jnp.bfloat16),
        cost_estimate=pl.CostEstimate(
            flops=2 * blocks * own * slots * tokens * width,
            transcendentals=0,
            bytes_accessed=2 * blocks * (tokens + own * slots) * width,
        ),
        name="dispatch",
    )(codes, rows)


def combine_body(own, slots, at_ref, codes_ref, rows_ref, out_ref):
    pick = selection(codes_ref[0], own, slots)
    rows = rows_ref[...].reshape(own * slots, rows_ref.shape[-1])
    out_ref[0] = lax.dot_general(
        pick, rows, (((0,), (0,)), ((), ())), preferred_element_type=jnp.float32
    ).astype(out_ref.dtype)


def combine(at, codes, rows, own, slots):
    count, tokens = at.shape[0], codes.shape[2]
    width = rows.shape[-1]
    return pl.pallas_call(
        partial(combine_body, own, slots),
        grid_spec=pltpu.PrefetchScalarGridSpec(
            num_scalar_prefetch=1,
            grid=(count,),
            in_specs=[
                pl.BlockSpec((1, codes.shape[1], tokens), lambda b, at: (at[b], 0, 0)),
                pl.BlockSpec((own, slots, width), lambda b, at: (0, at[b], 0)),
            ],
            out_specs=pl.BlockSpec((1, tokens, width), lambda b, at: (b, 0, 0)),
        ),
        out_shape=jax.ShapeDtypeStruct((count, tokens, width), jnp.bfloat16),
        cost_estimate=pl.CostEstimate(
            flops=2 * count * own * slots * tokens * width,
            transcendentals=0,
            bytes_accessed=2 * count * (tokens + own * slots) * width,
        ),
        name="combine",
    )(at, codes, rows)


def swap(values, axis, bit):
    size = lax.axis_size(axis)
    return lax.ppermute(values, axis, [(i, i ^ bit) for i in range(size)])


def added(left, right):
    return (left.astype(jnp.float32) + right.astype(jnp.float32)).astype(jnp.bfloat16)


def start_scatter(codes, rows, own, slots, group):
    blocks = codes.shape[0]
    if group != ("ctx", "expert") or lax.axis_size("ctx") != 4 or lax.axis_size("expert") != 2:
        every = jnp.arange(blocks, dtype=jnp.int32)
        return lax.psum_scatter(
            combine(every, codes, rows, own, slots), group, scatter_dimension=0
        )
    here = lax.axis_index(group).astype(jnp.int32)
    far = here ^ jnp.array([2, 3, 6, 7], jnp.int32)
    near = here ^ jnp.array([0, 1, 4, 5], jnp.int32)
    sent = swap(combine(far, codes, rows, own, slots), "ctx", 1)
    return added(combine(near, codes, rows, own, slots), sent)


def finish_scatter(part, middle=None, later=None, work=None):
    if part.ndim == 2:
        return part.astype(jnp.float32), None if work is None else work(later)
    half = part.shape[-1] // 2
    left, right = part[:, :, :half], part[:, :, half:]
    left_sent = swap(left[2:], "ctx", 2)
    right_sent = swap(jnp.stack([right[1], right[3]]), "expert", 1)
    if work is not None:
        left_sent, right_sent, _, later = lax.optimization_barrier(
            (left_sent, right_sent, middle, later)
        )
    left_on = swap(added(left[1], left_sent[1]), "expert", 1)
    right_on = swap(added(right[2], right_sent[1]), "ctx", 2)
    made = None
    if work is not None:
        left_on, right_on, made = lax.optimization_barrier((left_on, right_on, work(later)))
    wide = lambda *pieces: sum(piece.astype(jnp.float32) for piece in pieces)
    whole = jnp.concatenate(
        [wide(left[0], left_sent[0], left_on), wide(right[0], right_sent[0], right_on)], axis=1
    )
    return whole, made


def lane_half(shape):
    return lax.broadcasted_iota(jnp.int32, shape, 1) // HEAD_SIZE


def turn(values, cosine, sine):
    half_dim = HEAD_SIZE // 2
    width = values.shape[1]
    lane = lax.broadcasted_iota(jnp.int32, values.shape, 1) % HEAD_SIZE
    partner = jnp.where(
        lane < half_dim,
        pltpu.roll(values, width - half_dim, 1),
        pltpu.roll(values, half_dim, 1),
    )
    return values * cosine + partner * sine


def to_key_half(values, swap, key_half):
    moved = jnp.where(swap, pltpu.roll(values, HEAD_SIZE, 1), values)
    return jnp.where(lane_half(values.shape) == key_half, moved, 0.0)


def head_place(group):
    head = pl.program_id(0)
    key_half = (head // group) % 2
    return head, key_half, (head % 2) != key_half


def attend_forward_body(
    group, prompt_rows, cont_len, pos_ref, q_ref, cos_ref, sin_ref, kp_ref, vp_ref, kc_ref, vc_ref,
    qr_ref, out_ref, log_ref,
):
    head, key_half, swap = head_place(group)
    rotated = turn(q_ref[...], cos_ref[...], sin_ref[...]).astype(jnp.bfloat16)
    qr_ref[...] = rotated
    query = to_key_half(rotated.astype(jnp.float32), swap, key_half) * ATT_SCALE
    query = query.astype(jnp.bfloat16)
    nt = (((1,), (1,)), ((), ()))

    def finish(parts, rows):
        highest = parts[0][0].max(axis=1, keepdims=True)
        for scores, _ in parts[1:]:
            highest = jnp.maximum(highest, scores.max(axis=1, keepdims=True))
        lifted = [jnp.exp(scores - highest) for scores, _ in parts]
        total = lifted[0].sum(axis=1, keepdims=True)
        for piece in lifted[1:]:
            total = total + piece.sum(axis=1, keepdims=True)
        inverse = 1.0 / total
        result = None
        for piece, (_, value) in zip(lifted, parts):
            term = jnp.dot(
                (piece * inverse).astype(jnp.bfloat16), value, preferred_element_type=jnp.float32
            )
            result = term if result is None else result + term
        log_total = jnp.broadcast_to(highest + jnp.log(total), (total.shape[0], 128))
        log_ref[0, :, rows] = jnp.transpose(log_total)[:8]
        keep = jnp.where(lane_half(result.shape) == key_half, result, 0.0)
        keep = jnp.where(swap, pltpu.roll(keep, HEAD_SIZE, 1), keep).astype(jnp.bfloat16)

        @pl.when(head % 2 == 0)
        def _():
            out_ref[rows, :] = keep

        @pl.when(head % 2 == 1)
        def _():
            out_ref[rows, :] = out_ref[rows, :] + keep

    total_rows = q_ref.shape[0]
    first = lax.dot_general(
        query[:prompt_rows], kp_ref[...], nt, preferred_element_type=jnp.float32
    )
    row = lax.broadcasted_iota(jnp.int32, first.shape, 0) + pos_ref[0]
    first = jnp.where(lax.broadcasted_iota(jnp.int32, first.shape, 1) <= row, first, NEG)
    finish([(first, vp_ref[...])], pl.ds(0, prompt_rows))
    lower = query[prompt_rows:]
    wide = lax.dot_general(lower, kp_ref[...], nt, preferred_element_type=jnp.float32)
    near = lax.dot_general(lower, kc_ref[...], nt, preferred_element_type=jnp.float32)
    row = lax.broadcasted_iota(jnp.int32, near.shape, 0)
    col = lax.broadcasted_iota(jnp.int32, near.shape, 1)
    near = jnp.where((col <= row) & (col // cont_len == row // cont_len), near, NEG)
    finish([(wide, vp_ref[...]), (near, vc_ref[...])], pl.ds(prompt_rows, total_rows - prompt_rows))


def attend_forward(q_lin, key_prompt, value_prompt, key_cont, value_cont, cosine, sine, start, rows, cont_len):
    tokens, width = q_lin.shape
    heads = width // HEAD_SIZE
    group = heads // (key_prompt.shape[1] // HEAD_SIZE)
    keys, near = key_prompt.shape[0], key_cont.shape[0]
    tile = lambda h, *_: (0, h // 2)
    key_tile = lambda h, *_: (0, h // (2 * group))
    same = lambda h, *_: (0, 0)
    return pl.pallas_call(
        partial(attend_forward_body, group, rows, cont_len),
        grid_spec=pltpu.PrefetchScalarGridSpec(
            num_scalar_prefetch=1,
            grid=(heads,),
            in_specs=[
                pl.BlockSpec((tokens, 128), tile),
                pl.BlockSpec((tokens, 128), same),
                pl.BlockSpec((tokens, 128), same),
                pl.BlockSpec((keys, 128), key_tile),
                pl.BlockSpec((keys, 128), key_tile),
                pl.BlockSpec((near, 128), key_tile),
                pl.BlockSpec((near, 128), key_tile),
            ],
            out_specs=[
                pl.BlockSpec((tokens, 128), tile),
                pl.BlockSpec((tokens, 128), tile),
                pl.BlockSpec((1, 8, tokens), lambda h, *_: (h, 0, 0)),
            ],
        ),
        out_shape=[
            jax.ShapeDtypeStruct((tokens, width), jnp.bfloat16),
            jax.ShapeDtypeStruct((tokens, width), jnp.bfloat16),
            jax.ShapeDtypeStruct((heads, 8, tokens), jnp.float32),
        ],
        cost_estimate=pl.CostEstimate(
            flops=4 * heads * tokens * (keys + near) * 128,
            transcendentals=heads * tokens * (keys + near),
            bytes_accessed=8 * tokens * width,
        ),
        name="attend_forward",
    )(start, q_lin, cosine, sine, key_prompt, value_prompt, key_cont, value_cont)


def attend_backward_body(
    group, prompt_rows, cont_len, chunk, pos_ref, q_ref, do_ref, out_ref, log_ref, cos_ref, sin_ref,
    kcos_ref, ksin_ref, kp_ref, vp_ref, kc_ref, vc_ref,
    dq_ref, dkp_ref, dvp_ref, dkc_ref, dvc_ref, dk_acc, dv_acc,
):
    head, key_half, swap = head_place(group)
    tokens = q_ref.shape[0]
    keys = kp_ref.shape[0]
    near = kc_ref.shape[0]
    nt = (((1,), (1,)), ((), ()))
    tn = (((0,), (0,)), ((), ()))

    @pl.when(head % (2 * group) == 0)
    def _():
        dk_acc[...] = jnp.zeros_like(dk_acc)
        dv_acc[...] = jnp.zeros_like(dv_acc)

    query = to_key_half(q_ref[...].astype(jnp.float32), swap, key_half) * ATT_SCALE
    query = query.astype(jnp.bfloat16)
    d_out = to_key_half(do_ref[...].astype(jnp.float32), swap, key_half)
    result = to_key_half(out_ref[...].astype(jnp.float32), swap, key_half)
    centre = jnp.transpose(
        jnp.broadcast_to(jnp.sum(d_out * result, axis=1, keepdims=True), (tokens, 128))
    )[:1]
    d_out = d_out.astype(jnp.bfloat16)
    log_total = log_ref[0][:1]
    row = lax.broadcasted_iota(jnp.int32, (1, tokens), 1)
    limit = jnp.where(row < prompt_rows, row + pos_ref[0], keys)

    def step(key, value, query, d_out, log_total, centre, allowed, at, count):
        scores = lax.dot_general(key, query, nt, preferred_element_type=jnp.float32)
        scores = jnp.where(allowed(scores.shape), scores, NEG)
        weights = jnp.exp(scores - log_total)
        d_weights = lax.dot_general(value, d_out, nt, preferred_element_type=jnp.float32)
        d_scores = (weights * (d_weights - centre)).astype(jnp.bfloat16)
        dv_acc[at : at + count] += jnp.dot(
            weights.astype(jnp.bfloat16), d_out, preferred_element_type=jnp.float32
        )
        dk_acc[at : at + count] += jnp.dot(d_scores, query, preferred_element_type=jnp.float32)
        return lax.dot_general(d_scores, key, tn, preferred_element_type=jnp.float32)

    d_query = jnp.zeros((tokens, 128), jnp.float32)
    for at in range(0, keys, chunk):

        def seen(shape, at=at):
            return lax.broadcasted_iota(jnp.int32, shape, 0) + at <= limit

        d_query = d_query + step(
            kp_ref[at : at + chunk], vp_ref[at : at + chunk], query, d_out, log_total, centre, seen,
            at, chunk,
        )

    def nearby(shape):
        key_at = lax.broadcasted_iota(jnp.int32, shape, 0)
        query_at = lax.broadcasted_iota(jnp.int32, shape, 1)
        return (key_at <= query_at) & (key_at // cont_len == query_at // cont_len)

    tail = step(
        kc_ref[...], vc_ref[...], query[prompt_rows:], d_out[prompt_rows:],
        log_total[:, prompt_rows:], centre[:, prompt_rows:], nearby, keys, near,
    )
    d_query = jnp.concatenate([d_query[:prompt_rows], d_query[prompt_rows:] + tail], axis=0)
    d_query = jnp.where(lane_half(d_query.shape) == key_half, d_query * ATT_SCALE, 0.0)
    d_query = jnp.where(swap, pltpu.roll(d_query, HEAD_SIZE, 1), d_query)
    d_query = turn(d_query, cos_ref[...], -sin_ref[...]).astype(jnp.bfloat16)

    @pl.when(head % 2 == 0)
    def _():
        dq_ref[...] = d_query

    @pl.when(head % 2 == 1)
    def _():
        dq_ref[...] = dq_ref[...] + d_query

    @pl.when(head % (2 * group) == 2 * group - 1)
    def _():
        dk = turn(dk_acc[...], kcos_ref[...], -ksin_ref[...]).astype(jnp.bfloat16)
        dv = dv_acc[...].astype(jnp.bfloat16)
        dkp_ref[...] = dk[:keys]
        dkc_ref[...] = dk[keys:]
        dvp_ref[...] = dv[:keys]
        dvc_ref[...] = dv[keys:]


def attend_backward(
    query, d_out, result, log_total, key_prompt, value_prompt, key_cont, value_cont, cosine, sine,
    key_cosine, key_sine, start, rows, cont_len,
):
    tokens, width = query.shape
    heads = width // HEAD_SIZE
    key_width = key_prompt.shape[1]
    group = heads // (key_width // HEAD_SIZE)
    keys, near = key_prompt.shape[0], key_cont.shape[0]
    chunk = min(256, keys)
    tile = lambda h, *_: (0, h // 2)
    key_tile = lambda h, *_: (0, h // (2 * group))
    same = lambda h, *_: (0, 0)
    return pl.pallas_call(
        partial(attend_backward_body, group, rows, cont_len, chunk),
        grid_spec=pltpu.PrefetchScalarGridSpec(
            num_scalar_prefetch=1,
            grid=(heads,),
            in_specs=[
                pl.BlockSpec((tokens, 128), tile),
                pl.BlockSpec((tokens, 128), tile),
                pl.BlockSpec((tokens, 128), tile),
                pl.BlockSpec((1, 8, tokens), lambda h, *_: (h, 0, 0)),
                pl.BlockSpec((tokens, 128), same),
                pl.BlockSpec((tokens, 128), same),
                pl.BlockSpec((keys + near, 128), same),
                pl.BlockSpec((keys + near, 128), same),
                pl.BlockSpec((keys, 128), key_tile),
                pl.BlockSpec((keys, 128), key_tile),
                pl.BlockSpec((near, 128), key_tile),
                pl.BlockSpec((near, 128), key_tile),
            ],
            out_specs=[
                pl.BlockSpec((tokens, 128), tile),
                pl.BlockSpec((keys, 128), key_tile),
                pl.BlockSpec((keys, 128), key_tile),
                pl.BlockSpec((near, 128), key_tile),
                pl.BlockSpec((near, 128), key_tile),
            ],
            scratch_shapes=[
                pltpu.VMEM((keys + near, 128), jnp.float32),
                pltpu.VMEM((keys + near, 128), jnp.float32),
            ],
        ),
        out_shape=[
            jax.ShapeDtypeStruct((tokens, width), jnp.bfloat16),
            jax.ShapeDtypeStruct((keys, key_width), jnp.bfloat16),
            jax.ShapeDtypeStruct((keys, key_width), jnp.bfloat16),
            jax.ShapeDtypeStruct((near, key_width), jnp.bfloat16),
            jax.ShapeDtypeStruct((near, key_width), jnp.bfloat16),
        ],
        cost_estimate=pl.CostEstimate(
            flops=10 * heads * tokens * (keys + near) * 128,
            transcendentals=heads * tokens * (keys + near),
            bytes_accessed=8 * tokens * width,
        ),
        name="attend_backward",
    )(
        start, query, d_out, result, log_total, cosine, sine, key_cosine, key_sine, key_prompt,
        value_prompt, key_cont, value_cont,
    )


def reduce_experts(grad, split):
    if split == 1:
        return lax.psum_scatter(
            grad, ("dp", "ctx"), scatter_dimension=1, tiled=True
        ).astype(jnp.float32)
    part = lax.psum_scatter(grad, "dp", scatter_dimension=1, tiled=True)
    return lax.all_to_all(part, "ctx", split_axis=1, concat_axis=0, tiled=True).astype(jnp.float32)


def scatter_keys(d_key, d_value, rows):
    size = lax.axis_size("ctx")
    here = lax.axis_index("ctx")

    def share(owner):
        return jnp.concatenate(
            [
                lax.dynamic_slice_in_dim(d_key, owner * rows, rows, axis=0),
                lax.dynamic_slice_in_dim(d_value, owner * rows, rows, axis=0),
            ],
            axis=1,
        )

    total = share(here).astype(jnp.float32)
    for hop in range(1, size):
        moved = lax.ppermute(
            share((here + hop) % size), "ctx", [(i, (i + hop) % size) for i in range(size)]
        )
        total = total + moved.astype(jnp.float32)
    total = total.astype(jnp.bfloat16)
    return (total[:, : d_key.shape[1]], total[:, d_key.shape[1] :])


def fold_dense(grad, cut):
    rows, width = grad.shape
    parts = lax.axis_size("dp")
    core = lax.axis_index("ctx") % 2
    pair = lax.axis_index("ctx") // 2
    side = lax.axis_index("expert")
    take = partial(lax.dynamic_index_in_dim, keepdims=False)
    grad = grad.reshape(parts, 2, 2, 2, rows // (8 * parts), width)
    one = added(take(grad, core, 2), swap(take(grad, 1 - core, 2), "ctx", 1))
    left, right = one[..., :cut], one[..., cut:]
    left_sent = swap(take(left, 1 - pair, 1), "ctx", 2)
    right_sent = swap(take(right, 1 - side, 2), "expert", 1)
    left = added(take(left, pair, 1), left_sent)
    right = added(take(right, side, 2), right_sent)
    left_sent = swap(take(left, 1 - side, 1), "expert", 1)
    right_sent = swap(take(right, 1 - pair, 1), "ctx", 2)
    return jnp.concatenate(
        [added(take(left, side, 1), left_sent), added(take(right, pair, 1), right_sent)], axis=-1
    )


def finish_dense(grad, folded):
    if not folded:
        return lax.psum(grad, "expert").astype(jnp.float32)
    other = swap(grad, "expert", 1)
    first = lax.axis_index("expert") == 0
    return jnp.concatenate(
        [jnp.where(first, grad, other), jnp.where(first, other, grad)], axis=0
    ).astype(jnp.float32)


def start_dense(grad, cut):
    parts = lax.axis_size("dp")
    folded = (
        lax.axis_size("ctx") == 4
        and lax.axis_size("expert") == 2
        and grad.shape[0] % (64 * parts) == 0
    )
    if not folded:
        return lax.psum_scatter(grad, ("dp", "ctx"), scatter_dimension=0, tiled=True), False
    return lax.psum_scatter(fold_dense(grad, cut), "dp", scatter_dimension=0), True


def per_device(
    x_prompt,
    x_cont,
    norm1_gain,
    w_query,
    key_weight,
    value_weight,
    w_out,
    norm2_gain,
    w_router,
    w_gate_up,
    w_down,
    routes_prompt,
    routes_cont,
    slot_order,
    dy_prompt,
    dy_cont,
):
    model_width = x_prompt.shape[2]
    prompt_rows = x_prompt.shape[1]
    cont_count = x_cont.shape[1]
    cont_len = x_cont.shape[2]
    cont_rows = cont_count * cont_len
    count_of_tokens = prompt_rows + cont_rows
    key_value_width = KEY_VALUE_HEADS * HEAD_SIZE
    local_experts = w_gate_up.shape[0]
    expert_groups = lax.axis_size("expert")
    expert_total = local_experts * expert_groups
    top_count = routes_prompt.shape[2]
    capacity = (count_of_tokens * top_count + expert_total - 1) // expert_total
    hidden_units = w_down.shape[1]
    prompt_total = prompt_rows * lax.axis_size("ctx")
    count_of_keys = prompt_total + cont_rows
    split = lax.axis_size("ctx") if local_experts % lax.axis_size("ctx") == 0 else 1
    own = local_experts // split
    blocks = split * expert_groups
    slots = -(-capacity // 8) * 8
    group = ("ctx", "expert") if split > 1 else ("expert",)
    block_index = lax.axis_index(group)
    own_offset = lax.axis_index("ctx") * own if split > 1 else 0
    first_expert = lax.axis_index("expert") * local_experts + own_offset
    gate_up_own = w_gate_up
    down_own = w_down
    if split > 1:
        gate_up_own = lax.dynamic_slice_in_dim(w_gate_up, own_offset, own, axis=0)
        down_own = lax.dynamic_slice_in_dim(w_down, own_offset, own, axis=0)
    routes = jnp.concatenate(
        [routes_prompt[0], routes_cont[0].reshape(cont_rows, top_count)], axis=0
    )
    codes_all = lax.all_gather(
        slot_codes(routes, slot_order[0, 0], expert_total, capacity), group, axis=0, tiled=False
    )
    own_codes = lax.dynamic_slice_in_dim(codes_all, first_expert, own, axis=1)
    own_codes = jnp.pad(own_codes, ((0, 0), (0, -own % 8), (0, 0)), constant_values=-2.0)
    upstream_low = jnp.concatenate([dy_prompt[0], dy_cont[0].reshape(cont_rows, model_width)], axis=0)
    upstream = upstream_low.astype(jnp.float32)
    upstream_all = lax.all_gather(upstream_low, group, axis=0, tiled=False)
    d_slot_rows = dispatch(own_codes, upstream_all, own, slots)
    d_plain = jnp.einsum("ecd,efd->ecf", d_slot_rows, down_own, preferred_element_type=jnp.float32)
    gain_one = norm1_gain.astype(jnp.float32)
    gain_two = norm2_gain.astype(jnp.float32)
    tokens = jnp.concatenate(
        [x_prompt[0], x_cont[0].reshape(cont_rows, model_width)], axis=0
    ).astype(jnp.float32)
    normed_one, scale_one = rms_forward(tokens, gain_one)
    h1_low = normed_one.astype(jnp.bfloat16)
    q_lin = jnp.dot(h1_low, w_query, preferred_element_type=jnp.float32)
    key_linear = jnp.dot(h1_low, key_weight, preferred_element_type=jnp.float32)
    value_linear = jnp.dot(h1_low, value_weight, preferred_element_type=jnp.float32)
    row_index = jnp.arange(count_of_tokens, dtype=jnp.int32)
    cont_offset = row_index - prompt_rows
    start = lax.axis_index("ctx") * prompt_rows
    query_pos = jnp.where(
        cont_offset >= 0, prompt_total + cont_offset % cont_len, start + row_index
    )
    key_index = jnp.arange(count_of_keys, dtype=jnp.int32)
    key_pos = jnp.where(
        key_index >= prompt_total, prompt_total + (key_index - prompt_total) % cont_len, key_index
    )
    start = start.astype(jnp.int32)[None]
    cosine, sine = signed_tables(query_pos.astype(jnp.float32), 128)
    key_cosine, key_sine = signed_tables(key_pos.astype(jnp.float32), 128)
    wide_cosine, wide_sine = signed_tables(query_pos.astype(jnp.float32), key_value_width)
    half_dim = HEAD_SIZE // 2
    lane = jnp.arange(key_value_width, dtype=jnp.int32) % HEAD_SIZE
    partner = jnp.where(
        lane < half_dim, jnp.roll(key_linear, -half_dim, axis=1), jnp.roll(key_linear, half_dim, axis=1)
    )
    key_row_block = (key_linear * wide_cosine + partner * wide_sine).astype(jnp.bfloat16)
    value_row_block = value_linear.astype(jnp.bfloat16)
    prompt_kv = lax.all_gather(
        jnp.stack([key_row_block[:prompt_rows], value_row_block[:prompt_rows]]),
        "ctx",
        axis=1,
        tiled=True,
    )
    keys_values = (
        prompt_kv[0], prompt_kv[1], key_row_block[prompt_rows:], value_row_block[prompt_rows:]
    )
    query_row_block, merged_low, log_total = attend_forward(
        q_lin, *keys_values, cosine, sine, start, prompt_rows, cont_len
    )
    branch = jnp.dot(merged_low, w_out, preferred_element_type=jnp.float32)
    resid = tokens + RESID * branch
    normed_two, scale_two = rms_forward(resid, gain_two)
    h2_low = normed_two.astype(jnp.bfloat16)
    rows_all = lax.all_gather(h2_low, group, axis=0, tiled=False)
    rows_all, d_plain = lax.optimization_barrier((rows_all, d_plain))
    slot_rows = dispatch(own_codes, rows_all, own, slots)
    logits = jnp.einsum("btd,de->bet", rows_all, w_router, preferred_element_type=jnp.float32)
    named = codes_all > -1.5
    logits = jnp.where(named, logits, NEG)
    lifted = jnp.where(named, jnp.exp(logits - jnp.max(logits, axis=1, keepdims=True)), 0.0)
    gates_all = lifted / jnp.sum(lifted, axis=1, keepdims=True)
    own_gates = lax.dynamic_slice_in_dim(gates_all, first_expert, own, axis=1)
    gates = lax.dynamic_index_in_dim(gates_all, block_index, 0, keepdims=False)
    slot_index = jnp.arange(slots, dtype=jnp.int32).astype(jnp.float32)
    picked = own_codes[:, :own, None, :] == slot_index[None, None, :, None]
    slot_gate = jnp.sum(jnp.where(picked, own_gates[:, :, None, :], 0.0), axis=-1)
    slot_gate = slot_gate.transpose(1, 0, 2).reshape(own, blocks * slots)
    both = jnp.einsum("ecd,edf->ecf", slot_rows, gate_up_own, preferred_element_type=jnp.float32)
    gate_part = both[..., :hidden_units]
    up_part = both[..., hidden_units:]
    weight = RESID * slot_gate[:, :, None]
    logistic = jax.nn.sigmoid(gate_part)
    silu = gate_part * logistic
    hidden = silu * up_part
    d_slot_gate = RESID * jnp.sum(hidden * d_plain, axis=-1)
    weighted = (weight * hidden).astype(jnp.bfloat16)
    d_hidden = weight * d_plain
    d_gate = d_hidden * up_part * logistic * (1.0 + gate_part * (1.0 - logistic))
    d_both = jnp.concatenate([d_gate, d_hidden * silu], axis=-1).astype(jnp.bfloat16)
    grad_down = jnp.einsum(
        "ecf,ecd->efd", weighted, d_slot_rows, preferred_element_type=jnp.float32
    ).astype(jnp.bfloat16)
    d_both, grad_down = lax.optimization_barrier((d_both, grad_down))
    grad_down = reduce_experts(grad_down, split)
    d_slots = jnp.einsum(
        "ecf,edf->ecd", d_both, gate_up_own, preferred_element_type=jnp.float32
    ).astype(jnp.bfloat16)
    d_rows_parts, weighted, slot_rows = lax.optimization_barrier(
        (start_scatter(own_codes, d_slots, own, slots, group), weighted, slot_rows)
    )
    grad_gate_up = jnp.einsum(
        "ecd,ecf->edf", slot_rows, d_both, preferred_element_type=jnp.float32
    ).astype(jnp.bfloat16)

    def forward_rows(weighted):
        expert_out = jnp.einsum(
            "ecf,efd->ecd", weighted, down_own, preferred_element_type=jnp.float32
        ).astype(jnp.bfloat16)
        return start_scatter(own_codes, expert_out, own, slots, group)

    d_rows, mixed_part = finish_scatter(d_rows_parts, grad_gate_up, weighted, forward_rows)
    d_gates_own = jnp.sum(
        jnp.where(
            picked,
            d_slot_gate.reshape(own, blocks, slots).transpose(1, 0, 2)[..., None],
            0.0,
        ),
        axis=2,
    )
    d_gates = lax.psum_scatter(
        lax.dynamic_update_slice_in_dim(
            jnp.zeros((blocks, expert_total, count_of_tokens), jnp.float32),
            d_gates_own,
            first_expert,
            axis=1,
        ),
        group,
        scatter_dimension=0,
    )
    grad_gate_up = reduce_experts(grad_gate_up, split)
    d_logits = (
        gates * (d_gates - jnp.sum(gates * d_gates, axis=0, keepdims=True))
    ).astype(jnp.bfloat16)
    grad_router = jnp.einsum("td,et->de", h2_low, d_logits, preferred_element_type=jnp.float32)
    d_normed_two = d_rows + jnp.einsum(
        "et,de->td", d_logits, w_router, preferred_element_type=jnp.float32
    )
    d_resid_norm, grad_norm2 = rms_backward(resid, scale_two, gain_two, d_normed_two)
    d_resid = upstream + d_resid_norm
    d_branch = (RESID * d_resid).astype(jnp.bfloat16)
    grad_out = jnp.einsum(
        "tq,td->qd", merged_low, d_branch, preferred_element_type=jnp.float32
    ).astype(jnp.bfloat16)
    grad_out = start_dense(grad_out, grad_out.shape[1] // 256 * 128)
    merged_gradient = jnp.einsum(
        "td,qd->tq", d_branch, w_out, preferred_element_type=jnp.float32
    ).astype(jnp.bfloat16)
    mixed_part, merged_gradient = lax.optimization_barrier((mixed_part, merged_gradient))
    d_query_low, d_key_prompt, d_value_prompt, d_key_cont, d_value_cont = attend_backward(
        query_row_block, merged_gradient, merged_low, log_total, *keys_values, cosine, sine,
        key_cosine, key_sine, start, prompt_rows, cont_len,
    )
    mixed, d_key_prompt = finish_scatter(mixed_part, d_key_prompt, d_key_prompt, lambda v: v)
    output = resid + mixed
    y_prompt = output[:prompt_rows].astype(jnp.bfloat16)[None]
    y_cont = output[prompt_rows:].reshape(1, cont_count, cont_len, model_width).astype(jnp.bfloat16)
    d_key_prompt, d_value_prompt = scatter_keys(d_key_prompt, d_value_prompt, prompt_rows)
    d_key_low = jnp.concatenate([d_key_prompt, d_key_cont], axis=0)
    d_value_low = jnp.concatenate([d_value_prompt, d_value_cont], axis=0)
    grad_query = jnp.einsum("td,tq->dq", h1_low, d_query_low, preferred_element_type=jnp.float32)
    grad_key = jnp.einsum("td,tq->dq", h1_low, d_key_low, preferred_element_type=jnp.float32)
    grad_value = jnp.einsum("td,tq->dq", h1_low, d_value_low, preferred_element_type=jnp.float32)
    d_normed_one = jnp.einsum("tq,dq->td", d_query_low, w_query, preferred_element_type=jnp.float32)
    d_normed_one = d_normed_one + jnp.einsum(
        "tq,dq->td", d_key_low, key_weight, preferred_element_type=jnp.float32
    )
    d_normed_one = d_normed_one + jnp.einsum(
        "tq,dq->td", d_value_low, value_weight, preferred_element_type=jnp.float32
    )
    d_tokens_norm, grad_norm1 = rms_backward(tokens, scale_one, gain_one, d_normed_one)
    d_tokens = d_resid + d_tokens_norm
    dx_prompt = d_tokens[:prompt_rows][None]
    dx_cont = d_tokens[prompt_rows:].reshape(1, cont_count, cont_len, model_width)
    small = jnp.concatenate([grad_router, grad_norm1[:, None], grad_norm2[:, None]], axis=1)
    small = jnp.pad(small, ((0, 0), (0, -small.shape[1] % 128)))
    dense = jnp.concatenate([grad_query, grad_key, grad_value, small], axis=1).astype(jnp.bfloat16)
    heads_width = QUERY_HEADS * HEAD_SIZE
    edge = heads_width + 2 * key_value_width
    dense = finish_dense(*start_dense(dense, edge // 256 * 128))
    grad_out = finish_dense(*grad_out)
    return (
        y_prompt,
        y_cont,
        dx_prompt,
        dx_cont,
        dense[:, edge + expert_total],
        dense[:, :heads_width],
        dense[:, heads_width : heads_width + key_value_width],
        dense[:, heads_width + key_value_width : edge],
        grad_out,
        dense[:, edge + expert_total + 1],
        dense[:, edge : edge + expert_total],
        grad_gate_up,
        grad_down,
    )


def solution(mesh):
    return jax.shard_map(
        per_device,
        mesh=mesh,
        in_specs=(
            P(("dp", "expert"), "ctx", None),
            P(("dp", "expert"), "ctx", None, None),
            P(),
            P(),
            P(),
            P(),
            P(),
            P(),
            P(),
            P("expert", None, None),
            P("expert", None, None),
            P(("dp", "expert"), "ctx", None),
            P(("dp", "expert"), "ctx", None, None),
            P(("dp", "expert"), "ctx", None),
            P(("dp", "expert"), "ctx", None),
            P(("dp", "expert"), "ctx", None, None),
        ),
        out_specs=(
            P(("dp", "expert"), "ctx", None),
            P(("dp", "expert"), "ctx", None, None),
            P(("dp", "expert"), "ctx", None),
            P(("dp", "expert"), "ctx", None, None),
            P(("dp", "ctx")),
            P(("dp", "ctx"), None),
            P(("dp", "ctx"), None),
            P(("dp", "ctx"), None),
            P(("dp", "ctx"), None),
            P(("dp", "ctx")),
            P(("dp", "ctx"), None),
            P("expert", ("dp", "ctx"), None),
            P("expert", ("dp", "ctx"), None),
        ),
        check_vma=False,
    )
```

```python
from functools import partial

import jax
import jax.numpy as jnp
from jax import lax
from jax.experimental import pallas as pl
from jax.experimental.pallas import tpu as pltpu
from jax.sharding import PartitionSpec as P

QUERY_HEADS = 24
KEY_VALUE_HEADS = 8
HEAD_SIZE = 64


EPS = 1e-06
RESID = 0.22
ATT_SCALE = 0.015625
THETA = 10000.0
NEG = -1e30
LOG2E = 1.4426950408889634


def signed_tables(positions):
    lane = jnp.arange(2 * HEAD_SIZE, dtype=jnp.int32) % HEAD_SIZE
    half_dim = HEAD_SIZE // 2
    frequency = THETA ** (-((lane % half_dim).astype(jnp.float32) * 2.0 / HEAD_SIZE))
    angles = positions[:, None] * frequency[None, :]
    return (jnp.cos(angles), jnp.where(lane < half_dim, -1.0, 1.0) * jnp.sin(angles))


def rms_forward(values, norm_gain):
    inverse = lax.rsqrt(jnp.mean(values * values, axis=-1, keepdims=True) + EPS)
    return (values * inverse * norm_gain, inverse)


def rms_backward(values, inverse, norm_gain, upstream):
    normed = values * inverse
    weighted = upstream * norm_gain
    projected = jnp.mean(weighted * normed, axis=-1, keepdims=True)
    return (inverse * (weighted - normed * projected), jnp.sum(upstream * normed, axis=0))


def slot_codes(routes, visit_order, experts, capacity):
    count = routes.shape[0]
    ids = jnp.arange(count, dtype=jnp.int32)
    visit = jnp.arange(count, dtype=jnp.float32)
    place = (visit_order[:, None] == ids[None, :]).astype(jnp.float32)
    place_row = jnp.sum(place * visit[:, None], axis=0)
    place_col = jnp.sum((visit_order[None, :] == ids[:, None]).astype(jnp.float32) * visit[None, :], axis=1)
    earlier = (place_col[:, None] < place_row[None, :]).astype(jnp.bfloat16)
    named = jnp.any(
        routes.T[None, :, :] == jnp.arange(experts, dtype=jnp.int32)[:, None, None], axis=1
    )
    rank = jnp.dot(named.astype(jnp.bfloat16), earlier, preferred_element_type=jnp.float32)
    return jnp.where(named, jnp.where(rank < capacity, rank, -1.0), -2.0)


def selection(codes, own, slots):
    tokens = codes.shape[-1]
    slot_index = lax.broadcasted_iota(jnp.int32, (slots, tokens), 0).astype(jnp.float32)
    picks = [
        jnp.where(codes[e : e + 1, :] == slot_index, 1.0, 0.0).astype(jnp.bfloat16)
        for e in range(own)
    ]
    return jnp.concatenate(picks, axis=0)


def dispatch_body(own, slots, codes_ref, rows_ref, out_ref):
    pick = selection(codes_ref[0], own, slots)
    moved = jnp.dot(pick, rows_ref[0], preferred_element_type=jnp.float32).astype(jnp.bfloat16)
    for e in range(own):
        out_ref[e] = moved[e * slots : (e + 1) * slots]


def dispatch(codes, rows, own, slots):
    blocks, _, width = rows.shape
    tokens = codes.shape[2]
    return pl.pallas_call(
        partial(dispatch_body, own, slots),
        grid=(blocks,),
        in_specs=[
            pl.BlockSpec((1, codes.shape[1], tokens), lambda b: (b, 0, 0)),
            pl.BlockSpec((1, tokens, width), lambda b: (b, 0, 0)),
        ],
        out_specs=pl.BlockSpec((own, slots, width), lambda b: (0, b, 0)),
        out_shape=jax.ShapeDtypeStruct((own, blocks * slots, width), jnp.bfloat16),
        cost_estimate=pl.CostEstimate(
            flops=2 * blocks * own * slots * tokens * width,
            transcendentals=0,
            bytes_accessed=2 * blocks * (tokens + own * slots) * width,
        ),
        name="dispatch",
    )(codes, rows)


def experts_body(at_ref, rows_ref, gate_up_ref, plain_ref, weight_ref, out_ref, both_ref, d_weight_ref):
    total = rows_ref.shape[1]
    hidden_units = plain_ref.shape[2]
    chunk = total // 2 if total % 16 == 0 else total
    for at in range(0, total, chunk):
        rows = pl.ds(at, chunk)
        both = jnp.dot(rows_ref[0, rows], gate_up_ref[0], preferred_element_type=jnp.float32)
        gate, up = both[:, :hidden_units], both[:, hidden_units:]
        plain, weight = plain_ref[0, rows], weight_ref[0, rows]
        logistic = jax.nn.sigmoid(gate)
        silu = gate * logistic
        hidden = silu * up
        d_weight_ref[0, rows] = jnp.sum(hidden * plain, axis=1, keepdims=True)
        out_ref[0, rows] = (weight * hidden).astype(jnp.bfloat16)
        d_hidden = weight * plain
        d_gate = d_hidden * up * (logistic + silu * (1.0 - logistic))
        both_ref[0, rows, :hidden_units] = d_gate.astype(jnp.bfloat16)
        both_ref[0, rows, hidden_units:] = (d_hidden * silu).astype(jnp.bfloat16)


def experts(offset, rows, gate_up, plain, weight):
    own, total, width = rows.shape
    hidden_units = plain.shape[2]
    part = total // 2 if total % 32 == 0 else total
    tile = lambda e, r, at: (e, r, 0)
    return pl.pallas_call(
        experts_body,
        grid_spec=pltpu.PrefetchScalarGridSpec(
            num_scalar_prefetch=1,
            grid=(own, total // part),
            in_specs=[
                pl.BlockSpec((1, part, width), tile),
                pl.BlockSpec((1, width, 2 * hidden_units), lambda e, r, at: (at[0] + e, 0, 0)),
                pl.BlockSpec((1, part, hidden_units), tile),
                pl.BlockSpec((1, part, 1), tile),
            ],
            out_specs=[
                pl.BlockSpec((1, part, hidden_units), tile),
                pl.BlockSpec((1, part, 2 * hidden_units), tile),
                pl.BlockSpec((1, part, 1), tile),
            ],
        ),
        out_shape=[
            jax.ShapeDtypeStruct((own, total, hidden_units), jnp.bfloat16),
            jax.ShapeDtypeStruct((own, total, 2 * hidden_units), jnp.bfloat16),
            jax.ShapeDtypeStruct((own, total, 1), jnp.float32),
        ],
        cost_estimate=pl.CostEstimate(
            flops=4 * own * total * width * hidden_units,
            transcendentals=own * total * hidden_units,
            bytes_accessed=2 * own * (total * (width + 4 * hidden_units) + 2 * width * hidden_units),
        ),
        name="experts",
    )(jnp.asarray(offset, jnp.int32).reshape(1), rows, gate_up, plain, weight)


def combine_body(own, slots, at_ref, codes_ref, rows_ref, out_ref):
    pick = selection(codes_ref[0], own, slots)
    rows = rows_ref[...].reshape(own * slots, rows_ref.shape[-1])
    out_ref[0] = lax.dot_general(
        pick, rows, (((0,), (0,)), ((), ())), preferred_element_type=jnp.float32
    ).astype(out_ref.dtype)


def combine(at, codes, rows, own, slots):
    count, tokens = at.shape[0], codes.shape[2]
    width = rows.shape[-1]
    return pl.pallas_call(
        partial(combine_body, own, slots),
        grid_spec=pltpu.PrefetchScalarGridSpec(
            num_scalar_prefetch=1,
            grid=(count,),
            in_specs=[
                pl.BlockSpec((1, codes.shape[1], tokens), lambda b, at: (at[b], 0, 0)),
                pl.BlockSpec((own, slots, width), lambda b, at: (0, at[b], 0)),
            ],
            out_specs=pl.BlockSpec((1, tokens, width), lambda b, at: (b, 0, 0)),
        ),
        out_shape=jax.ShapeDtypeStruct((count, tokens, width), jnp.bfloat16),
        cost_estimate=pl.CostEstimate(
            flops=2 * count * own * slots * tokens * width,
            transcendentals=0,
            bytes_accessed=2 * count * (tokens + own * slots) * width,
        ),
        name="combine",
    )(at, codes, rows)


def swap(values, axis, bit):
    size = lax.axis_size(axis)
    return lax.ppermute(values, axis, [(i, i ^ bit) for i in range(size)])


def exchange(values, bit, axis, stride, dim):
    take = partial(lax.dynamic_index_in_dim, axis=dim, keepdims=False)
    away = swap(take(values, 1 - bit), axis, stride)
    stay = take(values, bit)
    first = bit == 0
    return jnp.stack([jnp.where(first, stay, away), jnp.where(first, away, stay)])


def paired(group):
    return group == ("ctx", "expert") and lax.axis_size("ctx") == 4 and lax.axis_size("expert") == 2


def gather_gates(gates, group, first_expert, own):
    if not paired(group):
        whole = lax.all_gather(gates, group, axis=0, tiled=False)
        return lax.dynamic_slice_in_dim(whole, first_expert, own, axis=1)
    ctx, side = lax.axis_index("ctx"), lax.axis_index("expert")
    parts = gates.reshape(2, 2, 2, own, gates.shape[1])
    parts = exchange(parts, side, "expert", 1, 0)
    parts = exchange(parts, ctx % 2, "ctx", 1, 2)
    parts = exchange(parts, ctx // 2, "ctx", 2, 2)
    return parts.reshape(8, own, gates.shape[1])


def return_gates(values, group, first_expert, experts):
    blocks, own, tokens = values.shape
    if not paired(group):
        whole = jnp.zeros((blocks, experts, tokens), values.dtype)
        whole = lax.dynamic_update_slice_in_dim(whole, values, first_expert, axis=1)
        return lax.psum_scatter(whole, group, scatter_dimension=0)
    ctx, side = lax.axis_index("ctx"), lax.axis_index("expert")
    parts = values.reshape(2, 2, 2, own, tokens)
    parts = exchange(parts, ctx // 2, "ctx", 2, 0)
    parts = exchange(parts, ctx % 2, "ctx", 1, 1)
    parts = exchange(parts, side, "expert", 1, 2)
    return parts.transpose(0, 2, 1, 3, 4).reshape(experts, tokens)


def added(left, right):
    return (left.astype(jnp.float32) + right.astype(jnp.float32)).astype(jnp.bfloat16)


def start_scatter(codes, rows, own, slots, group):
    blocks = codes.shape[0]
    if group != ("ctx", "expert") or lax.axis_size("ctx") != 4 or lax.axis_size("expert") != 2:
        every = jnp.arange(blocks, dtype=jnp.int32)
        return lax.psum_scatter(
            combine(every, codes, rows, own, slots), group, scatter_dimension=0
        )
    here = lax.axis_index(group).astype(jnp.int32)
    far = here ^ jnp.array([2, 3, 6, 7], jnp.int32)
    near = here ^ jnp.array([0, 1, 4, 5], jnp.int32)
    sent = swap(combine(far, codes, rows, own, slots), "ctx", 1)
    return added(combine(near, codes, rows, own, slots), sent)


def finish_scatter(part, middle=None, later=None, work=None):
    if part.ndim == 2:
        return part.astype(jnp.float32), None if work is None else work(later)
    half = part.shape[-1] // 2
    left, right = part[:, :, :half], part[:, :, half:]
    left_sent = swap(left[2:], "ctx", 2)
    right_sent = swap(jnp.stack([right[1], right[3]]), "expert", 1)
    if work is not None:
        left_sent, right_sent, _, later = lax.optimization_barrier(
            (left_sent, right_sent, middle, later)
        )
    left_on = swap(added(left[1], left_sent[1]), "expert", 1)
    right_on = swap(added(right[2], right_sent[1]), "ctx", 2)
    made = None
    if work is not None:
        left_on, right_on, made = lax.optimization_barrier((left_on, right_on, work(later)))
    wide = lambda *pieces: sum(piece.astype(jnp.float32) for piece in pieces)
    whole = jnp.concatenate(
        [wide(left[0], left_sent[0], left_on), wide(right[0], right_sent[0], right_on)], axis=1
    )
    return whole, made


def lane_half(shape):
    return lax.broadcasted_iota(jnp.int32, shape, 1) // HEAD_SIZE


def turn(values, cosine, sine):
    half_dim = HEAD_SIZE // 2
    width = values.shape[1]
    lane = lax.broadcasted_iota(jnp.int32, values.shape, 1) % HEAD_SIZE
    partner = jnp.where(
        lane < half_dim,
        pltpu.roll(values, width - half_dim, 1),
        pltpu.roll(values, half_dim, 1),
    )
    return values * cosine + partner * sine


def to_key_half(values, swap, key_half):
    moved = jnp.where(swap, pltpu.roll(values, HEAD_SIZE, 1), values)
    return jnp.where(lane_half(values.shape) == key_half, moved, 0.0)


def project_keys_body(rows, h_ref, kw_ref, vw_ref, cos_ref, sin_ref, prompt_ref, cont_ref):
    key = jnp.dot(h_ref[...], kw_ref[...], preferred_element_type=jnp.float32)
    key = turn(key, cos_ref[...], sin_ref[...]).astype(jnp.bfloat16)
    value = jnp.dot(h_ref[...], vw_ref[...], preferred_element_type=jnp.float32)
    value = value.astype(jnp.bfloat16)
    prompt_ref[0] = key[:rows]
    prompt_ref[1] = value[:rows]
    cont_ref[0] = key[rows:]
    cont_ref[1] = value[rows:]


def project_keys(hidden, key_weight, value_weight, cosine, sine, rows):
    tokens, depth = hidden.shape
    width = key_weight.shape[1]
    whole = lambda j: (0, 0)
    column = lambda j: (0, j)
    return pl.pallas_call(
        partial(project_keys_body, rows),
        grid=(width // 128,),
        in_specs=[
            pl.BlockSpec((tokens, depth), whole),
            pl.BlockSpec((depth, 128), column),
            pl.BlockSpec((depth, 128), column),
            pl.BlockSpec((tokens, 128), whole),
            pl.BlockSpec((tokens, 128), whole),
        ],
        out_specs=[
            pl.BlockSpec((2, rows, 128), lambda j: (0, 0, j)),
            pl.BlockSpec((2, tokens - rows, 128), lambda j: (0, 0, j)),
        ],
        out_shape=[
            jax.ShapeDtypeStruct((2, rows, width), jnp.bfloat16),
            jax.ShapeDtypeStruct((2, tokens - rows, width), jnp.bfloat16),
        ],
        cost_estimate=pl.CostEstimate(
            flops=4 * tokens * depth * width,
            transcendentals=0,
            bytes_accessed=2 * (tokens * depth + 2 * depth * width + 2 * tokens * width),
        ),
        name="project_keys",
    )(hidden, key_weight, value_weight, cosine, sine)


def gather_keys(near_kv):
    if lax.axis_size("ctx") != 4:
        return lax.all_gather(near_kv, "ctx", axis=1, tiled=True)
    rows = near_kv.shape[1]
    here = lax.axis_index("ctx")
    pair = swap(near_kv, "ctx", 2)
    whole = jnp.zeros((2, 4 * rows, near_kv.shape[2]), near_kv.dtype)
    pieces = ((0, near_kv), (2, pair), (1, swap(near_kv, "ctx", 1)), (3, swap(pair, "ctx", 1)))
    for step, piece in pieces:
        whole = lax.dynamic_update_slice_in_dim(whole, piece, (here ^ step) * rows, axis=1)
    return whole


def head_place(group):
    head = pl.program_id(0)
    key_half = (head // group) % 2
    return head, key_half, (head % 2) != key_half


def attend_forward_body(
    group, prompt_rows, cont_len, pos_ref, q_ref, cos_ref, sin_ref, kp_ref, vp_ref, kc_ref, vc_ref,
    qr_ref, out_ref, log_ref,
):
    head, key_half, swap = head_place(group)
    rotated = turn(q_ref[...], cos_ref[...], sin_ref[...]).astype(jnp.bfloat16)
    qr_ref[...] = rotated
    query = to_key_half(rotated.astype(jnp.float32), swap, key_half) * ATT_SCALE
    query = query.astype(jnp.bfloat16)
    nt = (((1,), (1,)), ((), ()))

    def finish(parts, rows):
        highest = parts[0][0].max(axis=1, keepdims=True)
        for scores, _ in parts[1:]:
            highest = jnp.maximum(highest, scores.max(axis=1, keepdims=True))
        lifted = [jnp.exp2(scores * LOG2E - highest * LOG2E) for scores, _ in parts]
        total = lifted[0].sum(axis=1, keepdims=True)
        for piece in lifted[1:]:
            total = total + piece.sum(axis=1, keepdims=True)
        inverse = 1.0 / total
        result = None
        for piece, (_, value) in zip(lifted, parts):
            term = jnp.dot(
                piece.astype(jnp.bfloat16), value, preferred_element_type=jnp.float32
            )
            result = term if result is None else result + term
        log_total = jnp.broadcast_to(highest + jnp.log(total), (total.shape[0], 128))
        log_ref[0, :, rows] = jnp.transpose(log_total)[:8]
        keep = jnp.where(lane_half(result.shape) == key_half, result * inverse, 0.0)
        keep = jnp.where(swap, pltpu.roll(keep, HEAD_SIZE, 1), keep).astype(jnp.bfloat16)

        @pl.when(head % 2 == 0)
        def _():
            out_ref[rows, :] = keep

        @pl.when(head % 2 == 1)
        def _():
            out_ref[rows, :] = out_ref[rows, :] + keep

    total_rows = q_ref.shape[0]
    first = lax.dot_general(
        query[:prompt_rows], kp_ref[...], nt, preferred_element_type=jnp.float32
    )
    row = lax.broadcasted_iota(jnp.int32, first.shape, 0) + pos_ref[0]
    first = jnp.where(lax.broadcasted_iota(jnp.int32, first.shape, 1) <= row, first, NEG)
    finish([(first, vp_ref[...])], pl.ds(0, prompt_rows))
    lower = query[prompt_rows:]
    wide = lax.dot_general(lower, kp_ref[...], nt, preferred_element_type=jnp.float32)
    near = lax.dot_general(lower, kc_ref[...], nt, preferred_element_type=jnp.float32)
    row = lax.broadcasted_iota(jnp.int32, near.shape, 0)
    col = lax.broadcasted_iota(jnp.int32, near.shape, 1)
    near = jnp.where((col <= row) & (col // cont_len == row // cont_len), near, NEG)
    finish([(wide, vp_ref[...]), (near, vc_ref[...])], pl.ds(prompt_rows, total_rows - prompt_rows))


def attend_forward(q_lin, key_prompt, value_prompt, key_cont, value_cont, cosine, sine, start, rows, cont_len):
    tokens, width = q_lin.shape
    heads = width // HEAD_SIZE
    group = heads // (key_prompt.shape[1] // HEAD_SIZE)
    keys, near = key_prompt.shape[0], key_cont.shape[0]
    tile = lambda h, *_: (0, h // 2)
    key_tile = lambda h, *_: (0, h // (2 * group))
    same = lambda h, *_: (0, 0)
    return pl.pallas_call(
        partial(attend_forward_body, group, rows, cont_len),
        grid_spec=pltpu.PrefetchScalarGridSpec(
            num_scalar_prefetch=1,
            grid=(heads,),
            in_specs=[
                pl.BlockSpec((tokens, 128), tile),
                pl.BlockSpec((tokens, 128), same),
                pl.BlockSpec((tokens, 128), same),
                pl.BlockSpec((keys, 128), key_tile),
                pl.BlockSpec((keys, 128), key_tile),
                pl.BlockSpec((near, 128), key_tile),
                pl.BlockSpec((near, 128), key_tile),
            ],
            out_specs=[
                pl.BlockSpec((tokens, 128), tile),
                pl.BlockSpec((tokens, 128), tile),
                pl.BlockSpec((1, 8, tokens), lambda h, *_: (h, 0, 0)),
            ],
        ),
        out_shape=[
            jax.ShapeDtypeStruct((tokens, width), jnp.bfloat16),
            jax.ShapeDtypeStruct((tokens, width), jnp.bfloat16),
            jax.ShapeDtypeStruct((heads, 8, tokens), jnp.float32),
        ],
        cost_estimate=pl.CostEstimate(
            flops=4 * heads * tokens * (keys + near) * 128,
            transcendentals=heads * tokens * (keys + near),
            bytes_accessed=8 * tokens * width,
        ),
        name="attend_forward",
    )(start, q_lin, cosine, sine, key_prompt, value_prompt, key_cont, value_cont)


def attend_backward_body(
    group, prompt_rows, cont_len, chunk, pos_ref, q_ref, do_ref, out_ref, log_ref, cos_ref, sin_ref,
    kcos_ref, ksin_ref, kp_ref, vp_ref, kc_ref, vc_ref,
    dq_ref, dkp_ref, dvp_ref, dkc_ref, dvc_ref, dk_acc, dv_acc,
):
    head, key_half, swap = head_place(group)
    tokens = q_ref.shape[0]
    keys = kp_ref.shape[0]
    near = kc_ref.shape[0]
    nt = (((1,), (1,)), ((), ()))
    tn = (((0,), (0,)), ((), ()))

    @pl.when(head % (2 * group) == 0)
    def _():
        dk_acc[...] = jnp.zeros_like(dk_acc)
        dv_acc[...] = jnp.zeros_like(dv_acc)

    query = to_key_half(q_ref[...].astype(jnp.float32), swap, key_half) * ATT_SCALE
    query = query.astype(jnp.bfloat16)
    d_out = to_key_half(do_ref[...].astype(jnp.float32), swap, key_half)
    result = to_key_half(out_ref[...].astype(jnp.float32), swap, key_half)
    centre = jnp.transpose(
        jnp.broadcast_to(jnp.sum(d_out * result, axis=1, keepdims=True), (tokens, 128))
    )[:1]
    d_out = d_out.astype(jnp.bfloat16)
    log_total = log_ref[0][:1]
    row = lax.broadcasted_iota(jnp.int32, (1, tokens), 1)
    limit = jnp.where(row < prompt_rows, row + pos_ref[0], keys)

    def step(key, value, query, d_out, log_total, centre, allowed, at, count):
        scores = lax.dot_general(key, query, nt, preferred_element_type=jnp.float32)
        scores = jnp.where(allowed(scores.shape), scores, NEG)
        weights = jnp.exp2(scores * LOG2E - log_total * LOG2E)
        d_weights = lax.dot_general(value, d_out, nt, preferred_element_type=jnp.float32)
        d_scores = (weights * (d_weights - centre)).astype(jnp.bfloat16)
        dv_acc[at : at + count] += jnp.dot(
            weights.astype(jnp.bfloat16), d_out, preferred_element_type=jnp.float32
        )
        dk_acc[at : at + count] += jnp.dot(d_scores, query, preferred_element_type=jnp.float32)
        return lax.dot_general(d_scores, key, tn, preferred_element_type=jnp.float32)

    d_query = jnp.zeros((tokens, 128), jnp.float32)
    for at in range(0, keys, chunk):

        def seen(shape, at=at):
            return lax.broadcasted_iota(jnp.int32, shape, 0) + at <= limit

        d_query = d_query + step(
            kp_ref[at : at + chunk], vp_ref[at : at + chunk], query, d_out, log_total, centre, seen,
            at, chunk,
        )

    def nearby(shape):
        key_at = lax.broadcasted_iota(jnp.int32, shape, 0)
        query_at = lax.broadcasted_iota(jnp.int32, shape, 1)
        return (key_at <= query_at) & (key_at // cont_len == query_at // cont_len)

    tail = step(
        kc_ref[...], vc_ref[...], query[prompt_rows:], d_out[prompt_rows:],
        log_total[:, prompt_rows:], centre[:, prompt_rows:], nearby, keys, near,
    )
    d_query = jnp.concatenate([d_query[:prompt_rows], d_query[prompt_rows:] + tail], axis=0)
    d_query = jnp.where(lane_half(d_query.shape) == key_half, d_query * ATT_SCALE, 0.0)
    d_query = jnp.where(swap, pltpu.roll(d_query, HEAD_SIZE, 1), d_query)
    d_query = turn(d_query, cos_ref[...], -sin_ref[...]).astype(jnp.bfloat16)

    @pl.when(head % 2 == 0)
    def _():
        dq_ref[...] = d_query

    @pl.when(head % 2 == 1)
    def _():
        dq_ref[...] = dq_ref[...] + d_query

    @pl.when(head % (2 * group) == 2 * group - 1)
    def _():
        dk = turn(dk_acc[...], kcos_ref[...], -ksin_ref[...]).astype(jnp.bfloat16)
        dv = dv_acc[...].astype(jnp.bfloat16)
        dkp_ref[...] = dk[:keys]
        dkc_ref[...] = dk[keys:]
        dvp_ref[...] = dv[:keys]
        dvc_ref[...] = dv[keys:]


def attend_backward(
    query, d_out, result, log_total, key_prompt, value_prompt, key_cont, value_cont, cosine, sine,
    key_cosine, key_sine, start, rows, cont_len,
):
    tokens, width = query.shape
    heads = width // HEAD_SIZE
    key_width = key_prompt.shape[1]
    group = heads // (key_width // HEAD_SIZE)
    keys, near = key_prompt.shape[0], key_cont.shape[0]
    chunk = min(256, keys)
    tile = lambda h, *_: (0, h // 2)
    key_tile = lambda h, *_: (0, h // (2 * group))
    same = lambda h, *_: (0, 0)
    return pl.pallas_call(
        partial(attend_backward_body, group, rows, cont_len, chunk),
        grid_spec=pltpu.PrefetchScalarGridSpec(
            num_scalar_prefetch=1,
            grid=(heads,),
            in_specs=[
                pl.BlockSpec((tokens, 128), tile),
                pl.BlockSpec((tokens, 128), tile),
                pl.BlockSpec((tokens, 128), tile),
                pl.BlockSpec((1, 8, tokens), lambda h, *_: (h, 0, 0)),
                pl.BlockSpec((tokens, 128), same),
                pl.BlockSpec((tokens, 128), same),
                pl.BlockSpec((keys + near, 128), same),
                pl.BlockSpec((keys + near, 128), same),
                pl.BlockSpec((keys, 128), key_tile),
                pl.BlockSpec((keys, 128), key_tile),
                pl.BlockSpec((near, 128), key_tile),
                pl.BlockSpec((near, 128), key_tile),
            ],
            out_specs=[
                pl.BlockSpec((tokens, 128), tile),
                pl.BlockSpec((keys, 128), key_tile),
                pl.BlockSpec((keys, 128), key_tile),
                pl.BlockSpec((near, 128), key_tile),
                pl.BlockSpec((near, 128), key_tile),
            ],
            scratch_shapes=[
                pltpu.VMEM((keys + near, 128), jnp.float32),
                pltpu.VMEM((keys + near, 128), jnp.float32),
            ],
        ),
        out_shape=[
            jax.ShapeDtypeStruct((tokens, width), jnp.bfloat16),
            jax.ShapeDtypeStruct((keys, key_width), jnp.bfloat16),
            jax.ShapeDtypeStruct((keys, key_width), jnp.bfloat16),
            jax.ShapeDtypeStruct((near, key_width), jnp.bfloat16),
            jax.ShapeDtypeStruct((near, key_width), jnp.bfloat16),
        ],
        cost_estimate=pl.CostEstimate(
            flops=10 * heads * tokens * (keys + near) * 128,
            transcendentals=heads * tokens * (keys + near),
            bytes_accessed=8 * tokens * width,
        ),
        name="attend_backward",
    )(
        start, query, d_out, result, log_total, cosine, sine, key_cosine, key_sine, key_prompt,
        value_prompt, key_cont, value_cont,
    )


def reduce_experts(grad, split):
    if split == 1:
        return lax.psum_scatter(
            grad, ("dp", "ctx"), scatter_dimension=1, tiled=True
        ).astype(jnp.float32)
    part = lax.psum_scatter(grad, "dp", scatter_dimension=1, tiled=True)
    size = lax.axis_size("ctx")
    if size & (size - 1):
        return lax.all_to_all(part, "ctx", split_axis=1, concat_axis=0, tiled=True).astype(
            jnp.float32
        )
    own, rows, width = part.shape
    here = lax.axis_index("ctx")
    part = part.reshape(own, size, rows // size, width)
    whole = jnp.zeros((own * size, rows // size, width), jnp.float32)
    for step in range(size):
        piece = lax.dynamic_index_in_dim(part, here ^ step, 1, keepdims=False)
        if step:
            piece = swap(piece, "ctx", step)
        whole = lax.dynamic_update_slice_in_dim(
            whole, piece.astype(jnp.float32), (here ^ step) * own, axis=0
        )
    return whole


def scatter_keys(d_key, d_value, rows):
    size = lax.axis_size("ctx")
    here = lax.axis_index("ctx")

    def share(owner):
        return jnp.concatenate(
            [
                lax.dynamic_slice_in_dim(d_key, owner * rows, rows, axis=0),
                lax.dynamic_slice_in_dim(d_value, owner * rows, rows, axis=0),
            ],
            axis=1,
        )

    total = share(here).astype(jnp.float32)
    for hop in range(1, size):
        moved = lax.ppermute(
            share((here + hop) % size), "ctx", [(i, (i + hop) % size) for i in range(size)]
        )
        total = total + moved.astype(jnp.float32)
    total = total.astype(jnp.bfloat16)
    return (total[:, : d_key.shape[1]], total[:, d_key.shape[1] :])


def fold_dense(grad, cut):
    rows, width = grad.shape
    parts = lax.axis_size("dp")
    core = lax.axis_index("ctx") % 2
    pair = lax.axis_index("ctx") // 2
    side = lax.axis_index("expert")
    take = partial(lax.dynamic_index_in_dim, keepdims=False)
    grad = grad.reshape(parts, 2, 2, 2, rows // (8 * parts), width)
    one = added(take(grad, core, 2), swap(take(grad, 1 - core, 2), "ctx", 1))
    left, right = one[..., :cut], one[..., cut:]
    left_sent = swap(take(left, 1 - pair, 1), "ctx", 2)
    right_sent = swap(take(right, 1 - side, 2), "expert", 1)
    left = added(take(left, pair, 1), left_sent)
    right = added(take(right, side, 2), right_sent)
    left_sent = swap(take(left, 1 - side, 1), "expert", 1)
    right_sent = swap(take(right, 1 - pair, 1), "ctx", 2)
    return jnp.concatenate(
        [added(take(left, side, 1), left_sent), added(take(right, pair, 1), right_sent)], axis=-1
    )


def scatter_parts(parts):
    size = lax.axis_size("dp")
    here = lax.axis_index("dp")
    take = partial(lax.dynamic_index_in_dim, axis=0, keepdims=False)
    total = take(parts, here).astype(jnp.float32)
    for hop in range(1, size):
        moved = lax.ppermute(
            take(parts, (here + hop) % size), "dp", [(i, (i + hop) % size) for i in range(size)]
        )
        total = total + moved.astype(jnp.float32)
    return total.astype(jnp.bfloat16)


def finish_dense(grad, folded):
    if not folded:
        return lax.psum(grad, "expert").astype(jnp.float32)
    other = swap(grad, "expert", 1)
    first = lax.axis_index("expert") == 0
    return jnp.concatenate(
        [jnp.where(first, grad, other), jnp.where(first, other, grad)], axis=0
    ).astype(jnp.float32)


def start_dense(grad, cut):
    parts = lax.axis_size("dp")
    folded = (
        lax.axis_size("ctx") == 4
        and lax.axis_size("expert") == 2
        and grad.shape[0] % (64 * parts) == 0
    )
    if not folded:
        return lax.psum_scatter(grad, ("dp", "ctx"), scatter_dimension=0, tiled=True), False
    return scatter_parts(fold_dense(grad, cut)), True


def per_device(
    x_prompt,
    x_cont,
    norm1_gain,
    w_query,
    key_weight,
    value_weight,
    w_out,
    norm2_gain,
    w_router,
    w_gate_up,
    w_down,
    routes_prompt,
    routes_cont,
    slot_order,
    dy_prompt,
    dy_cont,
):
    model_width = x_prompt.shape[2]
    prompt_rows = x_prompt.shape[1]
    cont_count = x_cont.shape[1]
    cont_len = x_cont.shape[2]
    cont_rows = cont_count * cont_len
    count_of_tokens = prompt_rows + cont_rows
    key_value_width = KEY_VALUE_HEADS * HEAD_SIZE
    local_experts = w_gate_up.shape[0]
    expert_groups = lax.axis_size("expert")
    expert_total = local_experts * expert_groups
    top_count = routes_prompt.shape[2]
    capacity = (count_of_tokens * top_count + expert_total - 1) // expert_total
    hidden_units = w_down.shape[1]
    prompt_total = prompt_rows * lax.axis_size("ctx")
    count_of_keys = prompt_total + cont_rows
    split = lax.axis_size("ctx") if local_experts % lax.axis_size("ctx") == 0 else 1
    own = local_experts // split
    blocks = split * expert_groups
    slots = -(-capacity // 8) * 8
    group = ("ctx", "expert") if split > 1 else ("expert",)
    block_index = lax.axis_index(group)
    own_offset = lax.axis_index("ctx") * own if split > 1 else 0
    first_expert = lax.axis_index("expert") * local_experts + own_offset
    gate_up_own = w_gate_up
    down_own = w_down
    if split > 1:
        gate_up_own = lax.dynamic_slice_in_dim(w_gate_up, own_offset, own, axis=0)
        down_own = lax.dynamic_slice_in_dim(w_down, own_offset, own, axis=0)
    routes = jnp.concatenate(
        [routes_prompt[0], routes_cont[0].reshape(cont_rows, top_count)], axis=0
    )
    codes = slot_codes(routes, slot_order[0, 0], expert_total, capacity)
    upstream_low = jnp.concatenate([dy_prompt[0], dy_cont[0].reshape(cont_rows, model_width)], axis=0)
    upstream = upstream_low.astype(jnp.float32)
    assert capacity <= 256
    fold = model_width // count_of_tokens
    code_rows = -(-expert_total // (8 * fold)) * 8
    code_table = jnp.pad(
        codes.astype(jnp.bfloat16),
        ((0, code_rows * fold - expert_total), (0, 0)),
        constant_values=-2.0,
    )
    code_table = jnp.concatenate(
        [code_table[i * code_rows : (i + 1) * code_rows] for i in range(fold)], axis=1
    )
    upstream_all = lax.all_gather(
        jnp.concatenate([upstream_low, code_table], axis=0), group, axis=0, tiled=False
    )
    codes_all = upstream_all[:, count_of_tokens:]
    codes_all = jnp.concatenate(
        [
            codes_all[:, :, i * count_of_tokens : (i + 1) * count_of_tokens] for i in range(fold)
        ],
        axis=1,
    ).astype(jnp.float32)
    own_codes = lax.dynamic_slice_in_dim(codes_all, first_expert, own, axis=1)
    own_codes = jnp.pad(own_codes, ((0, 0), (0, -own % 8), (0, 0)), constant_values=-2.0)
    d_slot_rows = dispatch(own_codes, upstream_all, own, slots)
    d_plain = jnp.einsum("ecd,efd->ecf", d_slot_rows, down_own, preferred_element_type=jnp.float32)
    gain_one = norm1_gain.astype(jnp.float32)
    gain_two = norm2_gain.astype(jnp.float32)
    tokens = jnp.concatenate(
        [x_prompt[0], x_cont[0].reshape(cont_rows, model_width)], axis=0
    ).astype(jnp.float32)
    normed_one, scale_one = rms_forward(tokens, gain_one)
    h1_low = normed_one.astype(jnp.bfloat16)
    row_index = jnp.arange(count_of_tokens, dtype=jnp.int32)
    cont_offset = row_index - prompt_rows
    start = lax.axis_index("ctx") * prompt_rows
    query_pos = jnp.where(
        cont_offset >= 0, prompt_total + cont_offset % cont_len, start + row_index
    )
    key_index = jnp.arange(count_of_keys, dtype=jnp.int32)
    key_pos = jnp.where(
        key_index >= prompt_total, prompt_total + (key_index - prompt_total) % cont_len, key_index
    )
    start = start.astype(jnp.int32)[None]
    cosine, sine = signed_tables(query_pos.astype(jnp.float32))
    key_cosine, key_sine = signed_tables(key_pos.astype(jnp.float32))
    near_kv, cont_kv = project_keys(
        h1_low, key_weight, value_weight, cosine, sine, prompt_rows
    )
    prompt_kv = gather_keys(near_kv)
    keys_values = (prompt_kv[0], prompt_kv[1], cont_kv[0], cont_kv[1])
    q_lin = jnp.dot(h1_low, w_query, preferred_element_type=jnp.float32)
    query_row_block, merged_low, log_total = attend_forward(
        q_lin, *keys_values, cosine, sine, start, prompt_rows, cont_len
    )
    branch = jnp.dot(merged_low, w_out, preferred_element_type=jnp.float32)
    resid = tokens + RESID * branch
    normed_two, scale_two = rms_forward(resid, gain_two)
    h2_low = normed_two.astype(jnp.bfloat16)
    rows_all = lax.all_gather(h2_low, group, axis=0, tiled=False)
    named = codes > -1.5
    logits = jnp.einsum("td,de->et", h2_low, w_router, preferred_element_type=jnp.float32)
    logits = jnp.where(named, logits, NEG)
    lifted = jnp.where(named, jnp.exp(logits - jnp.max(logits, axis=0, keepdims=True)), 0.0)
    gates = lifted / jnp.sum(lifted, axis=0, keepdims=True)
    own_gates, rows_all, d_plain = lax.optimization_barrier(
        (gather_gates(gates, group, first_expert, own), rows_all, d_plain)
    )
    slot_rows = dispatch(own_codes, rows_all, own, slots)
    slot_index = jnp.arange(slots, dtype=jnp.int32).astype(jnp.float32)
    picked = own_codes[:, :own, None, :] == slot_index[None, None, :, None]
    slot_gate = jnp.sum(jnp.where(picked, own_gates[:, :, None, :], 0.0), axis=-1)
    slot_gate = slot_gate.transpose(1, 0, 2).reshape(own, blocks * slots)
    weighted, d_both, d_slot_gate = experts(
        own_offset, slot_rows, w_gate_up, d_plain, RESID * slot_gate[:, :, None]
    )
    d_slot_gate = RESID * d_slot_gate[:, :, 0]
    grad_down = jnp.einsum(
        "ecf,ecd->efd", weighted, d_slot_rows, preferred_element_type=jnp.float32
    ).astype(jnp.bfloat16)
    d_both, grad_down = lax.optimization_barrier((d_both, grad_down))
    grad_down = reduce_experts(grad_down, split)
    d_slots = jnp.einsum(
        "ecf,edf->ecd", d_both, gate_up_own, preferred_element_type=jnp.float32
    ).astype(jnp.bfloat16)
    d_rows_parts, weighted, slot_rows = lax.optimization_barrier(
        (start_scatter(own_codes, d_slots, own, slots, group), weighted, slot_rows)
    )
    grad_gate_up = jnp.einsum(
        "ecd,ecf->edf", slot_rows, d_both, preferred_element_type=jnp.float32
    ).astype(jnp.bfloat16)

    def forward_rows(weighted):
        return jnp.einsum(
            "ecf,efd->ecd", weighted, down_own, preferred_element_type=jnp.float32
        ).astype(jnp.bfloat16)

    d_rows, expert_out = finish_scatter(d_rows_parts, grad_gate_up, weighted, forward_rows)
    d_gates_own = jnp.sum(
        jnp.where(
            picked,
            d_slot_gate.reshape(own, blocks, slots).transpose(1, 0, 2)[..., None],
            0.0,
        ),
        axis=2,
    )
    d_gates = return_gates(d_gates_own, group, first_expert, expert_total)
    cut = hidden_units
    grad_gate_up = jnp.concatenate(
        [
            reduce_experts(grad_gate_up[..., :cut], split),
            reduce_experts(grad_gate_up[..., cut:], split),
        ],
        axis=-1,
    )
    d_logits = (
        gates * (d_gates - jnp.sum(gates * d_gates, axis=0, keepdims=True))
    ).astype(jnp.bfloat16)
    grad_router = jnp.einsum("td,et->de", h2_low, d_logits, preferred_element_type=jnp.float32)
    d_normed_two = d_rows + jnp.einsum(
        "et,de->td", d_logits, w_router, preferred_element_type=jnp.float32
    )
    d_resid_norm, grad_norm2 = rms_backward(resid, scale_two, gain_two, d_normed_two)
    d_resid = upstream + d_resid_norm
    d_branch = (RESID * d_resid).astype(jnp.bfloat16)
    grad_out = jnp.einsum(
        "tq,td->qd", merged_low, d_branch, preferred_element_type=jnp.float32
    ).astype(jnp.bfloat16)
    grad_out = start_dense(grad_out, grad_out.shape[1] // 256 * 128)
    merged_gradient = jnp.einsum(
        "td,qd->tq", d_branch, w_out, preferred_element_type=jnp.float32
    ).astype(jnp.bfloat16)
    d_query_low, d_key_prompt, d_value_prompt, d_key_cont, d_value_cont = attend_backward(
        query_row_block, merged_gradient, merged_low, log_total, *keys_values, cosine, sine,
        key_cosine, key_sine, start, prompt_rows, cont_len,
    )
    expert_out, d_key_prompt = lax.optimization_barrier((expert_out, d_key_prompt))
    mixed, _ = finish_scatter(start_scatter(own_codes, expert_out, own, slots, group))
    output = resid + mixed
    y_prompt = output[:prompt_rows].astype(jnp.bfloat16)[None]
    y_cont = output[prompt_rows:].reshape(1, cont_count, cont_len, model_width).astype(jnp.bfloat16)
    d_key_prompt, d_value_prompt = scatter_keys(d_key_prompt, d_value_prompt, prompt_rows)
    d_key_low = jnp.concatenate([d_key_prompt, d_key_cont], axis=0)
    d_value_low = jnp.concatenate([d_value_prompt, d_value_cont], axis=0)
    grad_query = jnp.einsum("td,tq->dq", h1_low, d_query_low, preferred_element_type=jnp.float32)
    grad_key = jnp.einsum("td,tq->dq", h1_low, d_key_low, preferred_element_type=jnp.float32)
    grad_value = jnp.einsum("td,tq->dq", h1_low, d_value_low, preferred_element_type=jnp.float32)
    d_normed_one = jnp.einsum("tq,dq->td", d_query_low, w_query, preferred_element_type=jnp.float32)
    d_normed_one = d_normed_one + jnp.einsum(
        "tq,dq->td", d_key_low, key_weight, preferred_element_type=jnp.float32
    )
    d_normed_one = d_normed_one + jnp.einsum(
        "tq,dq->td", d_value_low, value_weight, preferred_element_type=jnp.float32
    )
    d_tokens_norm, grad_norm1 = rms_backward(tokens, scale_one, gain_one, d_normed_one)
    d_tokens = d_resid + d_tokens_norm
    dx_prompt = d_tokens[:prompt_rows][None]
    dx_cont = d_tokens[prompt_rows:].reshape(1, cont_count, cont_len, model_width)
    small = jnp.concatenate([grad_router, grad_norm1[:, None], grad_norm2[:, None]], axis=1)
    small = jnp.pad(small, ((0, 0), (0, -small.shape[1] % 128)))
    dense = jnp.concatenate([grad_query, grad_key, grad_value, small], axis=1).astype(jnp.bfloat16)
    heads_width = QUERY_HEADS * HEAD_SIZE
    edge = heads_width + 2 * key_value_width
    dense = finish_dense(*start_dense(dense, edge // 256 * 128))
    grad_out = finish_dense(*grad_out)
    return (
        y_prompt,
        y_cont,
        dx_prompt,
        dx_cont,
        dense[:, edge + expert_total],
        dense[:, :heads_width],
        dense[:, heads_width : heads_width + key_value_width],
        dense[:, heads_width + key_value_width : edge],
        grad_out,
        dense[:, edge + expert_total + 1],
        dense[:, edge : edge + expert_total],
        grad_gate_up,
        grad_down,
    )


def solution(mesh):
    return jax.shard_map(
        per_device,
        mesh=mesh,
        in_specs=(
            P(("dp", "expert"), "ctx", None),
            P(("dp", "expert"), "ctx", None, None),
            P(),
            P(),
            P(),
            P(),
            P(),
            P(),
            P(),
            P("expert", None, None),
            P("expert", None, None),
            P(("dp", "expert"), "ctx", None),
            P(("dp", "expert"), "ctx", None, None),
            P(("dp", "expert"), "ctx", None),
            P(("dp", "expert"), "ctx", None),
            P(("dp", "expert"), "ctx", None, None),
        ),
        out_specs=(
            P(("dp", "expert"), "ctx", None),
            P(("dp", "expert"), "ctx", None, None),
            P(("dp", "expert"), "ctx", None),
            P(("dp", "expert"), "ctx", None, None),
            P(("dp", "ctx")),
            P(("dp", "ctx"), None),
            P(("dp", "ctx"), None),
            P(("dp", "ctx"), None),
            P(("dp", "ctx"), None),
            P(("dp", "ctx")),
            P(("dp", "ctx"), None),
            P("expert", ("dp", "ctx"), None),
            P("expert", ("dp", "ctx"), None),
        ),
        check_vma=False,
    )
```

```python
from functools import partial

import jax
import jax.numpy as jnp
from jax import lax
from jax.experimental import pallas as pl
from jax.experimental.pallas import tpu as pltpu
from jax.sharding import PartitionSpec as P

QUERY_HEADS = 24
KEY_VALUE_HEADS = 8
HEAD_SIZE = 64


EPS = 1e-06
RESID = 0.22
ATT_SCALE = 0.015625
THETA = 10000.0
NEG = -1e30
LOG2E = 1.4426950408889634


def signed_tables(positions):
    lane = jnp.arange(2 * HEAD_SIZE, dtype=jnp.int32) % HEAD_SIZE
    half_dim = HEAD_SIZE // 2
    frequency = THETA ** (-((lane % half_dim).astype(jnp.float32) * 2.0 / HEAD_SIZE))
    angles = positions[:, None] * frequency[None, :]
    return (jnp.cos(angles), jnp.where(lane < half_dim, -1.0, 1.0) * jnp.sin(angles))


def rms_forward(values, norm_gain):
    inverse = lax.rsqrt(jnp.mean(values * values, axis=-1, keepdims=True) + EPS)
    return (values * inverse * norm_gain, inverse)


def rms_backward(values, inverse, norm_gain, upstream):
    normed = values * inverse
    weighted = upstream * norm_gain
    projected = jnp.mean(weighted * normed, axis=-1, keepdims=True)
    return (inverse * (weighted - normed * projected), jnp.sum(upstream * normed, axis=0))


def slot_codes(routes, visit_order, experts, capacity):
    count = routes.shape[0]
    ids = jnp.arange(count, dtype=jnp.int32)
    visit = jnp.arange(count, dtype=jnp.float32)
    place = (visit_order[:, None] == ids[None, :]).astype(jnp.float32)
    place_row = jnp.sum(place * visit[:, None], axis=0)
    place_col = jnp.sum((visit_order[None, :] == ids[:, None]).astype(jnp.float32) * visit[None, :], axis=1)
    earlier = (place_col[:, None] < place_row[None, :]).astype(jnp.bfloat16)
    named = jnp.any(
        routes.T[None, :, :] == jnp.arange(experts, dtype=jnp.int32)[:, None, None], axis=1
    )
    rank = jnp.dot(named.astype(jnp.bfloat16), earlier, preferred_element_type=jnp.float32)
    return jnp.where(named, jnp.where(rank < capacity, rank, -1.0), -2.0)


def selection(codes, own, slots):
    tokens = codes.shape[-1]
    slot_index = lax.broadcasted_iota(jnp.int32, (slots, tokens), 0).astype(jnp.float32)
    picks = [
        jnp.where(codes[e : e + 1, :] == slot_index, 1.0, 0.0).astype(jnp.bfloat16)
        for e in range(own)
    ]
    return jnp.concatenate(picks, axis=0)


def dispatch_body(own, slots, codes_ref, rows_ref, out_ref):
    pick = selection(codes_ref[0], own, slots)
    moved = jnp.dot(pick, rows_ref[0], preferred_element_type=jnp.float32).astype(jnp.bfloat16)
    for e in range(own):
        out_ref[e] = moved[e * slots : (e + 1) * slots]


def dispatch(codes, rows, own, slots):
    blocks, _, width = rows.shape
    tokens = codes.shape[2]
    return pl.pallas_call(
        partial(dispatch_body, own, slots),
        grid=(blocks,),
        in_specs=[
            pl.BlockSpec((1, codes.shape[1], tokens), lambda b: (b, 0, 0)),
            pl.BlockSpec((1, tokens, width), lambda b: (b, 0, 0)),
        ],
        out_specs=pl.BlockSpec((own, slots, width), lambda b: (0, b, 0)),
        out_shape=jax.ShapeDtypeStruct((own, blocks * slots, width), jnp.bfloat16),
        cost_estimate=pl.CostEstimate(
            flops=2 * blocks * own * slots * tokens * width,
            transcendentals=0,
            bytes_accessed=2 * blocks * (tokens + own * slots) * width,
        ),
        name="dispatch",
    )(codes, rows)


def experts_body(at_ref, rows_ref, gate_up_ref, plain_ref, weight_ref, out_ref, both_ref, d_weight_ref):
    total = rows_ref.shape[1]
    hidden_units = plain_ref.shape[2]
    chunk = total // 2 if total % 16 == 0 else total
    for at in range(0, total, chunk):
        rows = pl.ds(at, chunk)
        both = jnp.dot(rows_ref[0, rows], gate_up_ref[0], preferred_element_type=jnp.float32)
        gate, up = both[:, :hidden_units], both[:, hidden_units:]
        plain, weight = plain_ref[0, rows], weight_ref[0, rows]
        logistic = jax.nn.sigmoid(gate)
        silu = gate * logistic
        hidden = silu * up
        d_weight_ref[0, rows] = jnp.sum(hidden * plain, axis=1, keepdims=True)
        out_ref[0, rows] = (weight * hidden).astype(jnp.bfloat16)
        d_hidden = weight * plain
        d_gate = d_hidden * up * (logistic + silu * (1.0 - logistic))
        both_ref[0, rows, :hidden_units] = d_gate.astype(jnp.bfloat16)
        both_ref[0, rows, hidden_units:] = (d_hidden * silu).astype(jnp.bfloat16)


def experts(offset, rows, gate_up, plain, weight):
    own, total, width = rows.shape
    hidden_units = plain.shape[2]
    part = total // 2 if total % 32 == 0 else total
    tile = lambda e, r, at: (e, r, 0)
    return pl.pallas_call(
        experts_body,
        grid_spec=pltpu.PrefetchScalarGridSpec(
            num_scalar_prefetch=1,
            grid=(own, total // part),
            in_specs=[
                pl.BlockSpec((1, part, width), tile),
                pl.BlockSpec((1, width, 2 * hidden_units), lambda e, r, at: (at[0] + e, 0, 0)),
                pl.BlockSpec((1, part, hidden_units), tile),
                pl.BlockSpec((1, part, 1), tile),
            ],
            out_specs=[
                pl.BlockSpec((1, part, hidden_units), tile),
                pl.BlockSpec((1, part, 2 * hidden_units), tile),
                pl.BlockSpec((1, part, 1), tile),
            ],
        ),
        out_shape=[
            jax.ShapeDtypeStruct((own, total, hidden_units), jnp.bfloat16),
            jax.ShapeDtypeStruct((own, total, 2 * hidden_units), jnp.bfloat16),
            jax.ShapeDtypeStruct((own, total, 1), jnp.float32),
        ],
        cost_estimate=pl.CostEstimate(
            flops=4 * own * total * width * hidden_units,
            transcendentals=own * total * hidden_units,
            bytes_accessed=2 * own * (total * (width + 4 * hidden_units) + 2 * width * hidden_units),
        ),
        name="experts",
    )(jnp.asarray(offset, jnp.int32).reshape(1), rows, gate_up, plain, weight)


def combine_body(own, slots, at_ref, codes_ref, rows_ref, out_ref):
    pick = selection(codes_ref[0], own, slots)
    rows = rows_ref[...].reshape(own * slots, rows_ref.shape[-1])
    out_ref[0] = lax.dot_general(
        pick, rows, (((0,), (0,)), ((), ())), preferred_element_type=jnp.float32
    ).astype(out_ref.dtype)


def combine(at, codes, rows, own, slots):
    count, tokens = at.shape[0], codes.shape[2]
    width = rows.shape[-1]
    return pl.pallas_call(
        partial(combine_body, own, slots),
        grid_spec=pltpu.PrefetchScalarGridSpec(
            num_scalar_prefetch=1,
            grid=(count,),
            in_specs=[
                pl.BlockSpec((1, codes.shape[1], tokens), lambda b, at: (at[b], 0, 0)),
                pl.BlockSpec((own, slots, width), lambda b, at: (0, at[b], 0)),
            ],
            out_specs=pl.BlockSpec((1, tokens, width), lambda b, at: (b, 0, 0)),
        ),
        out_shape=jax.ShapeDtypeStruct((count, tokens, width), jnp.bfloat16),
        cost_estimate=pl.CostEstimate(flops=1, transcendentals=0, bytes_accessed=1),
        name="combine",
    )(at, codes, rows)


def swap(values, axis, bit):
    size = lax.axis_size(axis)
    return lax.ppermute(values, axis, [(i, i ^ bit) for i in range(size)])


def exchange(values, bit, axis, stride, dim):
    take = partial(lax.dynamic_index_in_dim, axis=dim, keepdims=False)
    away = swap(take(values, 1 - bit), axis, stride)
    stay = take(values, bit)
    first = bit == 0
    return jnp.stack([jnp.where(first, stay, away), jnp.where(first, away, stay)])


def paired(group):
    return group == ("ctx", "expert") and lax.axis_size("ctx") == 4 and lax.axis_size("expert") == 2


def gather_gates(gates, group, first_expert, own):
    if not paired(group):
        whole = lax.all_gather(gates, group, axis=0, tiled=False)
        return lax.dynamic_slice_in_dim(whole, first_expert, own, axis=1)
    ctx, side = lax.axis_index("ctx"), lax.axis_index("expert")
    parts = gates.reshape(2, 2, 2, own, gates.shape[1])
    parts = exchange(parts, side, "expert", 1, 0)
    parts = exchange(parts, ctx % 2, "ctx", 1, 2)
    parts = exchange(parts, ctx // 2, "ctx", 2, 2)
    return parts.reshape(8, own, gates.shape[1])


def return_gates(values, group, first_expert, experts):
    blocks, own, tokens = values.shape
    if not paired(group):
        whole = jnp.zeros((blocks, experts, tokens), values.dtype)
        whole = lax.dynamic_update_slice_in_dim(whole, values, first_expert, axis=1)
        return lax.psum_scatter(whole, group, scatter_dimension=0)
    ctx, side = lax.axis_index("ctx"), lax.axis_index("expert")
    parts = values.reshape(2, 2, 2, own, tokens)
    parts = exchange(parts, ctx // 2, "ctx", 2, 0)
    parts = exchange(parts, ctx % 2, "ctx", 1, 1)
    parts = exchange(parts, side, "expert", 1, 2)
    return parts.transpose(0, 2, 1, 3, 4).reshape(experts, tokens)


def added(left, right):
    return (left.astype(jnp.float32) + right.astype(jnp.float32)).astype(jnp.bfloat16)


def pair_sums(codes, rows, own, slots, group):
    if not paired(group):
        every = jnp.arange(codes.shape[0], dtype=jnp.int32)
        return lax.psum_scatter(
            combine(every, codes, rows, own, slots), group, scatter_dimension=0
        ), None
    here = lax.axis_index(group).astype(jnp.int32)
    far = here ^ jnp.array([2, 3, 6, 7], jnp.int32)
    near = here ^ jnp.array([0, 1, 4, 5], jnp.int32)
    return combine(far, codes, rows, own, slots), combine(near, codes, rows, own, slots)


def scatter_one(far, near):
    return far if near is None else added(near, swap(far, "ctx", 1))


def scatter_two(part):
    if part.ndim == 2:
        return part, ()
    half = part.shape[-1] // 2
    left, right = part[:, :, :half], part[:, :, half:]
    moved = swap(left[2:], "ctx", 2), swap(jnp.stack([right[1], right[3]]), "expert", 1)
    return (left[0], left[1], right[0], right[2]), moved


def scatter_three(kept, moved):
    if not moved:
        return kept, ()
    left, left_other, right, right_other = kept
    left_sent, right_sent = moved
    onward = (
        swap(added(left_other, left_sent[1]), "expert", 1),
        swap(added(right_other, right_sent[1]), "ctx", 2),
    )
    return (left, left_sent[0], right, right_sent[0]), onward


def scatter_end(kept, moved):
    if not moved:
        return kept.astype(jnp.float32)
    wide = lambda *pieces: sum(piece.astype(jnp.float32) for piece in pieces)
    return jnp.concatenate(
        [wide(kept[0], kept[1], moved[0]), wide(kept[2], kept[3], moved[1])], axis=1
    )


def lane_half(shape):
    return lax.broadcasted_iota(jnp.int32, shape, 1) // HEAD_SIZE


def turn(values, cosine, sine):
    half_dim = HEAD_SIZE // 2
    width = values.shape[1]
    lane = lax.broadcasted_iota(jnp.int32, values.shape, 1) % HEAD_SIZE
    partner = jnp.where(
        lane < half_dim,
        pltpu.roll(values, width - half_dim, 1),
        pltpu.roll(values, half_dim, 1),
    )
    return values * cosine + partner * sine


def to_key_half(values, swap, key_half):
    moved = jnp.where(swap, pltpu.roll(values, HEAD_SIZE, 1), values)
    return jnp.where(lane_half(values.shape) == key_half, moved, 0.0)


def project_keys_body(rows, h_ref, kw_ref, vw_ref, cos_ref, sin_ref, prompt_ref, cont_ref):
    key = jnp.dot(h_ref[...], kw_ref[...], preferred_element_type=jnp.float32)
    key = turn(key, cos_ref[...], sin_ref[...]).astype(jnp.bfloat16)
    value = jnp.dot(h_ref[...], vw_ref[...], preferred_element_type=jnp.float32)
    value = value.astype(jnp.bfloat16)
    prompt_ref[0] = key[:rows]
    prompt_ref[1] = value[:rows]
    cont_ref[0] = key[rows:]
    cont_ref[1] = value[rows:]


def project_keys(hidden, key_weight, value_weight, cosine, sine, rows):
    tokens, depth = hidden.shape
    width = key_weight.shape[1]
    whole = lambda j: (0, 0)
    column = lambda j: (0, j)
    return pl.pallas_call(
        partial(project_keys_body, rows),
        grid=(width // 128,),
        in_specs=[
            pl.BlockSpec((tokens, depth), whole),
            pl.BlockSpec((depth, 128), column),
            pl.BlockSpec((depth, 128), column),
            pl.BlockSpec((tokens, 128), whole),
            pl.BlockSpec((tokens, 128), whole),
        ],
        out_specs=[
            pl.BlockSpec((2, rows, 128), lambda j: (0, 0, j)),
            pl.BlockSpec((2, tokens - rows, 128), lambda j: (0, 0, j)),
        ],
        out_shape=[
            jax.ShapeDtypeStruct((2, rows, width), jnp.bfloat16),
            jax.ShapeDtypeStruct((2, tokens - rows, width), jnp.bfloat16),
        ],
        cost_estimate=pl.CostEstimate(
            flops=4 * tokens * depth * width,
            transcendentals=0,
            bytes_accessed=2 * (tokens * depth + 2 * depth * width + 2 * tokens * width),
        ),
        name="project_keys",
    )(hidden, key_weight, value_weight, cosine, sine)


def gather_keys(near_kv):
    if lax.axis_size("ctx") != 4:
        return lax.all_gather(near_kv, "ctx", axis=1, tiled=True)
    rows = near_kv.shape[1]
    here = lax.axis_index("ctx")
    pair = swap(near_kv, "ctx", 2)
    whole = jnp.zeros((2, 4 * rows, near_kv.shape[2]), near_kv.dtype)
    pieces = ((0, near_kv), (2, pair), (1, swap(near_kv, "ctx", 1)), (3, swap(pair, "ctx", 1)))
    for step, piece in pieces:
        whole = lax.dynamic_update_slice_in_dim(whole, piece, (here ^ step) * rows, axis=1)
    return whole


def head_place(group):
    head = pl.program_id(0)
    key_half = (head // group) % 2
    return head, key_half, (head % 2) != key_half


def attend_forward_body(
    group, prompt_rows, cont_len, pos_ref, q_ref, cos_ref, sin_ref, kp_ref, vp_ref, kc_ref, vc_ref,
    qr_ref, out_ref, log_ref,
):
    head, key_half, swap = head_place(group)
    rotated = turn(q_ref[...], cos_ref[...], sin_ref[...]).astype(jnp.bfloat16)
    qr_ref[...] = rotated
    query = to_key_half(rotated.astype(jnp.float32), swap, key_half) * ATT_SCALE
    query = query.astype(jnp.bfloat16)
    nt = (((1,), (1,)), ((), ()))

    def finish(parts, rows):
        highest = parts[0][0].max(axis=1, keepdims=True)
        for scores, _ in parts[1:]:
            highest = jnp.maximum(highest, scores.max(axis=1, keepdims=True))
        lifted = [jnp.exp2(scores * LOG2E - highest * LOG2E) for scores, _ in parts]
        total = lifted[0].sum(axis=1, keepdims=True)
        for piece in lifted[1:]:
            total = total + piece.sum(axis=1, keepdims=True)
        inverse = 1.0 / total
        result = None
        for piece, (_, value) in zip(lifted, parts):
            term = jnp.dot(
                piece.astype(jnp.bfloat16), value, preferred_element_type=jnp.float32
            )
            result = term if result is None else result + term
        log_total = jnp.broadcast_to(highest + jnp.log(total), (total.shape[0], 128))
        log_ref[0, :, rows] = jnp.transpose(log_total)[:8]
        keep = jnp.where(lane_half(result.shape) == key_half, result * inverse, 0.0)
        keep = jnp.where(swap, pltpu.roll(keep, HEAD_SIZE, 1), keep).astype(jnp.bfloat16)

        @pl.when(head % 2 == 0)
        def _():
            out_ref[rows, :] = keep

        @pl.when(head % 2 == 1)
        def _():
            out_ref[rows, :] = out_ref[rows, :] + keep

    total_rows = q_ref.shape[0]
    first = lax.dot_general(
        query[:prompt_rows], kp_ref[...], nt, preferred_element_type=jnp.float32
    )
    row = lax.broadcasted_iota(jnp.int32, first.shape, 0) + pos_ref[0]
    first = jnp.where(lax.broadcasted_iota(jnp.int32, first.shape, 1) <= row, first, NEG)
    finish([(first, vp_ref[...])], pl.ds(0, prompt_rows))
    lower = query[prompt_rows:]
    wide = lax.dot_general(lower, kp_ref[...], nt, preferred_element_type=jnp.float32)
    near = lax.dot_general(lower, kc_ref[...], nt, preferred_element_type=jnp.float32)
    row = lax.broadcasted_iota(jnp.int32, near.shape, 0)
    col = lax.broadcasted_iota(jnp.int32, near.shape, 1)
    near = jnp.where((col <= row) & (col // cont_len == row // cont_len), near, NEG)
    finish([(wide, vp_ref[...]), (near, vc_ref[...])], pl.ds(prompt_rows, total_rows - prompt_rows))


def attend_forward(q_lin, prompt_kv, cont_kv, cosine, sine, start, rows, cont_len):
    tokens, width = q_lin.shape
    heads = width // HEAD_SIZE
    group = heads // (prompt_kv.shape[2] // HEAD_SIZE)
    keys, near = prompt_kv.shape[1], cont_kv.shape[1]
    tile = lambda h, *_: (0, h // 2)
    same = lambda h, *_: (0, 0)
    return pl.pallas_call(
        partial(attend_forward_body, group, rows, cont_len),
        grid_spec=pltpu.PrefetchScalarGridSpec(
            num_scalar_prefetch=1,
            grid=(heads,),
            in_specs=[
                pl.BlockSpec((tokens, 128), tile),
                pl.BlockSpec((tokens, 128), same),
                pl.BlockSpec((tokens, 128), same),
                pl.BlockSpec((None, keys, 128), lambda h, *_: (0, 0, h // (2 * group))),
                pl.BlockSpec((None, keys, 128), lambda h, *_: (1, 0, h // (2 * group))),
                pl.BlockSpec((None, near, 128), lambda h, *_: (0, 0, h // (2 * group))),
                pl.BlockSpec((None, near, 128), lambda h, *_: (1, 0, h // (2 * group))),
            ],
            out_specs=[
                pl.BlockSpec((tokens, 128), tile),
                pl.BlockSpec((tokens, 128), tile),
                pl.BlockSpec((1, 8, tokens), lambda h, *_: (h, 0, 0)),
            ],
        ),
        out_shape=[
            jax.ShapeDtypeStruct((tokens, width), jnp.bfloat16),
            jax.ShapeDtypeStruct((tokens, width), jnp.bfloat16),
            jax.ShapeDtypeStruct((heads, 8, tokens), jnp.float32),
        ],
        cost_estimate=pl.CostEstimate(
            flops=4 * heads * tokens * (keys + near) * 128,
            transcendentals=heads * tokens * (keys + near),
            bytes_accessed=8 * tokens * width,
        ),
        name="attend_forward",
    )(start, q_lin, cosine, sine, prompt_kv, prompt_kv, cont_kv, cont_kv)


def attend_backward_body(
    group, prompt_rows, cont_len, chunk, pos_ref, q_ref, do_ref, out_ref, log_ref, cos_ref, sin_ref,
    kcos_ref, ksin_ref, kp_ref, vp_ref, kc_ref, vc_ref,
    dq_ref, dkp_ref, dvp_ref, dkc_ref, dvc_ref, dk_acc, dv_acc,
):
    head, key_half, swap = head_place(group)
    tokens = q_ref.shape[0]
    keys = kp_ref.shape[0]
    near = kc_ref.shape[0]
    nt = (((1,), (1,)), ((), ()))
    tn = (((0,), (0,)), ((), ()))

    @pl.when(head % (2 * group) == 0)
    def _():
        dk_acc[...] = jnp.zeros_like(dk_acc)
        dv_acc[...] = jnp.zeros_like(dv_acc)

    query = to_key_half(q_ref[...].astype(jnp.float32), swap, key_half) * ATT_SCALE
    query = query.astype(jnp.bfloat16)
    d_out = to_key_half(do_ref[...].astype(jnp.float32), swap, key_half)
    result = to_key_half(out_ref[...].astype(jnp.float32), swap, key_half)
    centre = jnp.transpose(
        jnp.broadcast_to(jnp.sum(d_out * result, axis=1, keepdims=True), (tokens, 128))
    )[:1]
    d_out = d_out.astype(jnp.bfloat16)
    log_total = log_ref[0][:1]
    row = lax.broadcasted_iota(jnp.int32, (1, tokens), 1)
    limit = jnp.where(row < prompt_rows, row + pos_ref[0], keys)

    def step(key, value, query, d_out, log_total, centre, allowed, at, count):
        scores = lax.dot_general(key, query, nt, preferred_element_type=jnp.float32)
        scores = jnp.where(allowed(scores.shape), scores, NEG)
        weights = jnp.exp2(scores * LOG2E - log_total * LOG2E)
        d_weights = lax.dot_general(value, d_out, nt, preferred_element_type=jnp.float32)
        d_scores = (weights * (d_weights - centre)).astype(jnp.bfloat16)
        dv_acc[at : at + count] += jnp.dot(
            weights.astype(jnp.bfloat16), d_out, preferred_element_type=jnp.float32
        )
        dk_acc[at : at + count] += jnp.dot(d_scores, query, preferred_element_type=jnp.float32)
        return lax.dot_general(d_scores, key, tn, preferred_element_type=jnp.float32)

    d_query = jnp.zeros((tokens, 128), jnp.float32)
    for at in range(0, keys, chunk):

        def seen(shape, at=at):
            return lax.broadcasted_iota(jnp.int32, shape, 0) + at <= limit

        d_query = d_query + step(
            kp_ref[at : at + chunk], vp_ref[at : at + chunk], query, d_out, log_total, centre, seen,
            at, chunk,
        )

    def nearby(shape):
        key_at = lax.broadcasted_iota(jnp.int32, shape, 0)
        query_at = lax.broadcasted_iota(jnp.int32, shape, 1)
        return (key_at <= query_at) & (key_at // cont_len == query_at // cont_len)

    tail = step(
        kc_ref[...], vc_ref[...], query[prompt_rows:], d_out[prompt_rows:],
        log_total[:, prompt_rows:], centre[:, prompt_rows:], nearby, keys, near,
    )
    d_query = jnp.concatenate([d_query[:prompt_rows], d_query[prompt_rows:] + tail], axis=0)
    d_query = jnp.where(lane_half(d_query.shape) == key_half, d_query * ATT_SCALE, 0.0)
    d_query = jnp.where(swap, pltpu.roll(d_query, HEAD_SIZE, 1), d_query)
    d_query = turn(d_query, cos_ref[...], -sin_ref[...]).astype(jnp.bfloat16)

    @pl.when(head % 2 == 0)
    def _():
        dq_ref[...] = d_query

    @pl.when(head % 2 == 1)
    def _():
        dq_ref[...] = dq_ref[...] + d_query

    @pl.when(head % (2 * group) == 2 * group - 1)
    def _():
        dk = turn(dk_acc[...], kcos_ref[...], -ksin_ref[...]).astype(jnp.bfloat16)
        dv = dv_acc[...].astype(jnp.bfloat16)
        dkp_ref[...] = dk[:keys]
        dkc_ref[...] = dk[keys:]
        dvp_ref[...] = dv[:keys]
        dvc_ref[...] = dv[keys:]


def attend_backward(
    query, d_out, result, log_total, prompt_kv, cont_kv, cosine, sine,
    key_cosine, key_sine, start, rows, cont_len,
):
    tokens, width = query.shape
    heads = width // HEAD_SIZE
    key_width = prompt_kv.shape[2]
    group = heads // (key_width // HEAD_SIZE)
    keys, near = prompt_kv.shape[1], cont_kv.shape[1]
    chunk = min(256, keys)
    tile = lambda h, *_: (0, h // 2)
    key_tile = lambda h, *_: (0, h // (2 * group))
    same = lambda h, *_: (0, 0)
    return pl.pallas_call(
        partial(attend_backward_body, group, rows, cont_len, chunk),
        grid_spec=pltpu.PrefetchScalarGridSpec(
            num_scalar_prefetch=1,
            grid=(heads,),
            in_specs=[
                pl.BlockSpec((tokens, 128), tile),
                pl.BlockSpec((tokens, 128), tile),
                pl.BlockSpec((tokens, 128), tile),
                pl.BlockSpec((1, 8, tokens), lambda h, *_: (h, 0, 0)),
                pl.BlockSpec((tokens, 128), same),
                pl.BlockSpec((tokens, 128), same),
                pl.BlockSpec((keys + near, 128), same),
                pl.BlockSpec((keys + near, 128), same),
                pl.BlockSpec((None, keys, 128), lambda h, *_: (0, 0, h // (2 * group))),
                pl.BlockSpec((None, keys, 128), lambda h, *_: (1, 0, h // (2 * group))),
                pl.BlockSpec((None, near, 128), lambda h, *_: (0, 0, h // (2 * group))),
                pl.BlockSpec((None, near, 128), lambda h, *_: (1, 0, h // (2 * group))),
            ],
            out_specs=[
                pl.BlockSpec((tokens, 128), tile),
                pl.BlockSpec((keys, 128), key_tile),
                pl.BlockSpec((keys, 128), key_tile),
                pl.BlockSpec((near, 128), key_tile),
                pl.BlockSpec((near, 128), key_tile),
            ],
            scratch_shapes=[
                pltpu.VMEM((keys + near, 128), jnp.float32),
                pltpu.VMEM((keys + near, 128), jnp.float32),
            ],
        ),
        out_shape=[
            jax.ShapeDtypeStruct((tokens, width), jnp.bfloat16),
            jax.ShapeDtypeStruct((keys, key_width), jnp.bfloat16),
            jax.ShapeDtypeStruct((keys, key_width), jnp.bfloat16),
            jax.ShapeDtypeStruct((near, key_width), jnp.bfloat16),
            jax.ShapeDtypeStruct((near, key_width), jnp.bfloat16),
        ],
        cost_estimate=pl.CostEstimate(
            flops=10 * heads * tokens * (keys + near) * 128,
            transcendentals=heads * tokens * (keys + near),
            bytes_accessed=8 * tokens * width,
        ),
        name="attend_backward",
    )(
        start, query, d_out, result, log_total, cosine, sine, key_cosine, key_sine, prompt_kv,
        prompt_kv, cont_kv, cont_kv,
    )


def reduce_experts(grad, split):
    axes = ("dp", "ctx") if split == 1 else "dp"
    return lax.psum_scatter(grad, axes, scatter_dimension=1, tiled=True)


def send_experts(part, split):
    size = lax.axis_size("ctx")
    if split == 1:
        return (part,)
    if size & (size - 1):
        return (lax.all_to_all(part, "ctx", split_axis=1, concat_axis=0, tiled=True),)
    own, rows, width = part.shape
    here = lax.axis_index("ctx")
    part = part.reshape(own, size, rows // size, width)
    pieces = [lax.dynamic_index_in_dim(part, here ^ step, 1, keepdims=False) for step in range(size)]
    return tuple(swap(piece, "ctx", step) if step else piece for step, piece in enumerate(pieces))


def place_experts(pieces):
    if len(pieces) == 1:
        return pieces[0].astype(jnp.float32)
    here = lax.axis_index("ctx")
    own, rows, width = pieces[0].shape
    whole = jnp.zeros((own * len(pieces), rows, width), jnp.float32)
    for step, piece in enumerate(pieces):
        whole = lax.dynamic_update_slice_in_dim(
            whole, piece.astype(jnp.float32), (here ^ step) * own, axis=0
        )
    return whole


def scatter_keys(d_key, d_value, rows):
    size = lax.axis_size("ctx")
    here = lax.axis_index("ctx")

    def share(owner):
        return jnp.concatenate(
            [
                lax.dynamic_slice_in_dim(d_key, owner * rows, rows, axis=0),
                lax.dynamic_slice_in_dim(d_value, owner * rows, rows, axis=0),
            ],
            axis=1,
        )

    total = share(here).astype(jnp.float32)
    for hop in range(1, size):
        moved = lax.ppermute(
            share((here + hop) % size), "ctx", [(i, (i + hop) % size) for i in range(size)]
        )
        total = total + moved.astype(jnp.float32)
    total = total.astype(jnp.bfloat16)
    return (total[:, : d_key.shape[1]], total[:, d_key.shape[1] :])


def folds(grad):
    return paired(("ctx", "expert")) and grad.shape[0] % (64 * lax.axis_size("dp")) == 0


def fold_one(grad):
    if not folds(grad):
        return lax.psum_scatter(grad, ("dp", "ctx"), scatter_dimension=0, tiled=True)
    rows, width = grad.shape
    parts = lax.axis_size("dp")
    core = lax.axis_index("ctx") % 2
    take = partial(lax.dynamic_index_in_dim, axis=2, keepdims=False)
    grad = grad.reshape(parts, 2, 2, 2, rows // (8 * parts), width)
    return added(take(grad, core), swap(take(grad, 1 - core), "ctx", 1))


def fold_two(one, cut):
    if one.ndim == 2:
        return one, ()
    pair = lax.axis_index("ctx") // 2
    side = lax.axis_index("expert")
    take = partial(lax.dynamic_index_in_dim, keepdims=False)
    left, right = one[..., :cut], one[..., cut:]
    moved = swap(take(left, 1 - pair, 1), "ctx", 2), swap(take(right, 1 - side, 2), "expert", 1)
    return (take(left, pair, 1), take(right, side, 2)), moved


def fold_three(kept, moved):
    if not moved:
        return kept
    pair = lax.axis_index("ctx") // 2
    side = lax.axis_index("expert")
    take = partial(lax.dynamic_index_in_dim, keepdims=False)
    left, right = added(kept[0], moved[0]), added(kept[1], moved[1])
    left_sent = swap(take(left, 1 - side, 1), "expert", 1)
    right_sent = swap(take(right, 1 - pair, 1), "ctx", 2)
    whole = jnp.concatenate(
        [added(take(left, side, 1), left_sent), added(take(right, pair, 1), right_sent)], axis=-1
    )
    return scatter_parts(whole)


def scatter_parts(parts):
    size = lax.axis_size("dp")
    here = lax.axis_index("dp")
    take = partial(lax.dynamic_index_in_dim, axis=0, keepdims=False)
    total = take(parts, here).astype(jnp.float32)
    for hop in range(1, size):
        moved = lax.ppermute(
            take(parts, (here + hop) % size), "dp", [(i, (i + hop) % size) for i in range(size)]
        )
        total = total + moved.astype(jnp.float32)
    return total.astype(jnp.bfloat16)


def finish_dense(grad, rows):
    if grad.shape[0] == rows:
        return lax.psum(grad, "expert").astype(jnp.float32)
    other = swap(grad, "expert", 1)
    first = lax.axis_index("expert") == 0
    return jnp.concatenate(
        [jnp.where(first, grad, other), jnp.where(first, other, grad)], axis=0
    ).astype(jnp.float32)


def per_device(
    x_prompt,
    x_cont,
    norm1_gain,
    w_query,
    key_weight,
    value_weight,
    w_out,
    norm2_gain,
    w_router,
    w_gate_up,
    w_down,
    routes_prompt,
    routes_cont,
    slot_order,
    dy_prompt,
    dy_cont,
):
    model_width = x_prompt.shape[2]
    prompt_rows = x_prompt.shape[1]
    cont_count = x_cont.shape[1]
    cont_len = x_cont.shape[2]
    cont_rows = cont_count * cont_len
    count_of_tokens = prompt_rows + cont_rows
    key_value_width = KEY_VALUE_HEADS * HEAD_SIZE
    local_experts = w_gate_up.shape[0]
    expert_groups = lax.axis_size("expert")
    expert_total = local_experts * expert_groups
    top_count = routes_prompt.shape[2]
    capacity = (count_of_tokens * top_count + expert_total - 1) // expert_total
    hidden_units = w_down.shape[1]
    prompt_total = prompt_rows * lax.axis_size("ctx")
    count_of_keys = prompt_total + cont_rows
    split = lax.axis_size("ctx") if local_experts % lax.axis_size("ctx") == 0 else 1
    own = local_experts // split
    blocks = split * expert_groups
    slots = -(-capacity // 8) * 8
    group = ("ctx", "expert") if split > 1 else ("expert",)
    block_index = lax.axis_index(group)
    own_offset = lax.axis_index("ctx") * own if split > 1 else 0
    first_expert = lax.axis_index("expert") * local_experts + own_offset
    gate_up_own = w_gate_up
    down_own = w_down
    if split > 1:
        gate_up_own = lax.dynamic_slice_in_dim(w_gate_up, own_offset, own, axis=0)
        down_own = lax.dynamic_slice_in_dim(w_down, own_offset, own, axis=0)
    routes = jnp.concatenate(
        [routes_prompt[0], routes_cont[0].reshape(cont_rows, top_count)], axis=0
    )
    codes = slot_codes(routes, slot_order[0, 0], expert_total, capacity)
    upstream_low = jnp.concatenate([dy_prompt[0], dy_cont[0].reshape(cont_rows, model_width)], axis=0)
    upstream = upstream_low.astype(jnp.float32)
    assert capacity <= 256
    fold = model_width // count_of_tokens
    code_rows = -(-expert_total // (8 * fold)) * 8
    code_table = jnp.pad(
        codes.astype(jnp.bfloat16),
        ((0, code_rows * fold - expert_total), (0, 0)),
        constant_values=-2.0,
    )
    code_table = jnp.concatenate(
        [code_table[i * code_rows : (i + 1) * code_rows] for i in range(fold)], axis=1
    )
    upstream_all = lax.all_gather(
        jnp.concatenate([upstream_low, code_table], axis=0), group, axis=0, tiled=False
    )
    codes_all = upstream_all[:, count_of_tokens:]
    codes_all = jnp.concatenate(
        [
            codes_all[:, :, i * count_of_tokens : (i + 1) * count_of_tokens] for i in range(fold)
        ],
        axis=1,
    ).astype(jnp.float32)
    own_codes = lax.dynamic_slice_in_dim(codes_all, first_expert, own, axis=1)
    own_codes = jnp.pad(own_codes, ((0, 0), (0, -own % 8), (0, 0)), constant_values=-2.0)
    d_slot_rows = dispatch(own_codes, upstream_all, own, slots)
    d_plain = jnp.einsum("ecd,efd->ecf", d_slot_rows, down_own, preferred_element_type=jnp.float32)
    gain_one = norm1_gain.astype(jnp.float32)
    gain_two = norm2_gain.astype(jnp.float32)
    tokens = jnp.concatenate(
        [x_prompt[0], x_cont[0].reshape(cont_rows, model_width)], axis=0
    ).astype(jnp.float32)
    normed_one, scale_one = rms_forward(tokens, gain_one)
    h1_low = normed_one.astype(jnp.bfloat16)
    row_index = jnp.arange(count_of_tokens, dtype=jnp.int32)
    cont_offset = row_index - prompt_rows
    start = lax.axis_index("ctx") * prompt_rows
    query_pos = jnp.where(
        cont_offset >= 0, prompt_total + cont_offset % cont_len, start + row_index
    )
    key_index = jnp.arange(count_of_keys, dtype=jnp.int32)
    key_pos = jnp.where(
        key_index >= prompt_total, prompt_total + (key_index - prompt_total) % cont_len, key_index
    )
    start = start.astype(jnp.int32)[None]
    cosine, sine = signed_tables(query_pos.astype(jnp.float32))
    key_cosine, key_sine = signed_tables(key_pos.astype(jnp.float32))
    near_kv, cont_kv = project_keys(
        h1_low, key_weight, value_weight, cosine, sine, prompt_rows
    )
    prompt_kv = gather_keys(near_kv)
    q_lin = jnp.dot(h1_low, w_query, preferred_element_type=jnp.float32)
    query_row_block, merged_low, log_total = attend_forward(
        q_lin, prompt_kv, cont_kv, cosine, sine, start, prompt_rows, cont_len
    )
    branch = jnp.dot(merged_low, w_out, preferred_element_type=jnp.float32)
    resid = tokens + RESID * branch
    normed_two, scale_two = rms_forward(resid, gain_two)
    h2_low = normed_two.astype(jnp.bfloat16)
    rows_all = lax.all_gather(h2_low, group, axis=0, tiled=False)
    named = codes > -1.5
    logits = jnp.einsum("td,de->et", h2_low, w_router, preferred_element_type=jnp.float32)
    logits = jnp.where(named, logits, NEG)
    lifted = jnp.where(named, jnp.exp(logits - jnp.max(logits, axis=0, keepdims=True)), 0.0)
    gates = lifted / jnp.sum(lifted, axis=0, keepdims=True)
    own_gates, rows_all, d_plain = lax.optimization_barrier(
        (gather_gates(gates, group, first_expert, own), rows_all, d_plain)
    )
    slot_rows = dispatch(own_codes, rows_all, own, slots)
    slot_index = jnp.arange(slots, dtype=jnp.int32).astype(jnp.float32)
    picked = own_codes[:, :own, None, :] == slot_index[None, None, :, None]
    slot_gate = jnp.sum(jnp.where(picked, own_gates[:, :, None, :], 0.0), axis=-1)
    slot_gate = slot_gate.transpose(1, 0, 2).reshape(own, blocks * slots)
    weighted, d_both, d_slot_gate = experts(
        own_offset, slot_rows, w_gate_up, d_plain, RESID * slot_gate[:, :, None]
    )
    d_slot_gate = RESID * d_slot_gate[:, :, 0]
    grad_down = jnp.einsum(
        "ecf,ecd->efd", weighted, d_slot_rows, preferred_element_type=jnp.float32
    ).astype(jnp.bfloat16)
    d_gates_own = jnp.sum(
        jnp.where(
            picked,
            d_slot_gate.reshape(own, blocks, slots).transpose(1, 0, 2)[..., None],
            0.0,
        ),
        axis=2,
    )
    d_both, _, d_gates = lax.optimization_barrier(
        (d_both, grad_down, return_gates(d_gates_own, group, first_expert, expert_total))
    )
    down_part = reduce_experts(grad_down, split)
    d_slots = jnp.einsum(
        "ecf,edf->ecd", d_both, gate_up_own, preferred_element_type=jnp.float32
    ).astype(jnp.bfloat16)
    part, weighted, slot_rows = lax.optimization_barrier(
        (scatter_one(*pair_sums(own_codes, d_slots, own, slots, group)), weighted, slot_rows)
    )
    kept, moved = scatter_two(part)
    grad_gate, grad_up = (
        jnp.einsum(
            "ecd,ecf->edf", slot_rows, d_part, preferred_element_type=jnp.float32
        ).astype(jnp.bfloat16)
        for d_part in (d_both[..., :hidden_units], d_both[..., hidden_units:])
    )
    expert_out = jnp.einsum(
        "ecf,efd->ecd", weighted, down_own, preferred_element_type=jnp.float32
    ).astype(jnp.bfloat16)
    moved, grad_gate, grad_up, expert_out = lax.optimization_barrier(
        (moved, grad_gate, grad_up, expert_out)
    )
    gate_part, up_part = reduce_experts(grad_gate, split), reduce_experts(grad_up, split)
    kept, moved = scatter_three(kept, moved)
    moved, sums = lax.optimization_barrier(
        (moved, pair_sums(own_codes, expert_out, own, slots, group))
    )
    d_rows = scatter_end(kept, moved)
    mixed_part = scatter_one(*sums)
    d_logits = (
        gates * (d_gates - jnp.sum(gates * d_gates, axis=0, keepdims=True))
    ).astype(jnp.bfloat16)
    grad_router = jnp.einsum("td,et->de", h2_low, d_logits, preferred_element_type=jnp.float32)
    d_normed_two = d_rows + jnp.einsum(
        "et,de->td", d_logits, w_router, preferred_element_type=jnp.float32
    )
    d_resid_norm, grad_norm2 = rms_backward(resid, scale_two, gain_two, d_normed_two)
    d_resid = upstream + d_resid_norm
    d_branch = (RESID * d_resid).astype(jnp.bfloat16)
    grad_out = jnp.einsum(
        "tq,td->qd", merged_low, d_branch, preferred_element_type=jnp.float32
    ).astype(jnp.bfloat16)
    out_cut = grad_out.shape[1] // 256 * 128
    grad_out = fold_one(grad_out)
    merged_gradient = jnp.einsum(
        "td,qd->tq", d_branch, w_out, preferred_element_type=jnp.float32
    ).astype(jnp.bfloat16)
    grad_out, mixed_part, down_part, merged_gradient = lax.optimization_barrier(
        (grad_out, mixed_part, down_part, merged_gradient)
    )
    mixed_kept, mixed_moved = scatter_two(mixed_part)
    out_kept, out_moved = fold_two(grad_out, out_cut)
    down_sent = send_experts(down_part, split)
    d_query_low, d_key_prompt, d_value_prompt, d_key_cont, d_value_cont = attend_backward(
        query_row_block, merged_gradient, merged_low, log_total, prompt_kv, cont_kv, cosine, sine,
        key_cosine, key_sine, start, prompt_rows, cont_len,
    )
    mixed_moved, out_moved, down_sent, d_key_prompt = lax.optimization_barrier(
        (mixed_moved, out_moved, down_sent, d_key_prompt)
    )
    mixed_kept, mixed_moved = scatter_three(mixed_kept, mixed_moved)
    grad_out = fold_three(out_kept, out_moved)
    mixed = scatter_end(mixed_kept, mixed_moved)
    output = resid + mixed
    y_prompt = output[:prompt_rows].astype(jnp.bfloat16)[None]
    y_cont = output[prompt_rows:].reshape(1, cont_count, cont_len, model_width).astype(jnp.bfloat16)
    d_key_prompt, d_value_prompt = scatter_keys(d_key_prompt, d_value_prompt, prompt_rows)
    d_key_low = jnp.concatenate([d_key_prompt, d_key_cont], axis=0)
    d_value_low = jnp.concatenate([d_value_prompt, d_value_cont], axis=0)
    grad_query = jnp.einsum("td,tq->dq", h1_low, d_query_low, preferred_element_type=jnp.float32)
    grad_key = jnp.einsum("td,tq->dq", h1_low, d_key_low, preferred_element_type=jnp.float32)
    grad_value = jnp.einsum("td,tq->dq", h1_low, d_value_low, preferred_element_type=jnp.float32)
    d_normed_one = jnp.einsum("tq,dq->td", d_query_low, w_query, preferred_element_type=jnp.float32)
    d_normed_one = d_normed_one + jnp.einsum(
        "tq,dq->td", d_key_low, key_weight, preferred_element_type=jnp.float32
    )
    d_normed_one = d_normed_one + jnp.einsum(
        "tq,dq->td", d_value_low, value_weight, preferred_element_type=jnp.float32
    )
    d_tokens_norm, grad_norm1 = rms_backward(tokens, scale_one, gain_one, d_normed_one)
    d_tokens = d_resid + d_tokens_norm
    dx_prompt = d_tokens[:prompt_rows][None]
    dx_cont = d_tokens[prompt_rows:].reshape(1, cont_count, cont_len, model_width)
    small = jnp.concatenate([grad_router, grad_norm1[:, None], grad_norm2[:, None]], axis=1)
    small = jnp.pad(small, ((0, 0), (0, -small.shape[1] % 128)))
    dense = jnp.concatenate([grad_query, grad_key, grad_value, small], axis=1).astype(jnp.bfloat16)
    heads_width = QUERY_HEADS * HEAD_SIZE
    edge = heads_width + 2 * key_value_width
    dense, gate_part = lax.optimization_barrier((fold_one(dense), gate_part))
    gate_sent = send_experts(gate_part, split)
    dense_kept, dense_moved = fold_two(dense, edge // 256 * 128)
    dense_moved, gate_sent = lax.optimization_barrier((dense_moved, gate_sent))
    dense_rows = w_query.shape[0] // (lax.axis_size("dp") * lax.axis_size("ctx"))
    dense = finish_dense(fold_three(dense_kept, dense_moved), dense_rows)
    grad_out = finish_dense(grad_out, dense_rows)
    grad_down = place_experts(down_sent)
    grad_gate = place_experts(gate_sent)
    dense, up_part = lax.optimization_barrier((dense, up_part))
    grad_up = place_experts(send_experts(up_part, split))
    grad_gate_up = jnp.concatenate([grad_gate, grad_up], axis=-1)
    return (
        y_prompt,
        y_cont,
        dx_prompt,
        dx_cont,
        dense[:, edge + expert_total],
        dense[:, :heads_width],
        dense[:, heads_width : heads_width + key_value_width],
        dense[:, heads_width + key_value_width : edge],
        grad_out,
        dense[:, edge + expert_total + 1],
        dense[:, edge : edge + expert_total],
        grad_gate_up,
        grad_down,
    )


def solution(mesh):
    return jax.shard_map(
        per_device,
        mesh=mesh,
        in_specs=(
            P(("dp", "expert"), "ctx", None),
            P(("dp", "expert"), "ctx", None, None),
            P(),
            P(),
            P(),
            P(),
            P(),
            P(),
            P(),
            P("expert", None, None),
            P("expert", None, None),
            P(("dp", "expert"), "ctx", None),
            P(("dp", "expert"), "ctx", None, None),
            P(("dp", "expert"), "ctx", None),
            P(("dp", "expert"), "ctx", None),
            P(("dp", "expert"), "ctx", None, None),
        ),
        out_specs=(
            P(("dp", "expert"), "ctx", None),
            P(("dp", "expert"), "ctx", None, None),
            P(("dp", "expert"), "ctx", None),
            P(("dp", "expert"), "ctx", None, None),
            P(("dp", "ctx")),
            P(("dp", "ctx"), None),
            P(("dp", "ctx"), None),
            P(("dp", "ctx"), None),
            P(("dp", "ctx"), None),
            P(("dp", "ctx")),
            P(("dp", "ctx"), None),
            P("expert", ("dp", "ctx"), None),
            P("expert", ("dp", "ctx"), None),
        ),
        check_vma=False,
    )
```

```python
from functools import partial

import jax
import jax.numpy as jnp
from jax import lax
from jax.experimental import pallas as pl
from jax.experimental.pallas import tpu as pltpu
from jax.sharding import PartitionSpec as P

QUERY_HEADS = 24
KEY_VALUE_HEADS = 8
HEAD_SIZE = 64


EPS = 1e-06
RESID = 0.22
ATT_SCALE = 0.015625
THETA = 10000.0
NEG = -1e30
LOG2E = 1.4426950408889634


def signed_tables(positions):
    lane = jnp.arange(2 * HEAD_SIZE, dtype=jnp.int32) % HEAD_SIZE
    half_dim = HEAD_SIZE // 2
    frequency = THETA ** (-((lane % half_dim).astype(jnp.float32) * 2.0 / HEAD_SIZE))
    angles = positions[:, None] * frequency[None, :]
    return (jnp.cos(angles), jnp.where(lane < half_dim, -1.0, 1.0) * jnp.sin(angles))


def rms_forward(values, norm_gain):
    inverse = lax.rsqrt(jnp.mean(values * values, axis=-1, keepdims=True) + EPS)
    return (values * inverse * norm_gain, inverse)


def rms_backward(values, inverse, norm_gain, upstream):
    normed = values * inverse
    weighted = upstream * norm_gain
    projected = jnp.mean(weighted * normed, axis=-1, keepdims=True)
    return (inverse * (weighted - normed * projected), jnp.sum(upstream * normed, axis=0))


def slot_codes(routes, visit_order, experts, capacity):
    count = routes.shape[0]
    ids = jnp.arange(count, dtype=jnp.int32)
    visit = jnp.arange(count, dtype=jnp.float32)
    place = (visit_order[:, None] == ids[None, :]).astype(jnp.float32)
    place_row = jnp.sum(place * visit[:, None], axis=0)
    place_col = jnp.sum((visit_order[None, :] == ids[:, None]).astype(jnp.float32) * visit[None, :], axis=1)
    earlier = (place_col[:, None] < place_row[None, :]).astype(jnp.bfloat16)
    named = jnp.any(
        routes.T[None, :, :] == jnp.arange(experts, dtype=jnp.int32)[:, None, None], axis=1
    )
    rank = jnp.dot(named.astype(jnp.bfloat16), earlier, preferred_element_type=jnp.float32)
    return jnp.where(named, jnp.where(rank < capacity, rank, -1.0), -2.0)


def selection(codes, own, slots):
    tokens = codes.shape[-1]
    slot_index = lax.broadcasted_iota(jnp.int32, (slots, tokens), 0).astype(jnp.float32)
    picks = [
        jnp.where(codes[e : e + 1, :] == slot_index, 1.0, 0.0).astype(jnp.bfloat16)
        for e in range(own)
    ]
    return jnp.concatenate(picks, axis=0)


def dispatch_body(own, slots, codes_ref, rows_ref, out_ref):
    pick = selection(codes_ref[0], own, slots)
    moved = jnp.dot(pick, rows_ref[0], preferred_element_type=jnp.float32).astype(jnp.bfloat16)
    for e in range(own):
        out_ref[e] = moved[e * slots : (e + 1) * slots]


def dispatch(codes, rows, own, slots):
    blocks, _, width = rows.shape
    tokens = codes.shape[2]
    return pl.pallas_call(
        partial(dispatch_body, own, slots),
        grid=(blocks,),
        in_specs=[
            pl.BlockSpec((1, codes.shape[1], tokens), lambda b: (b, 0, 0)),
            pl.BlockSpec((1, tokens, width), lambda b: (b, 0, 0)),
        ],
        out_specs=pl.BlockSpec((own, slots, width), lambda b: (0, b, 0)),
        out_shape=jax.ShapeDtypeStruct((own, blocks * slots, width), jnp.bfloat16),
        cost_estimate=pl.CostEstimate(
            flops=2 * blocks * own * slots * tokens * width,
            transcendentals=0,
            bytes_accessed=2 * blocks * (tokens + own * slots) * width,
        ),
        name="dispatch",
    )(codes, rows)


def experts_body(at_ref, rows_ref, gate_up_ref, plain_ref, weight_ref, out_ref, both_ref, d_weight_ref):
    total = rows_ref.shape[1]
    hidden_units = plain_ref.shape[2]
    chunk = total // 2 if total % 16 == 0 else total
    for at in range(0, total, chunk):
        rows = pl.ds(at, chunk)
        both = jnp.dot(rows_ref[0, rows], gate_up_ref[0], preferred_element_type=jnp.float32)
        gate, up = both[:, :hidden_units], both[:, hidden_units:]
        plain, weight = plain_ref[0, rows], weight_ref[0, rows]
        logistic = jax.nn.sigmoid(gate)
        silu = gate * logistic
        hidden = silu * up
        d_weight_ref[0, rows] = jnp.sum(hidden * plain, axis=1, keepdims=True)
        out_ref[0, rows] = (weight * hidden).astype(jnp.bfloat16)
        d_hidden = weight * plain
        d_gate = d_hidden * up * (logistic + silu * (1.0 - logistic))
        both_ref[0, rows, :hidden_units] = d_gate.astype(jnp.bfloat16)
        both_ref[0, rows, hidden_units:] = (d_hidden * silu).astype(jnp.bfloat16)


def experts(offset, rows, gate_up, plain, weight):
    own, total, width = rows.shape
    hidden_units = plain.shape[2]
    part = total // 2 if total % 32 == 0 else total
    tile = lambda e, r, at: (e, r, 0)
    return pl.pallas_call(
        experts_body,
        grid_spec=pltpu.PrefetchScalarGridSpec(
            num_scalar_prefetch=1,
            grid=(own, total // part),
            in_specs=[
                pl.BlockSpec((1, part, width), tile),
                pl.BlockSpec((1, width, 2 * hidden_units), lambda e, r, at: (at[0] + e, 0, 0)),
                pl.BlockSpec((1, part, hidden_units), tile),
                pl.BlockSpec((1, part, 1), tile),
            ],
            out_specs=[
                pl.BlockSpec((1, part, hidden_units), tile),
                pl.BlockSpec((1, part, 2 * hidden_units), tile),
                pl.BlockSpec((1, part, 1), tile),
            ],
        ),
        out_shape=[
            jax.ShapeDtypeStruct((own, total, hidden_units), jnp.bfloat16),
            jax.ShapeDtypeStruct((own, total, 2 * hidden_units), jnp.bfloat16),
            jax.ShapeDtypeStruct((own, total, 1), jnp.float32),
        ],
        cost_estimate=pl.CostEstimate(
            flops=4 * own * total * width * hidden_units,
            transcendentals=own * total * hidden_units,
            bytes_accessed=2 * own * (total * (width + 4 * hidden_units) + 2 * width * hidden_units),
        ),
        name="experts",
    )(jnp.asarray(offset, jnp.int32).reshape(1), rows, gate_up, plain, weight)


def combine_body(own, slots, at_ref, codes_ref, rows_ref, *refs):
    out_ref = refs[-1]
    pick = selection(codes_ref[0], own, slots)
    rows = rows_ref[...].reshape(own * slots, rows_ref.shape[-1])
    total = lax.dot_general(
        pick, rows, (((0,), (0,)), ((), ())), preferred_element_type=jnp.float32
    )
    for ref in refs[:-1]:
        total = total + ref[0].astype(jnp.float32)
    out_ref[0] = total.astype(out_ref.dtype)


def combine(at, codes, rows, own, slots, *more):
    count, tokens = at.shape[0], codes.shape[2]
    width = rows.shape[-1]
    return pl.pallas_call(
        partial(combine_body, own, slots),
        grid_spec=pltpu.PrefetchScalarGridSpec(
            num_scalar_prefetch=1,
            grid=(count,),
            in_specs=[
                pl.BlockSpec((1, codes.shape[1], tokens), lambda b, at: (at[b], 0, 0)),
                pl.BlockSpec((own, slots, width), lambda b, at: (0, at[b], 0)),
            ]
            + [pl.BlockSpec((1, tokens, width), lambda b, at: (b, 0, 0)) for _ in more],
            out_specs=pl.BlockSpec((1, tokens, width), lambda b, at: (b, 0, 0)),
        ),
        out_shape=jax.ShapeDtypeStruct((count, tokens, width), jnp.bfloat16),
        cost_estimate=pl.CostEstimate(flops=1, transcendentals=0, bytes_accessed=1),
        name="combine",
    )(at, codes, rows, *more)


def swap(values, axis, bit):
    size = lax.axis_size(axis)
    return lax.ppermute(values, axis, [(i, i ^ bit) for i in range(size)])


def exchange(values, bit, axis, stride, dim):
    take = partial(lax.dynamic_index_in_dim, axis=dim, keepdims=False)
    away = swap(take(values, 1 - bit), axis, stride)
    stay = take(values, bit)
    first = bit == 0
    return jnp.stack([jnp.where(first, stay, away), jnp.where(first, away, stay)])


def paired(group):
    return group == ("ctx", "expert") and lax.axis_size("ctx") == 4 and lax.axis_size("expert") == 2


def gather_gates(gates, group, first_expert, own):
    if not paired(group):
        whole = lax.all_gather(gates, group, axis=0, tiled=False)
        return lax.dynamic_slice_in_dim(whole, first_expert, own, axis=1)
    ctx, side = lax.axis_index("ctx"), lax.axis_index("expert")
    parts = gates.reshape(2, 2, 2, own, gates.shape[1])
    parts = exchange(parts, side, "expert", 1, 0)
    parts = exchange(parts, ctx % 2, "ctx", 1, 2)
    parts = exchange(parts, ctx // 2, "ctx", 2, 2)
    return parts.reshape(8, own, gates.shape[1])


def return_gates(values, group, first_expert, experts):
    blocks, own, tokens = values.shape
    if not paired(group):
        whole = jnp.zeros((blocks, experts, tokens), values.dtype)
        whole = lax.dynamic_update_slice_in_dim(whole, values, first_expert, axis=1)
        return lax.psum_scatter(whole, group, scatter_dimension=0)
    ctx, side = lax.axis_index("ctx"), lax.axis_index("expert")
    parts = values.reshape(2, 2, 2, own, tokens)
    parts = exchange(parts, ctx // 2, "ctx", 2, 0)
    parts = exchange(parts, ctx % 2, "ctx", 1, 1)
    parts = exchange(parts, side, "expert", 1, 2)
    return parts.transpose(0, 2, 1, 3, 4).reshape(experts, tokens)


def added(left, right):
    return (left.astype(jnp.float32) + right.astype(jnp.float32)).astype(jnp.bfloat16)


def far_sum(codes, rows, own, slots, group):
    if not paired(group):
        return jnp.zeros((), jnp.bfloat16)
    far = lax.axis_index(group).astype(jnp.int32) ^ jnp.array([2, 3, 6, 7], jnp.int32)
    return combine(far, codes, rows, own, slots)


def cross(far):
    return swap(far, "ctx", 1) if far.ndim else far


def scatter_one(codes, rows, own, slots, group, sent):
    if not paired(group):
        every = jnp.arange(codes.shape[0], dtype=jnp.int32)
        return lax.psum_scatter(
            combine(every, codes, rows, own, slots), group, scatter_dimension=0
        )
    near = lax.axis_index(group).astype(jnp.int32) ^ jnp.array([0, 1, 4, 5], jnp.int32)
    return combine(near, codes, rows, own, slots, sent)


def scatter_two(part):
    if part.ndim == 2:
        return part, ()
    half = part.shape[-1] // 2
    left, right = part[:, :, :half], part[:, :, half:]
    moved = swap(left[2:], "ctx", 2), swap(jnp.stack([right[1], right[3]]), "expert", 1)
    return (left[0], left[1], right[0], right[2]), moved


def scatter_three(kept, moved):
    if not moved:
        return kept, ()
    left, left_other, right, right_other = kept
    left_sent, right_sent = moved
    onward = (
        swap(added(left_other, left_sent[1]), "expert", 1),
        swap(added(right_other, right_sent[1]), "ctx", 2),
    )
    return (left, left_sent[0], right, right_sent[0]), onward


def scatter_end(kept, moved):
    if not moved:
        return kept.astype(jnp.float32)
    wide = lambda *pieces: sum(piece.astype(jnp.float32) for piece in pieces)
    return jnp.concatenate(
        [wide(kept[0], kept[1], moved[0]), wide(kept[2], kept[3], moved[1])], axis=1
    )


def lane_half(shape):
    return lax.broadcasted_iota(jnp.int32, shape, 1) // HEAD_SIZE


def turn(values, cosine, sine):
    half_dim = HEAD_SIZE // 2
    width = values.shape[1]
    lane = lax.broadcasted_iota(jnp.int32, values.shape, 1) % HEAD_SIZE
    partner = jnp.where(
        lane < half_dim,
        pltpu.roll(values, width - half_dim, 1),
        pltpu.roll(values, half_dim, 1),
    )
    return values * cosine + partner * sine


def to_key_half(values, swap, key_half):
    moved = jnp.where(swap, pltpu.roll(values, HEAD_SIZE, 1), values)
    return jnp.where(lane_half(values.shape) == key_half, moved, 0.0)


def project_keys_body(rows, h_ref, kw_ref, vw_ref, cos_ref, sin_ref, prompt_ref, cont_ref):
    key = jnp.dot(h_ref[...], kw_ref[...], preferred_element_type=jnp.float32)
    key = turn(key, cos_ref[...], sin_ref[...]).astype(jnp.bfloat16)
    value = jnp.dot(h_ref[...], vw_ref[...], preferred_element_type=jnp.float32)
    value = value.astype(jnp.bfloat16)
    prompt_ref[0] = key[:rows]
    prompt_ref[1] = value[:rows]
    cont_ref[0] = key[rows:]
    cont_ref[1] = value[rows:]


def project_keys(hidden, key_weight, value_weight, cosine, sine, rows):
    tokens, depth = hidden.shape
    width = key_weight.shape[1]
    whole = lambda j: (0, 0)
    column = lambda j: (0, j)
    return pl.pallas_call(
        partial(project_keys_body, rows),
        grid=(width // 128,),
        in_specs=[
            pl.BlockSpec((tokens, depth), whole),
            pl.BlockSpec((depth, 128), column),
            pl.BlockSpec((depth, 128), column),
            pl.BlockSpec((tokens, 128), whole),
            pl.BlockSpec((tokens, 128), whole),
        ],
        out_specs=[
            pl.BlockSpec((2, rows, 128), lambda j: (0, 0, j)),
            pl.BlockSpec((2, tokens - rows, 128), lambda j: (0, 0, j)),
        ],
        out_shape=[
            jax.ShapeDtypeStruct((2, rows, width), jnp.bfloat16),
            jax.ShapeDtypeStruct((2, tokens - rows, width), jnp.bfloat16),
        ],
        cost_estimate=pl.CostEstimate(
            flops=4 * tokens * depth * width,
            transcendentals=0,
            bytes_accessed=2 * (tokens * depth + 2 * depth * width + 2 * tokens * width),
        ),
        name="project_keys",
    )(hidden, key_weight, value_weight, cosine, sine)


def gather_keys(near_kv, work):
    if lax.axis_size("ctx") != 4:
        return lax.all_gather(near_kv, "ctx", axis=1, tiled=True), work
    rows = near_kv.shape[1]
    here = lax.axis_index("ctx")
    pair, side, work = lax.optimization_barrier(
        (swap(near_kv, "ctx", 2), swap(near_kv, "ctx", 1), work)
    )
    whole = jnp.zeros((2, 4 * rows, near_kv.shape[2]), near_kv.dtype)
    pieces = ((0, near_kv), (2, pair), (1, side), (3, swap(pair, "ctx", 1)))
    for step, piece in pieces:
        whole = lax.dynamic_update_slice_in_dim(whole, piece, (here ^ step) * rows, axis=1)
    return whole, work


def head_place(group):
    head = pl.program_id(0)
    key_half = (head // group) % 2
    return head, key_half, (head % 2) != key_half


def attend_forward_body(
    group, prompt_rows, cont_len, pos_ref, q_ref, cos_ref, sin_ref, kp_ref, vp_ref, kc_ref, vc_ref,
    qr_ref, out_ref, log_ref,
):
    head, key_half, swap = head_place(group)
    rotated = turn(q_ref[...], cos_ref[...], sin_ref[...]).astype(jnp.bfloat16)
    qr_ref[...] = rotated
    query = to_key_half(rotated.astype(jnp.float32), swap, key_half) * ATT_SCALE
    query = query.astype(jnp.bfloat16)
    nt = (((1,), (1,)), ((), ()))

    def finish(parts, rows):
        highest = parts[0][0].max(axis=1, keepdims=True)
        for scores, _ in parts[1:]:
            highest = jnp.maximum(highest, scores.max(axis=1, keepdims=True))
        lifted = [jnp.exp2(scores * LOG2E - highest * LOG2E) for scores, _ in parts]
        total = lifted[0].sum(axis=1, keepdims=True)
        for piece in lifted[1:]:
            total = total + piece.sum(axis=1, keepdims=True)
        inverse = 1.0 / total
        result = None
        for piece, (_, value) in zip(lifted, parts):
            term = jnp.dot(
                piece.astype(jnp.bfloat16), value, preferred_element_type=jnp.float32
            )
            result = term if result is None else result + term
        log_total = jnp.broadcast_to(highest + jnp.log(total), (total.shape[0], 128))
        log_ref[0, :, rows] = jnp.transpose(log_total)[:8]
        keep = jnp.where(lane_half(result.shape) == key_half, result * inverse, 0.0)
        keep = jnp.where(swap, pltpu.roll(keep, HEAD_SIZE, 1), keep).astype(jnp.bfloat16)

        @pl.when(head % 2 == 0)
        def _():
            out_ref[rows, :] = keep

        @pl.when(head % 2 == 1)
        def _():
            out_ref[rows, :] = out_ref[rows, :] + keep

    total_rows = q_ref.shape[0]
    first = lax.dot_general(
        query[:prompt_rows], kp_ref[...], nt, preferred_element_type=jnp.float32
    )
    row = lax.broadcasted_iota(jnp.int32, first.shape, 0) + pos_ref[0]
    first = jnp.where(lax.broadcasted_iota(jnp.int32, first.shape, 1) <= row, first, NEG)
    finish([(first, vp_ref[...])], pl.ds(0, prompt_rows))
    lower = query[prompt_rows:]
    wide = lax.dot_general(lower, kp_ref[...], nt, preferred_element_type=jnp.float32)
    near = lax.dot_general(lower, kc_ref[...], nt, preferred_element_type=jnp.float32)
    row = lax.broadcasted_iota(jnp.int32, near.shape, 0)
    col = lax.broadcasted_iota(jnp.int32, near.shape, 1)
    near = jnp.where((col <= row) & (col // cont_len == row // cont_len), near, NEG)
    finish([(wide, vp_ref[...]), (near, vc_ref[...])], pl.ds(prompt_rows, total_rows - prompt_rows))


def attend_forward(q_lin, prompt_kv, cont_kv, cosine, sine, start, rows, cont_len):
    tokens, width = q_lin.shape
    heads = width // HEAD_SIZE
    group = heads // (prompt_kv.shape[2] // HEAD_SIZE)
    keys, near = prompt_kv.shape[1], cont_kv.shape[1]
    tile = lambda h, *_: (0, h // 2)
    same = lambda h, *_: (0, 0)
    return pl.pallas_call(
        partial(attend_forward_body, group, rows, cont_len),
        grid_spec=pltpu.PrefetchScalarGridSpec(
            num_scalar_prefetch=1,
            grid=(heads,),
            in_specs=[
                pl.BlockSpec((tokens, 128), tile),
                pl.BlockSpec((tokens, 128), same),
                pl.BlockSpec((tokens, 128), same),
                pl.BlockSpec((None, keys, 128), lambda h, *_: (0, 0, h // (2 * group))),
                pl.BlockSpec((None, keys, 128), lambda h, *_: (1, 0, h // (2 * group))),
                pl.BlockSpec((None, near, 128), lambda h, *_: (0, 0, h // (2 * group))),
                pl.BlockSpec((None, near, 128), lambda h, *_: (1, 0, h // (2 * group))),
            ],
            out_specs=[
                pl.BlockSpec((tokens, 128), tile),
                pl.BlockSpec((tokens, 128), tile),
                pl.BlockSpec((1, 8, tokens), lambda h, *_: (h, 0, 0)),
            ],
        ),
        out_shape=[
            jax.ShapeDtypeStruct((tokens, width), jnp.bfloat16),
            jax.ShapeDtypeStruct((tokens, width), jnp.bfloat16),
            jax.ShapeDtypeStruct((heads, 8, tokens), jnp.float32),
        ],
        cost_estimate=pl.CostEstimate(
            flops=4 * heads * tokens * (keys + near) * 128,
            transcendentals=heads * tokens * (keys + near),
            bytes_accessed=8 * tokens * width,
        ),
        name="attend_forward",
    )(start, q_lin, cosine, sine, prompt_kv, prompt_kv, cont_kv, cont_kv)


def attend_backward_body(
    group, prompt_rows, cont_len, chunk, pos_ref, q_ref, do_ref, out_ref, log_ref, cos_ref, sin_ref,
    kcos_ref, ksin_ref, kp_ref, vp_ref, kc_ref, vc_ref,
    dq_ref, dkp_ref, dvp_ref, dkc_ref, dvc_ref, dk_acc, dv_acc,
):
    head, key_half, swap = head_place(group)
    tokens = q_ref.shape[0]
    keys = kp_ref.shape[0]
    near = kc_ref.shape[0]
    nt = (((1,), (1,)), ((), ()))
    tn = (((0,), (0,)), ((), ()))

    @pl.when(head % (2 * group) == 0)
    def _():
        dk_acc[...] = jnp.zeros_like(dk_acc)
        dv_acc[...] = jnp.zeros_like(dv_acc)

    query = to_key_half(q_ref[...].astype(jnp.float32), swap, key_half) * ATT_SCALE
    query = query.astype(jnp.bfloat16)
    d_out = to_key_half(do_ref[...].astype(jnp.float32), swap, key_half)
    result = to_key_half(out_ref[...].astype(jnp.float32), swap, key_half)
    centre = jnp.transpose(
        jnp.broadcast_to(jnp.sum(d_out * result, axis=1, keepdims=True), (tokens, 128))
    )[:1]
    d_out = d_out.astype(jnp.bfloat16)
    log_total = log_ref[0][:1]
    row = lax.broadcasted_iota(jnp.int32, (1, tokens), 1)
    limit = jnp.where(row < prompt_rows, row + pos_ref[0], keys)

    def step(key, value, query, d_out, log_total, centre, allowed, at, count):
        scores = lax.dot_general(key, query, nt, preferred_element_type=jnp.float32)
        scores = jnp.where(allowed(scores.shape), scores, NEG)
        weights = jnp.exp2(scores * LOG2E - log_total * LOG2E)
        d_weights = lax.dot_general(value, d_out, nt, preferred_element_type=jnp.float32)
        d_scores = (weights * (d_weights - centre)).astype(jnp.bfloat16)
        dv_acc[at : at + count] += jnp.dot(
            weights.astype(jnp.bfloat16), d_out, preferred_element_type=jnp.float32
        )
        dk_acc[at : at + count] += jnp.dot(d_scores, query, preferred_element_type=jnp.float32)
        return lax.dot_general(d_scores, key, tn, preferred_element_type=jnp.float32)

    d_query = jnp.zeros((tokens, 128), jnp.float32)
    for at in range(0, keys, chunk):

        def seen(shape, at=at):
            return lax.broadcasted_iota(jnp.int32, shape, 0) + at <= limit

        d_query = d_query + step(
            kp_ref[at : at + chunk], vp_ref[at : at + chunk], query, d_out, log_total, centre, seen,
            at, chunk,
        )

    def nearby(shape):
        key_at = lax.broadcasted_iota(jnp.int32, shape, 0)
        query_at = lax.broadcasted_iota(jnp.int32, shape, 1)
        return (key_at <= query_at) & (key_at // cont_len == query_at // cont_len)

    tail = step(
        kc_ref[...], vc_ref[...], query[prompt_rows:], d_out[prompt_rows:],
        log_total[:, prompt_rows:], centre[:, prompt_rows:], nearby, keys, near,
    )
    d_query = jnp.concatenate([d_query[:prompt_rows], d_query[prompt_rows:] + tail], axis=0)
    d_query = jnp.where(lane_half(d_query.shape) == key_half, d_query * ATT_SCALE, 0.0)
    d_query = jnp.where(swap, pltpu.roll(d_query, HEAD_SIZE, 1), d_query)
    d_query = turn(d_query, cos_ref[...], -sin_ref[...]).astype(jnp.bfloat16)

    @pl.when(head % 2 == 0)
    def _():
        dq_ref[...] = d_query

    @pl.when(head % 2 == 1)
    def _():
        dq_ref[...] = dq_ref[...] + d_query

    @pl.when(head % (2 * group) == 2 * group - 1)
    def _():
        dk = turn(dk_acc[...], kcos_ref[...], -ksin_ref[...]).astype(jnp.bfloat16)
        dv = dv_acc[...].astype(jnp.bfloat16)
        dkp_ref[...] = dk[:keys]
        dkc_ref[...] = dk[keys:]
        dvp_ref[...] = dv[:keys]
        dvc_ref[...] = dv[keys:]


def attend_backward(
    query, d_out, result, log_total, prompt_kv, cont_kv, cosine, sine,
    key_cosine, key_sine, start, rows, cont_len,
):
    tokens, width = query.shape
    heads = width // HEAD_SIZE
    key_width = prompt_kv.shape[2]
    group = heads // (key_width // HEAD_SIZE)
    keys, near = prompt_kv.shape[1], cont_kv.shape[1]
    chunk = min(256, keys)
    tile = lambda h, *_: (0, h // 2)
    key_tile = lambda h, *_: (0, h // (2 * group))
    same = lambda h, *_: (0, 0)
    return pl.pallas_call(
        partial(attend_backward_body, group, rows, cont_len, chunk),
        grid_spec=pltpu.PrefetchScalarGridSpec(
            num_scalar_prefetch=1,
            grid=(heads,),
            in_specs=[
                pl.BlockSpec((tokens, 128), tile),
                pl.BlockSpec((tokens, 128), tile),
                pl.BlockSpec((tokens, 128), tile),
                pl.BlockSpec((1, 8, tokens), lambda h, *_: (h, 0, 0)),
                pl.BlockSpec((tokens, 128), same),
                pl.BlockSpec((tokens, 128), same),
                pl.BlockSpec((keys + near, 128), same),
                pl.BlockSpec((keys + near, 128), same),
                pl.BlockSpec((None, keys, 128), lambda h, *_: (0, 0, h // (2 * group))),
                pl.BlockSpec((None, keys, 128), lambda h, *_: (1, 0, h // (2 * group))),
                pl.BlockSpec((None, near, 128), lambda h, *_: (0, 0, h // (2 * group))),
                pl.BlockSpec((None, near, 128), lambda h, *_: (1, 0, h // (2 * group))),
            ],
            out_specs=[
                pl.BlockSpec((tokens, 128), tile),
                pl.BlockSpec((keys, 128), key_tile),
                pl.BlockSpec((keys, 128), key_tile),
                pl.BlockSpec((near, 128), key_tile),
                pl.BlockSpec((near, 128), key_tile),
            ],
            scratch_shapes=[
                pltpu.VMEM((keys + near, 128), jnp.float32),
                pltpu.VMEM((keys + near, 128), jnp.float32),
            ],
        ),
        out_shape=[
            jax.ShapeDtypeStruct((tokens, width), jnp.bfloat16),
            jax.ShapeDtypeStruct((keys, key_width), jnp.bfloat16),
            jax.ShapeDtypeStruct((keys, key_width), jnp.bfloat16),
            jax.ShapeDtypeStruct((near, key_width), jnp.bfloat16),
            jax.ShapeDtypeStruct((near, key_width), jnp.bfloat16),
        ],
        cost_estimate=pl.CostEstimate(
            flops=10 * heads * tokens * (keys + near) * 128,
            transcendentals=heads * tokens * (keys + near),
            bytes_accessed=8 * tokens * width,
        ),
        name="attend_backward",
    )(
        start, query, d_out, result, log_total, cosine, sine, key_cosine, key_sine, prompt_kv,
        prompt_kv, cont_kv, cont_kv,
    )


def reduce_experts(grad, split):
    axes = ("dp", "ctx") if split == 1 else "dp"
    return lax.psum_scatter(grad, axes, scatter_dimension=1, tiled=True)


def send_experts(part, split):
    size = lax.axis_size("ctx")
    if split == 1:
        return (part,)
    if size & (size - 1):
        return (lax.all_to_all(part, "ctx", split_axis=1, concat_axis=0, tiled=True),)
    own, rows, width = part.shape
    here = lax.axis_index("ctx")
    part = part.reshape(own, size, rows // size, width)
    pieces = [lax.dynamic_index_in_dim(part, here ^ step, 1, keepdims=False) for step in range(size)]
    return tuple(swap(piece, "ctx", step) if step else piece for step, piece in enumerate(pieces))


def pairs_experts(part, split):
    if split != 4:
        return part, ()
    own, rows, width = part.shape
    part = part.reshape(own, 2, 2, rows // 4, width)
    pair = lax.axis_index("ctx") // 2
    take = partial(lax.dynamic_index_in_dim, axis=1, keepdims=False)
    return take(part, pair), swap(take(part, 1 - pair), "ctx", 2)


def cores_experts(kept, moved, split):
    if split != 4:
        return send_experts(kept, split)
    core = lax.axis_index("ctx") % 2
    take = partial(lax.dynamic_index_in_dim, axis=1, keepdims=False)
    crossed = swap(jnp.stack([take(kept, 1 - core), take(moved, 1 - core)]), "ctx", 1)
    return take(kept, core), crossed[0], take(moved, core), crossed[1]


def place_experts(whole, pieces, column):
    here = lax.axis_index("ctx")
    own = pieces[0].shape[0]
    for step, piece in enumerate(pieces):
        first = (here ^ step) * own if len(pieces) > 1 else 0
        whole = lax.dynamic_update_slice(whole, piece.astype(jnp.float32), (first, 0, column))
    return whole


def scatter_keys(d_key, d_value, rows):
    size = lax.axis_size("ctx")
    here = lax.axis_index("ctx")

    def share(owner):
        return jnp.concatenate(
            [
                lax.dynamic_slice_in_dim(d_key, owner * rows, rows, axis=0),
                lax.dynamic_slice_in_dim(d_value, owner * rows, rows, axis=0),
            ],
            axis=1,
        )

    total = share(here).astype(jnp.float32)
    for hop in range(1, size):
        moved = lax.ppermute(
            share((here + hop) % size), "ctx", [(i, (i + hop) % size) for i in range(size)]
        )
        total = total + moved.astype(jnp.float32)
    total = total.astype(jnp.bfloat16)
    return (total[:, : d_key.shape[1]], total[:, d_key.shape[1] :])


def folds(grad):
    return paired(("ctx", "expert")) and grad.shape[0] % (64 * lax.axis_size("dp")) == 0


def fold_one(grad):
    if not folds(grad):
        return lax.psum_scatter(grad, ("dp", "ctx"), scatter_dimension=0, tiled=True)
    rows, width = grad.shape
    parts = lax.axis_size("dp")
    core = lax.axis_index("ctx") % 2
    take = partial(lax.dynamic_index_in_dim, axis=2, keepdims=False)
    grad = grad.reshape(parts, 2, 2, 2, rows // (8 * parts), width)
    return added(take(grad, core), swap(take(grad, 1 - core), "ctx", 1))


def fold_two(one, cut):
    if one.ndim == 2:
        return one, ()
    pair = lax.axis_index("ctx") // 2
    side = lax.axis_index("expert")
    take = partial(lax.dynamic_index_in_dim, keepdims=False)
    left, right = one[..., :cut], one[..., cut:]
    moved = swap(take(left, 1 - pair, 1), "ctx", 2), swap(take(right, 1 - side, 2), "expert", 1)
    return (take(left, pair, 1), take(right, side, 2)), moved


def fold_three(kept, moved):
    if not moved:
        return kept
    pair = lax.axis_index("ctx") // 2
    side = lax.axis_index("expert")
    take = partial(lax.dynamic_index_in_dim, keepdims=False)
    left, right = added(kept[0], moved[0]), added(kept[1], moved[1])
    left_sent = swap(take(left, 1 - side, 1), "expert", 1)
    right_sent = swap(take(right, 1 - pair, 1), "ctx", 2)
    whole = jnp.concatenate(
        [added(take(left, side, 1), left_sent), added(take(right, pair, 1), right_sent)], axis=-1
    )
    return whole


def scatter_parts(parts):
    size = lax.axis_size("dp")
    here = lax.axis_index("dp")
    take = partial(lax.dynamic_index_in_dim, axis=0, keepdims=False)
    total = take(parts, here).astype(jnp.float32)
    for hop in range(1, size):
        moved = lax.ppermute(
            take(parts, (here + hop) % size), "dp", [(i, (i + hop) % size) for i in range(size)]
        )
        total = total + moved.astype(jnp.float32)
    return total.astype(jnp.bfloat16)


def finish_dense(grad):
    if grad.ndim == 2:
        return lax.psum(grad, "expert").astype(jnp.float32)
    grad = scatter_parts(grad)
    other = swap(grad, "expert", 1)
    first = lax.axis_index("expert") == 0
    return jnp.concatenate(
        [jnp.where(first, grad, other), jnp.where(first, other, grad)], axis=0
    ).astype(jnp.float32)


def per_device(
    x_prompt,
    x_cont,
    norm1_gain,
    w_query,
    key_weight,
    value_weight,
    w_out,
    norm2_gain,
    w_router,
    w_gate_up,
    w_down,
    routes_prompt,
    routes_cont,
    slot_order,
    dy_prompt,
    dy_cont,
):
    model_width = x_prompt.shape[2]
    prompt_rows = x_prompt.shape[1]
    cont_count = x_cont.shape[1]
    cont_len = x_cont.shape[2]
    cont_rows = cont_count * cont_len
    count_of_tokens = prompt_rows + cont_rows
    key_value_width = KEY_VALUE_HEADS * HEAD_SIZE
    local_experts = w_gate_up.shape[0]
    expert_groups = lax.axis_size("expert")
    expert_total = local_experts * expert_groups
    top_count = routes_prompt.shape[2]
    capacity = (count_of_tokens * top_count + expert_total - 1) // expert_total
    hidden_units = w_down.shape[1]
    prompt_total = prompt_rows * lax.axis_size("ctx")
    count_of_keys = prompt_total + cont_rows
    split = lax.axis_size("ctx") if local_experts % lax.axis_size("ctx") == 0 else 1
    own = local_experts // split
    blocks = split * expert_groups
    slots = -(-capacity // 8) * 8
    group = ("ctx", "expert") if split > 1 else ("expert",)
    block_index = lax.axis_index(group)
    own_offset = lax.axis_index("ctx") * own if split > 1 else 0
    first_expert = lax.axis_index("expert") * local_experts + own_offset
    gate_up_own = w_gate_up
    down_own = w_down
    if split > 1:
        gate_up_own = lax.dynamic_slice_in_dim(w_gate_up, own_offset, own, axis=0)
        down_own = lax.dynamic_slice_in_dim(w_down, own_offset, own, axis=0)
    routes = jnp.concatenate(
        [routes_prompt[0], routes_cont[0].reshape(cont_rows, top_count)], axis=0
    )
    codes = slot_codes(routes, slot_order[0, 0], expert_total, capacity)
    upstream_low = jnp.concatenate([dy_prompt[0], dy_cont[0].reshape(cont_rows, model_width)], axis=0)
    upstream = upstream_low.astype(jnp.float32)
    assert capacity <= 256
    fold = model_width // count_of_tokens
    code_rows = -(-expert_total // (8 * fold)) * 8
    code_table = jnp.pad(
        codes.astype(jnp.bfloat16),
        ((0, code_rows * fold - expert_total), (0, 0)),
        constant_values=-2.0,
    )
    code_table = jnp.concatenate(
        [code_table[i * code_rows : (i + 1) * code_rows] for i in range(fold)], axis=1
    )
    upstream_all = lax.all_gather(
        jnp.concatenate([upstream_low, code_table], axis=0), group, axis=0, tiled=False
    )
    codes_all = upstream_all[:, count_of_tokens:]
    codes_all = jnp.concatenate(
        [
            codes_all[:, :, i * count_of_tokens : (i + 1) * count_of_tokens] for i in range(fold)
        ],
        axis=1,
    ).astype(jnp.float32)
    own_codes = lax.dynamic_slice_in_dim(codes_all, first_expert, own, axis=1)
    own_codes = jnp.pad(own_codes, ((0, 0), (0, -own % 8), (0, 0)), constant_values=-2.0)
    d_slot_rows = dispatch(own_codes, upstream_all, own, slots)
    d_plain = jnp.einsum("ecd,efd->ecf", d_slot_rows, down_own, preferred_element_type=jnp.float32)
    gain_one = norm1_gain.astype(jnp.float32)
    gain_two = norm2_gain.astype(jnp.float32)
    tokens = jnp.concatenate(
        [x_prompt[0], x_cont[0].reshape(cont_rows, model_width)], axis=0
    ).astype(jnp.float32)
    normed_one, scale_one = rms_forward(tokens, gain_one)
    h1_low = normed_one.astype(jnp.bfloat16)
    row_index = jnp.arange(count_of_tokens, dtype=jnp.int32)
    cont_offset = row_index - prompt_rows
    start = lax.axis_index("ctx") * prompt_rows
    query_pos = jnp.where(
        cont_offset >= 0, prompt_total + cont_offset % cont_len, start + row_index
    )
    key_index = jnp.arange(count_of_keys, dtype=jnp.int32)
    key_pos = jnp.where(
        key_index >= prompt_total, prompt_total + (key_index - prompt_total) % cont_len, key_index
    )
    start = start.astype(jnp.int32)[None]
    cosine, sine = signed_tables(query_pos.astype(jnp.float32))
    key_cosine, key_sine = signed_tables(key_pos.astype(jnp.float32))
    near_kv, cont_kv = project_keys(
        h1_low, key_weight, value_weight, cosine, sine, prompt_rows
    )
    near_kv, h1_late = lax.optimization_barrier((near_kv, h1_low))
    prompt_kv, q_lin = gather_keys(
        near_kv, jnp.dot(h1_late, w_query, preferred_element_type=jnp.float32)
    )
    query_row_block, merged_low, log_total = attend_forward(
        q_lin, prompt_kv, cont_kv, cosine, sine, start, prompt_rows, cont_len
    )
    branch = jnp.dot(merged_low, w_out, preferred_element_type=jnp.float32)
    resid = tokens + RESID * branch
    normed_two, scale_two = rms_forward(resid, gain_two)
    h2_low = normed_two.astype(jnp.bfloat16)
    rows_all = lax.all_gather(h2_low, group, axis=0, tiled=False)
    named = codes > -1.5
    logits = jnp.einsum("td,de->et", h2_low, w_router, preferred_element_type=jnp.float32)
    logits = jnp.where(named, logits, NEG)
    lifted = jnp.where(named, jnp.exp(logits - jnp.max(logits, axis=0, keepdims=True)), 0.0)
    gates = lifted / jnp.sum(lifted, axis=0, keepdims=True)
    own_gates, rows_all, d_plain = lax.optimization_barrier(
        (gather_gates(gates, group, first_expert, own), rows_all, d_plain)
    )
    slot_rows = dispatch(own_codes, rows_all, own, slots)
    slot_index = jnp.arange(slots, dtype=jnp.int32).astype(jnp.float32)
    picked = own_codes[:, :own, None, :] == slot_index[None, None, :, None]
    slot_gate = jnp.sum(jnp.where(picked, own_gates[:, :, None, :], 0.0), axis=-1)
    slot_gate = slot_gate.transpose(1, 0, 2).reshape(own, blocks * slots)
    weighted, d_both, d_slot_gate = experts(
        own_offset, slot_rows, w_gate_up, d_plain, RESID * slot_gate[:, :, None]
    )
    d_slot_gate = RESID * d_slot_gate[:, :, 0]
    grad_down = jnp.einsum(
        "ecf,ecd->efd", weighted, d_slot_rows, preferred_element_type=jnp.float32
    ).astype(jnp.bfloat16)
    d_both, _, d_slot_gate = lax.optimization_barrier(
        (d_both, grad_down, d_slot_gate)
    )
    down_part = reduce_experts(grad_down, split)
    d_gates_own = jnp.sum(
        jnp.where(
            picked,
            d_slot_gate.reshape(own, blocks, slots).transpose(1, 0, 2)[..., None],
            0.0,
        ),
        axis=2,
    )
    d_gates = return_gates(d_gates_own, group, first_expert, expert_total)
    d_slots = jnp.einsum(
        "ecf,edf->ecd", d_both, gate_up_own, preferred_element_type=jnp.float32
    ).astype(jnp.bfloat16)
    far, d_gates, slot_rows = lax.optimization_barrier(
        (far_sum(own_codes, d_slots, own, slots, group), d_gates, slot_rows)
    )
    sent = cross(far)

    def expert_gradient(slot_rows, d_part):
        return jnp.einsum(
            "ecd,ecf->edf", slot_rows, d_part, preferred_element_type=jnp.float32
        ).astype(jnp.bfloat16)

    sent, grad_gate = lax.optimization_barrier(
        (sent, expert_gradient(slot_rows, d_both[..., :hidden_units]))
    )
    gate_part = reduce_experts(grad_gate, split)
    part, weighted, slot_rows = lax.optimization_barrier(
        (scatter_one(own_codes, d_slots, own, slots, group, sent), weighted, slot_rows)
    )
    kept, moved = scatter_two(part)
    expert_out = jnp.einsum(
        "ecf,efd->ecd", weighted, down_own, preferred_element_type=jnp.float32
    ).astype(jnp.bfloat16)
    far, slot_rows = lax.optimization_barrier(
        (far_sum(own_codes, expert_out, own, slots, group), slot_rows)
    )
    moved, sent, grad_up, expert_out = lax.optimization_barrier(
        (moved, cross(far), expert_gradient(slot_rows, d_both[..., hidden_units:]), expert_out)
    )
    up_part = reduce_experts(grad_up, split)
    kept, moved = scatter_three(kept, moved)
    moved, mixed_part = lax.optimization_barrier(
        (moved, scatter_one(own_codes, expert_out, own, slots, group, sent))
    )
    d_rows = scatter_end(kept, moved)
    d_logits = (
        gates * (d_gates - jnp.sum(gates * d_gates, axis=0, keepdims=True))
    ).astype(jnp.bfloat16)
    grad_router = jnp.einsum("td,et->de", h2_low, d_logits, preferred_element_type=jnp.float32)
    d_normed_two = d_rows + jnp.einsum(
        "et,de->td", d_logits, w_router, preferred_element_type=jnp.float32
    )
    d_resid_norm, grad_norm2 = rms_backward(resid, scale_two, gain_two, d_normed_two)
    d_resid = upstream + d_resid_norm
    d_branch = (RESID * d_resid).astype(jnp.bfloat16)
    grad_out = jnp.einsum(
        "tq,td->qd", merged_low, d_branch, preferred_element_type=jnp.float32
    ).astype(jnp.bfloat16)
    out_cut = grad_out.shape[1] // 256 * 128
    grad_out = fold_one(grad_out)
    merged_gradient = jnp.einsum(
        "td,qd->tq", d_branch, w_out, preferred_element_type=jnp.float32
    ).astype(jnp.bfloat16)
    grad_out, mixed_part, down_part, merged_gradient = lax.optimization_barrier(
        (grad_out, mixed_part, down_part, merged_gradient)
    )
    mixed_kept, mixed_moved = scatter_two(mixed_part)
    out_kept, out_moved = fold_two(grad_out, out_cut)
    down_kept, down_moved = pairs_experts(down_part, split)
    d_query_low, d_key_prompt, d_value_prompt, d_key_cont, d_value_cont = attend_backward(
        query_row_block, merged_gradient, merged_low, log_total, prompt_kv, cont_kv, cosine, sine,
        key_cosine, key_sine, start, prompt_rows, cont_len,
    )
    mixed_moved, out_moved, down_moved, d_key_prompt = lax.optimization_barrier(
        (mixed_moved, out_moved, down_moved, d_key_prompt)
    )
    mixed_kept, mixed_moved = scatter_three(mixed_kept, mixed_moved)
    grad_out = fold_three(out_kept, out_moved)
    mixed = scatter_end(mixed_kept, mixed_moved)
    output = resid + mixed
    y_prompt = output[:prompt_rows].astype(jnp.bfloat16)[None]
    y_cont = output[prompt_rows:].reshape(1, cont_count, cont_len, model_width).astype(jnp.bfloat16)
    d_key_prompt, d_value_prompt = scatter_keys(d_key_prompt, d_value_prompt, prompt_rows)
    d_key_low = jnp.concatenate([d_key_prompt, d_key_cont], axis=0)
    d_value_low = jnp.concatenate([d_value_prompt, d_value_cont], axis=0)
    grad_query = jnp.einsum("td,tq->dq", h1_low, d_query_low, preferred_element_type=jnp.float32)
    grad_key = jnp.einsum("td,tq->dq", h1_low, d_key_low, preferred_element_type=jnp.float32)
    grad_value = jnp.einsum("td,tq->dq", h1_low, d_value_low, preferred_element_type=jnp.float32)
    d_normed_one = jnp.einsum("tq,dq->td", d_query_low, w_query, preferred_element_type=jnp.float32)
    d_normed_one = d_normed_one + jnp.einsum(
        "tq,dq->td", d_key_low, key_weight, preferred_element_type=jnp.float32
    )
    d_normed_one = d_normed_one + jnp.einsum(
        "tq,dq->td", d_value_low, value_weight, preferred_element_type=jnp.float32
    )
    d_tokens_norm, grad_norm1 = rms_backward(tokens, scale_one, gain_one, d_normed_one)
    d_tokens = d_resid + d_tokens_norm
    dx_prompt = d_tokens[:prompt_rows][None]
    dx_cont = d_tokens[prompt_rows:].reshape(1, cont_count, cont_len, model_width)
    small = jnp.concatenate([grad_router, grad_norm1[:, None], grad_norm2[:, None]], axis=1)
    small = jnp.pad(small, ((0, 0), (0, -small.shape[1] % 128)))
    dense = jnp.concatenate([grad_query, grad_key, grad_value, small], axis=1).astype(jnp.bfloat16)
    heads_width = QUERY_HEADS * HEAD_SIZE
    edge = heads_width + 2 * key_value_width
    gate_part, dense = lax.optimization_barrier((gate_part, dense))
    gate_kept, gate_moved = pairs_experts(gate_part, split)
    dense = fold_three(*fold_two(fold_one(dense), edge // 256 * 128))
    dense, gate_moved = lax.optimization_barrier((dense, gate_moved))
    shares = lax.axis_size("dp") * lax.axis_size("ctx")
    grad_down = place_experts(
        jnp.zeros((local_experts, hidden_units // shares, model_width), jnp.float32),
        cores_experts(down_kept, down_moved, split),
        0,
    )
    grad_gate_up = place_experts(
        jnp.zeros((local_experts, model_width // shares, 2 * hidden_units), jnp.float32),
        cores_experts(gate_kept, gate_moved, split),
        0,
    )
    dense = finish_dense(jnp.concatenate([dense, grad_out], axis=-1))
    tail = edge + small.shape[1]
    dense, up_part, grad_gate_up = lax.optimization_barrier((dense, up_part, grad_gate_up))
    grad_gate_up = place_experts(grad_gate_up, send_experts(up_part, split), hidden_units)
    return (
        y_prompt,
        y_cont,
        dx_prompt,
        dx_cont,
        dense[:, edge + expert_total],
        dense[:, :heads_width],
        dense[:, heads_width : heads_width + key_value_width],
        dense[:, heads_width + key_value_width : edge],
        dense[:, tail:],
        dense[:, edge + expert_total + 1],
        dense[:, edge : edge + expert_total],
        grad_gate_up,
        grad_down,
    )


def solution(mesh):
    return jax.shard_map(
        per_device,
        mesh=mesh,
        in_specs=(
            P(("dp", "expert"), "ctx", None),
            P(("dp", "expert"), "ctx", None, None),
            P(),
            P(),
            P(),
            P(),
            P(),
            P(),
            P(),
            P("expert", None, None),
            P("expert", None, None),
            P(("dp", "expert"), "ctx", None),
            P(("dp", "expert"), "ctx", None, None),
            P(("dp", "expert"), "ctx", None),
            P(("dp", "expert"), "ctx", None),
            P(("dp", "expert"), "ctx", None, None),
        ),
        out_specs=(
            P(("dp", "expert"), "ctx", None),
            P(("dp", "expert"), "ctx", None, None),
            P(("dp", "expert"), "ctx", None),
            P(("dp", "expert"), "ctx", None, None),
            P(("dp", "ctx")),
            P(("dp", "ctx"), None),
            P(("dp", "ctx"), None),
            P(("dp", "ctx"), None),
            P(("dp", "ctx"), None),
            P(("dp", "ctx")),
            P(("dp", "ctx"), None),
            P("expert", ("dp", "ctx"), None),
            P("expert", ("dp", "ctx"), None),
        ),
        check_vma=False,
    )
```

```python
from functools import partial

import jax
import jax.numpy as jnp
from jax import lax
from jax.experimental import pallas as pl
from jax.experimental.pallas import tpu as pltpu
from jax.sharding import PartitionSpec as P

QUERY_HEADS = 24
KEY_VALUE_HEADS = 8
HEAD_SIZE = 64


EPS = 1e-06
RESID = 0.22
ATT_SCALE = 0.015625
THETA = 10000.0
NEG = -1e30
LOG2E = 1.4426950408889634


def signed_tables(positions):
    lane = jnp.arange(2 * HEAD_SIZE, dtype=jnp.int32) % HEAD_SIZE
    half_dim = HEAD_SIZE // 2
    frequency = THETA ** (-((lane % half_dim).astype(jnp.float32) * 2.0 / HEAD_SIZE))
    angles = positions[:, None] * frequency[None, :]
    return (jnp.cos(angles), jnp.where(lane < half_dim, -1.0, 1.0) * jnp.sin(angles))


def rms_forward(values, norm_gain):
    inverse = lax.rsqrt(jnp.mean(values * values, axis=-1, keepdims=True) + EPS)
    return (values * inverse * norm_gain, inverse)


def rms_backward(values, inverse, norm_gain, upstream):
    normed = values * inverse
    weighted = upstream * norm_gain
    projected = jnp.mean(weighted * normed, axis=-1, keepdims=True)
    return (inverse * (weighted - normed * projected), jnp.sum(upstream * normed, axis=0))


def slot_codes(routes, visit_order, experts, capacity):
    count = routes.shape[0]
    ids = jnp.arange(count, dtype=jnp.int32)
    visit = jnp.arange(count, dtype=jnp.float32)
    place = (visit_order[:, None] == ids[None, :]).astype(jnp.float32)
    place_row = jnp.sum(place * visit[:, None], axis=0)
    place_col = jnp.sum((visit_order[None, :] == ids[:, None]).astype(jnp.float32) * visit[None, :], axis=1)
    earlier = (place_col[:, None] < place_row[None, :]).astype(jnp.bfloat16)
    named = jnp.any(
        routes.T[None, :, :] == jnp.arange(experts, dtype=jnp.int32)[:, None, None], axis=1
    )
    rank = jnp.dot(named.astype(jnp.bfloat16), earlier, preferred_element_type=jnp.float32)
    return jnp.where(named, jnp.where(rank < capacity, rank, -1.0), -2.0)


def selection(codes, own, slots):
    tokens = codes.shape[-1]
    slot_index = lax.broadcasted_iota(jnp.int32, (slots, tokens), 0).astype(jnp.float32)
    picks = [
        jnp.where(codes[e : e + 1, :] == slot_index, 1.0, 0.0).astype(jnp.bfloat16)
        for e in range(own)
    ]
    return jnp.concatenate(picks, axis=0)


def dispatch_body(own, slots, codes_ref, rows_ref, out_ref):
    pick = selection(codes_ref[0], own, slots)
    moved = jnp.dot(pick, rows_ref[0], preferred_element_type=jnp.float32).astype(jnp.bfloat16)
    for e in range(own):
        out_ref[e] = moved[e * slots : (e + 1) * slots]


def dispatch(codes, rows, own, slots):
    blocks, _, width = rows.shape
    tokens = codes.shape[2]
    return pl.pallas_call(
        partial(dispatch_body, own, slots),
        grid=(blocks,),
        in_specs=[
            pl.BlockSpec((1, codes.shape[1], tokens), lambda b: (b, 0, 0)),
            pl.BlockSpec((1, tokens, width), lambda b: (b, 0, 0)),
        ],
        out_specs=pl.BlockSpec((own, slots, width), lambda b: (0, b, 0)),
        out_shape=jax.ShapeDtypeStruct((own, blocks * slots, width), jnp.bfloat16),
        cost_estimate=pl.CostEstimate(
            flops=2 * blocks * own * slots * tokens * width,
            transcendentals=0,
            bytes_accessed=2 * blocks * (tokens + own * slots) * width,
        ),
        name="dispatch",
    )(codes, rows)


def experts_body(at_ref, rows_ref, gate_up_ref, plain_ref, weight_ref, out_ref, both_ref, d_weight_ref):
    total = rows_ref.shape[1]
    hidden_units = plain_ref.shape[2]
    chunk = total // 2 if total % 16 == 0 else total
    for at in range(0, total, chunk):
        rows = pl.ds(at, chunk)
        both = jnp.dot(rows_ref[0, rows], gate_up_ref[0], preferred_element_type=jnp.float32)
        gate, up = both[:, :hidden_units], both[:, hidden_units:]
        plain, weight = plain_ref[0, rows], weight_ref[0, rows]
        logistic = jax.nn.sigmoid(gate)
        silu = gate * logistic
        hidden = silu * up
        d_weight_ref[0, rows] = jnp.sum(hidden * plain, axis=1, keepdims=True)
        out_ref[0, rows] = (weight * hidden).astype(jnp.bfloat16)
        d_hidden = weight * plain
        d_gate = d_hidden * up * (logistic + silu * (1.0 - logistic))
        both_ref[0, rows, :hidden_units] = d_gate.astype(jnp.bfloat16)
        both_ref[0, rows, hidden_units:] = (d_hidden * silu).astype(jnp.bfloat16)


def experts(offset, rows, gate_up, plain, weight):
    own, total, width = rows.shape
    hidden_units = plain.shape[2]
    part = total // 2 if total % 32 == 0 else total
    tile = lambda e, r, at: (e, r, 0)
    return pl.pallas_call(
        experts_body,
        grid_spec=pltpu.PrefetchScalarGridSpec(
            num_scalar_prefetch=1,
            grid=(own, total // part),
            in_specs=[
                pl.BlockSpec((1, part, width), tile),
                pl.BlockSpec((1, width, 2 * hidden_units), lambda e, r, at: (at[0] + e, 0, 0)),
                pl.BlockSpec((1, part, hidden_units), tile),
                pl.BlockSpec((1, part, 1), tile),
            ],
            out_specs=[
                pl.BlockSpec((1, part, hidden_units), tile),
                pl.BlockSpec((1, part, 2 * hidden_units), tile),
                pl.BlockSpec((1, part, 1), tile),
            ],
        ),
        out_shape=[
            jax.ShapeDtypeStruct((own, total, hidden_units), jnp.bfloat16),
            jax.ShapeDtypeStruct((own, total, 2 * hidden_units), jnp.bfloat16),
            jax.ShapeDtypeStruct((own, total, 1), jnp.float32),
        ],
        cost_estimate=pl.CostEstimate(
            flops=4 * own * total * width * hidden_units,
            transcendentals=own * total * hidden_units,
            bytes_accessed=2 * own * (total * (width + 4 * hidden_units) + 2 * width * hidden_units),
        ),
        name="experts",
    )(jnp.asarray(offset, jnp.int32).reshape(1), rows, gate_up, plain, weight)


def combine_body(own, slots, at_ref, codes_ref, rows_ref, *refs):
    out_ref = refs[-1]
    pick = selection(codes_ref[0], own, slots)
    rows = rows_ref[...].reshape(own * slots, rows_ref.shape[-1])
    total = lax.dot_general(
        pick, rows, (((0,), (0,)), ((), ())), preferred_element_type=jnp.float32
    )
    for ref in refs[:-1]:
        total = total + ref[0].astype(jnp.float32)
    out_ref[0] = total.astype(out_ref.dtype)


def combine(at, codes, rows, own, slots, *more):
    count, tokens = at.shape[0], codes.shape[2]
    width = rows.shape[-1]
    return pl.pallas_call(
        partial(combine_body, own, slots),
        grid_spec=pltpu.PrefetchScalarGridSpec(
            num_scalar_prefetch=1,
            grid=(count,),
            in_specs=[
                pl.BlockSpec((1, codes.shape[1], tokens), lambda b, at: (at[b], 0, 0)),
                pl.BlockSpec((own, slots, width), lambda b, at: (0, at[b], 0)),
            ]
            + [pl.BlockSpec((1, tokens, width), lambda b, at: (b, 0, 0)) for _ in more],
            out_specs=pl.BlockSpec((1, tokens, width), lambda b, at: (b, 0, 0)),
        ),
        out_shape=jax.ShapeDtypeStruct((count, tokens, width), jnp.bfloat16),
        cost_estimate=pl.CostEstimate(flops=1, transcendentals=0, bytes_accessed=1),
        name="combine",
    )(at, codes, rows, *more)


def swap(values, axis, bit):
    size = lax.axis_size(axis)
    return lax.ppermute(values, axis, [(i, i ^ bit) for i in range(size)])


def exchange(values, bit, axis, stride, dim):
    take = partial(lax.dynamic_index_in_dim, axis=dim, keepdims=False)
    away = swap(take(values, 1 - bit), axis, stride)
    stay = take(values, bit)
    first = bit == 0
    return jnp.stack([jnp.where(first, stay, away), jnp.where(first, away, stay)])


def paired(group):
    return group == ("ctx", "expert") and lax.axis_size("ctx") == 4 and lax.axis_size("expert") == 2


def gather_gates(gates, group, first_expert, own):
    if not paired(group):
        whole = lax.all_gather(gates, group, axis=0, tiled=False)
        return lax.dynamic_slice_in_dim(whole, first_expert, own, axis=1)
    ctx, side = lax.axis_index("ctx"), lax.axis_index("expert")
    parts = gates.reshape(2, 2, 2, own, gates.shape[1])
    parts = exchange(parts, side, "expert", 1, 0)
    parts = exchange(parts, ctx % 2, "ctx", 1, 2)
    parts = exchange(parts, ctx // 2, "ctx", 2, 2)
    return parts.reshape(8, own, gates.shape[1])


def return_gates(values, group, first_expert, experts):
    blocks, own, tokens = values.shape
    if not paired(group):
        whole = jnp.zeros((blocks, experts, tokens), values.dtype)
        whole = lax.dynamic_update_slice_in_dim(whole, values, first_expert, axis=1)
        return lax.psum_scatter(whole, group, scatter_dimension=0)
    ctx, side = lax.axis_index("ctx"), lax.axis_index("expert")
    parts = values.reshape(2, 2, 2, own, tokens)
    parts = exchange(parts, ctx // 2, "ctx", 2, 0)
    parts = exchange(parts, ctx % 2, "ctx", 1, 1)
    parts = exchange(parts, side, "expert", 1, 2)
    return parts.transpose(0, 2, 1, 3, 4).reshape(experts, tokens)


def added(left, right):
    return (left.astype(jnp.float32) + right.astype(jnp.float32)).astype(jnp.bfloat16)


def far_sum(codes, rows, own, slots, group):
    if not paired(group):
        return jnp.zeros((), jnp.bfloat16)
    far = lax.axis_index(group).astype(jnp.int32) ^ jnp.array([2, 3, 6, 7], jnp.int32)
    return combine(far, codes, rows, own, slots)


def cross(far):
    return swap(far, "ctx", 1) if far.ndim else far


def scatter_one(codes, rows, own, slots, group, sent):
    if not paired(group):
        every = jnp.arange(codes.shape[0], dtype=jnp.int32)
        return lax.psum_scatter(
            combine(every, codes, rows, own, slots), group, scatter_dimension=0
        )
    near = lax.axis_index(group).astype(jnp.int32) ^ jnp.array([0, 1, 4, 5], jnp.int32)
    return combine(near, codes, rows, own, slots, sent)


def scatter_two(part):
    if part.ndim == 2:
        return part, ()
    half = part.shape[-1] // 2
    left, right = part[:, :, :half], part[:, :, half:]
    moved = swap(left[2:], "ctx", 2), swap(jnp.stack([right[1], right[3]]), "expert", 1)
    return (left[0], left[1], right[0], right[2]), moved


def scatter_three(kept, moved):
    if not moved:
        return kept, ()
    left, left_other, right, right_other = kept
    left_sent, right_sent = moved
    onward = (
        swap(added(left_other, left_sent[1]), "expert", 1),
        swap(added(right_other, right_sent[1]), "ctx", 2),
    )
    return (left, left_sent[0], right, right_sent[0]), onward


def scatter_end(kept, moved):
    if not moved:
        return kept.astype(jnp.float32)
    wide = lambda *pieces: sum(piece.astype(jnp.float32) for piece in pieces)
    return jnp.concatenate(
        [wide(kept[0], kept[1], moved[0]), wide(kept[2], kept[3], moved[1])], axis=1
    )


def lane_half(shape):
    return lax.broadcasted_iota(jnp.int32, shape, 1) // HEAD_SIZE


def turn(values, cosine, sine):
    half_dim = HEAD_SIZE // 2
    width = values.shape[1]
    lane = lax.broadcasted_iota(jnp.int32, values.shape, 1) % HEAD_SIZE
    partner = jnp.where(
        lane < half_dim,
        pltpu.roll(values, width - half_dim, 1),
        pltpu.roll(values, half_dim, 1),
    )
    return values * cosine + partner * sine


def to_key_half(values, swap, key_half):
    moved = jnp.where(swap, pltpu.roll(values, HEAD_SIZE, 1), values)
    return jnp.where(lane_half(values.shape) == key_half, moved, 0.0)


def project_keys_body(rows, h_ref, kw_ref, vw_ref, cos_ref, sin_ref, prompt_ref, cont_ref):
    key = jnp.dot(h_ref[...], kw_ref[...], preferred_element_type=jnp.float32)
    key = turn(key, cos_ref[...], sin_ref[...]).astype(jnp.bfloat16)
    value = jnp.dot(h_ref[...], vw_ref[...], preferred_element_type=jnp.float32)
    value = value.astype(jnp.bfloat16)
    prompt_ref[0] = key[:rows]
    prompt_ref[1] = value[:rows]
    cont_ref[0] = key[rows:]
    cont_ref[1] = value[rows:]


def project_keys(hidden, key_weight, value_weight, cosine, sine, rows):
    tokens, depth = hidden.shape
    width = key_weight.shape[1]
    whole = lambda j: (0, 0)
    column = lambda j: (0, j)
    return pl.pallas_call(
        partial(project_keys_body, rows),
        grid=(width // 128,),
        in_specs=[
            pl.BlockSpec((tokens, depth), whole),
            pl.BlockSpec((depth, 128), column),
            pl.BlockSpec((depth, 128), column),
            pl.BlockSpec((tokens, 128), whole),
            pl.BlockSpec((tokens, 128), whole),
        ],
        out_specs=[
            pl.BlockSpec((2, rows, 128), lambda j: (0, 0, j)),
            pl.BlockSpec((2, tokens - rows, 128), lambda j: (0, 0, j)),
        ],
        out_shape=[
            jax.ShapeDtypeStruct((2, rows, width), jnp.bfloat16),
            jax.ShapeDtypeStruct((2, tokens - rows, width), jnp.bfloat16),
        ],
        cost_estimate=pl.CostEstimate(
            flops=4 * tokens * depth * width,
            transcendentals=0,
            bytes_accessed=2 * (tokens * depth + 2 * depth * width + 2 * tokens * width),
        ),
        name="project_keys",
    )(hidden, key_weight, value_weight, cosine, sine)


def gather_keys(near_kv, work):
    if lax.axis_size("ctx") != 4:
        return lax.all_gather(near_kv, "ctx", axis=1, tiled=True), work
    rows = near_kv.shape[1]
    here = lax.axis_index("ctx")
    pair, side, work = lax.optimization_barrier(
        (swap(near_kv, "ctx", 2), swap(near_kv, "ctx", 1), work)
    )
    whole = jnp.zeros((2, 4 * rows, near_kv.shape[2]), near_kv.dtype)
    pieces = ((0, near_kv), (2, pair), (1, side), (3, swap(pair, "ctx", 1)))
    for step, piece in pieces:
        whole = lax.dynamic_update_slice_in_dim(whole, piece, (here ^ step) * rows, axis=1)
    return whole, work


def head_place(group):
    head = pl.program_id(0)
    key_half = (head // group) % 2
    return head, key_half, (head % 2) != key_half


def attend_forward_body(
    group, prompt_rows, cont_len, pos_ref, q_ref, cos_ref, sin_ref, kp_ref, vp_ref, kc_ref, vc_ref,
    qr_ref, out_ref, log_ref,
):
    head, key_half, swap = head_place(group)
    rotated = turn(q_ref[...], cos_ref[...], sin_ref[...]).astype(jnp.bfloat16)
    qr_ref[...] = rotated
    query = to_key_half(rotated.astype(jnp.float32), swap, key_half) * ATT_SCALE
    query = query.astype(jnp.bfloat16)
    nt = (((1,), (1,)), ((), ()))

    def finish(parts, rows):
        highest = parts[0][0].max(axis=1, keepdims=True)
        for scores, _ in parts[1:]:
            highest = jnp.maximum(highest, scores.max(axis=1, keepdims=True))
        lifted = [jnp.exp2(scores * LOG2E - highest * LOG2E) for scores, _ in parts]
        total = lifted[0].sum(axis=1, keepdims=True)
        for piece in lifted[1:]:
            total = total + piece.sum(axis=1, keepdims=True)
        inverse = 1.0 / total
        result = None
        for piece, (_, value) in zip(lifted, parts):
            term = jnp.dot(
                piece.astype(jnp.bfloat16), value, preferred_element_type=jnp.float32
            )
            result = term if result is None else result + term
        log_total = jnp.broadcast_to(highest + jnp.log(total), (total.shape[0], 128))
        log_ref[0, :, rows] = jnp.transpose(log_total)[:8]
        keep = jnp.where(lane_half(result.shape) == key_half, result * inverse, 0.0)
        keep = jnp.where(swap, pltpu.roll(keep, HEAD_SIZE, 1), keep).astype(jnp.bfloat16)

        @pl.when(head % 2 == 0)
        def _():
            out_ref[rows, :] = keep

        @pl.when(head % 2 == 1)
        def _():
            out_ref[rows, :] = out_ref[rows, :] + keep

    total_rows = q_ref.shape[0]
    first = lax.dot_general(
        query[:prompt_rows], kp_ref[...], nt, preferred_element_type=jnp.float32
    )
    row = lax.broadcasted_iota(jnp.int32, first.shape, 0) + pos_ref[0]
    first = jnp.where(lax.broadcasted_iota(jnp.int32, first.shape, 1) <= row, first, NEG)
    finish([(first, vp_ref[...])], pl.ds(0, prompt_rows))
    lower = query[prompt_rows:]
    wide = lax.dot_general(lower, kp_ref[...], nt, preferred_element_type=jnp.float32)
    near = lax.dot_general(lower, kc_ref[...], nt, preferred_element_type=jnp.float32)
    row = lax.broadcasted_iota(jnp.int32, near.shape, 0)
    col = lax.broadcasted_iota(jnp.int32, near.shape, 1)
    near = jnp.where((col <= row) & (col // cont_len == row // cont_len), near, NEG)
    finish([(wide, vp_ref[...]), (near, vc_ref[...])], pl.ds(prompt_rows, total_rows - prompt_rows))


def attend_forward(q_lin, prompt_kv, cont_kv, cosine, sine, start, rows, cont_len):
    tokens, width = q_lin.shape
    heads = width // HEAD_SIZE
    group = heads // (prompt_kv.shape[2] // HEAD_SIZE)
    keys, near = prompt_kv.shape[1], cont_kv.shape[1]
    tile = lambda h, *_: (0, h // 2)
    same = lambda h, *_: (0, 0)
    return pl.pallas_call(
        partial(attend_forward_body, group, rows, cont_len),
        grid_spec=pltpu.PrefetchScalarGridSpec(
            num_scalar_prefetch=1,
            grid=(heads,),
            in_specs=[
                pl.BlockSpec((tokens, 128), tile),
                pl.BlockSpec((tokens, 128), same),
                pl.BlockSpec((tokens, 128), same),
                pl.BlockSpec((None, keys, 128), lambda h, *_: (0, 0, h // (2 * group))),
                pl.BlockSpec((None, keys, 128), lambda h, *_: (1, 0, h // (2 * group))),
                pl.BlockSpec((None, near, 128), lambda h, *_: (0, 0, h // (2 * group))),
                pl.BlockSpec((None, near, 128), lambda h, *_: (1, 0, h // (2 * group))),
            ],
            out_specs=[
                pl.BlockSpec((tokens, 128), tile),
                pl.BlockSpec((tokens, 128), tile),
                pl.BlockSpec((1, 8, tokens), lambda h, *_: (h, 0, 0)),
            ],
        ),
        out_shape=[
            jax.ShapeDtypeStruct((tokens, width), jnp.bfloat16),
            jax.ShapeDtypeStruct((tokens, width), jnp.bfloat16),
            jax.ShapeDtypeStruct((heads, 8, tokens), jnp.float32),
        ],
        cost_estimate=pl.CostEstimate(
            flops=4 * heads * tokens * (keys + near) * 128,
            transcendentals=heads * tokens * (keys + near),
            bytes_accessed=8 * tokens * width,
        ),
        name="attend_forward",
    )(start, q_lin, cosine, sine, prompt_kv, prompt_kv, cont_kv, cont_kv)


def attend_backward_body(
    group, prompt_rows, cont_len, chunk, pos_ref, q_ref, do_ref, out_ref, log_ref, cos_ref, sin_ref,
    kcos_ref, ksin_ref, kp_ref, vp_ref, kc_ref, vc_ref,
    dq_ref, dkp_ref, dvp_ref, dkc_ref, dvc_ref, dk_acc, dv_acc,
):
    head, key_half, swap = head_place(group)
    tokens = q_ref.shape[0]
    keys = kp_ref.shape[0]
    near = kc_ref.shape[0]
    nt = (((1,), (1,)), ((), ()))
    tn = (((0,), (0,)), ((), ()))

    @pl.when(head % (2 * group) == 0)
    def _():
        dk_acc[...] = jnp.zeros_like(dk_acc)
        dv_acc[...] = jnp.zeros_like(dv_acc)

    query = to_key_half(q_ref[...].astype(jnp.float32), swap, key_half) * ATT_SCALE
    query = query.astype(jnp.bfloat16)
    d_out = to_key_half(do_ref[...].astype(jnp.float32), swap, key_half)
    result = to_key_half(out_ref[...].astype(jnp.float32), swap, key_half)
    centre = jnp.transpose(
        jnp.broadcast_to(jnp.sum(d_out * result, axis=1, keepdims=True), (tokens, 128))
    )[:1]
    d_out = d_out.astype(jnp.bfloat16)
    log_total = log_ref[0][:1]
    row = lax.broadcasted_iota(jnp.int32, (1, tokens), 1)
    limit = jnp.where(row < prompt_rows, row + pos_ref[0], keys)

    def step(key, value, query, d_out, log_total, centre, allowed, at, count):
        scores = lax.dot_general(key, query, nt, preferred_element_type=jnp.float32)
        scores = jnp.where(allowed(scores.shape), scores, NEG)
        weights = jnp.exp2(scores * LOG2E - log_total * LOG2E)
        d_weights = lax.dot_general(value, d_out, nt, preferred_element_type=jnp.float32)
        d_scores = (weights * (d_weights - centre)).astype(jnp.bfloat16)
        dv_acc[at : at + count] += jnp.dot(
            weights.astype(jnp.bfloat16), d_out, preferred_element_type=jnp.float32
        )
        dk_acc[at : at + count] += jnp.dot(d_scores, query, preferred_element_type=jnp.float32)
        return lax.dot_general(d_scores, key, tn, preferred_element_type=jnp.float32)

    d_query = jnp.zeros((tokens, 128), jnp.float32)
    for at in range(0, keys, chunk):

        def seen(shape, at=at):
            return lax.broadcasted_iota(jnp.int32, shape, 0) + at <= limit

        d_query = d_query + step(
            kp_ref[at : at + chunk], vp_ref[at : at + chunk], query, d_out, log_total, centre, seen,
            at, chunk,
        )

    def nearby(shape):
        key_at = lax.broadcasted_iota(jnp.int32, shape, 0)
        query_at = lax.broadcasted_iota(jnp.int32, shape, 1)
        return (key_at <= query_at) & (key_at // cont_len == query_at // cont_len)

    tail = step(
        kc_ref[...], vc_ref[...], query[prompt_rows:], d_out[prompt_rows:],
        log_total[:, prompt_rows:], centre[:, prompt_rows:], nearby, keys, near,
    )
    d_query = jnp.concatenate([d_query[:prompt_rows], d_query[prompt_rows:] + tail], axis=0)
    d_query = jnp.where(lane_half(d_query.shape) == key_half, d_query * ATT_SCALE, 0.0)
    d_query = jnp.where(swap, pltpu.roll(d_query, HEAD_SIZE, 1), d_query)
    d_query = turn(d_query, cos_ref[...], -sin_ref[...]).astype(jnp.bfloat16)

    @pl.when(head % 2 == 0)
    def _():
        dq_ref[...] = d_query

    @pl.when(head % 2 == 1)
    def _():
        dq_ref[...] = dq_ref[...] + d_query

    @pl.when(head % (2 * group) == 2 * group - 1)
    def _():
        dk = turn(dk_acc[...], kcos_ref[...], -ksin_ref[...]).astype(jnp.bfloat16)
        dv = dv_acc[...].astype(jnp.bfloat16)
        dkp_ref[...] = dk[:keys]
        dkc_ref[...] = dk[keys:]
        dvp_ref[...] = dv[:keys]
        dvc_ref[...] = dv[keys:]


def attend_backward(
    query, d_out, result, log_total, prompt_kv, cont_kv, cosine, sine,
    key_cosine, key_sine, start, rows, cont_len,
):
    tokens, width = query.shape
    heads = width // HEAD_SIZE
    key_width = prompt_kv.shape[2]
    group = heads // (key_width // HEAD_SIZE)
    keys, near = prompt_kv.shape[1], cont_kv.shape[1]
    chunk = min(256, keys)
    tile = lambda h, *_: (0, h // 2)
    key_tile = lambda h, *_: (0, h // (2 * group))
    same = lambda h, *_: (0, 0)
    return pl.pallas_call(
        partial(attend_backward_body, group, rows, cont_len, chunk),
        grid_spec=pltpu.PrefetchScalarGridSpec(
            num_scalar_prefetch=1,
            grid=(heads,),
            in_specs=[
                pl.BlockSpec((tokens, 128), tile),
                pl.BlockSpec((tokens, 128), tile),
                pl.BlockSpec((tokens, 128), tile),
                pl.BlockSpec((1, 8, tokens), lambda h, *_: (h, 0, 0)),
                pl.BlockSpec((tokens, 128), same),
                pl.BlockSpec((tokens, 128), same),
                pl.BlockSpec((keys + near, 128), same),
                pl.BlockSpec((keys + near, 128), same),
                pl.BlockSpec((None, keys, 128), lambda h, *_: (0, 0, h // (2 * group))),
                pl.BlockSpec((None, keys, 128), lambda h, *_: (1, 0, h // (2 * group))),
                pl.BlockSpec((None, near, 128), lambda h, *_: (0, 0, h // (2 * group))),
                pl.BlockSpec((None, near, 128), lambda h, *_: (1, 0, h // (2 * group))),
            ],
            out_specs=[
                pl.BlockSpec((tokens, 128), tile),
                pl.BlockSpec((keys, 128), key_tile),
                pl.BlockSpec((keys, 128), key_tile),
                pl.BlockSpec((near, 128), key_tile),
                pl.BlockSpec((near, 128), key_tile),
            ],
            scratch_shapes=[
                pltpu.VMEM((keys + near, 128), jnp.float32),
                pltpu.VMEM((keys + near, 128), jnp.float32),
            ],
        ),
        out_shape=[
            jax.ShapeDtypeStruct((tokens, width), jnp.bfloat16),
            jax.ShapeDtypeStruct((keys, key_width), jnp.bfloat16),
            jax.ShapeDtypeStruct((keys, key_width), jnp.bfloat16),
            jax.ShapeDtypeStruct((near, key_width), jnp.bfloat16),
            jax.ShapeDtypeStruct((near, key_width), jnp.bfloat16),
        ],
        cost_estimate=pl.CostEstimate(
            flops=10 * heads * tokens * (keys + near) * 128,
            transcendentals=heads * tokens * (keys + near),
            bytes_accessed=8 * tokens * width,
        ),
        name="attend_backward",
    )(
        start, query, d_out, result, log_total, cosine, sine, key_cosine, key_sine, prompt_kv,
        prompt_kv, cont_kv, cont_kv,
    )


def reduce_experts(grad, split):
    axes = ("dp", "ctx") if split == 1 else "dp"
    return lax.psum_scatter(grad, axes, scatter_dimension=1, tiled=True)


def send_experts(part, split):
    size = lax.axis_size("ctx")
    if split == 1:
        return (part,)
    if size & (size - 1):
        return (lax.all_to_all(part, "ctx", split_axis=1, concat_axis=0, tiled=True),)
    own, rows, width = part.shape
    here = lax.axis_index("ctx")
    part = part.reshape(own, size, rows // size, width)
    pieces = [lax.dynamic_index_in_dim(part, here ^ step, 1, keepdims=False) for step in range(size)]
    return tuple(swap(piece, "ctx", step) if step else piece for step, piece in enumerate(pieces))


def pairs_experts(part, split):
    if split != 4:
        return part, ()
    own, rows, width = part.shape
    part = part.reshape(own, 2, 2, rows // 4, width)
    pair = lax.axis_index("ctx") // 2
    take = partial(lax.dynamic_index_in_dim, axis=1, keepdims=False)
    return take(part, pair), swap(take(part, 1 - pair), "ctx", 2)


def cores_experts(kept, moved, split):
    if split != 4:
        return send_experts(kept, split)
    core = lax.axis_index("ctx") % 2
    take = partial(lax.dynamic_index_in_dim, axis=1, keepdims=False)
    crossed = swap(jnp.stack([take(kept, 1 - core), take(moved, 1 - core)]), "ctx", 1)
    return take(kept, core), crossed[0], take(moved, core), crossed[1]


def place_experts(whole, pieces, column):
    here = lax.axis_index("ctx")
    own = pieces[0].shape[0]
    for step, piece in enumerate(pieces):
        first = (here ^ step) * own if len(pieces) > 1 else 0
        whole = lax.dynamic_update_slice(whole, piece.astype(jnp.float32), (first, 0, column))
    return whole


def scatter_keys(d_key, d_value, rows):
    size = lax.axis_size("ctx")
    here = lax.axis_index("ctx")

    def share(owner):
        return jnp.concatenate(
            [
                lax.dynamic_slice_in_dim(d_key, owner * rows, rows, axis=0),
                lax.dynamic_slice_in_dim(d_value, owner * rows, rows, axis=0),
            ],
            axis=1,
        )

    total = share(here).astype(jnp.float32)
    for hop in range(1, size):
        moved = lax.ppermute(
            share((here + hop) % size), "ctx", [(i, (i + hop) % size) for i in range(size)]
        )
        total = total + moved.astype(jnp.float32)
    total = total.astype(jnp.bfloat16)
    return (total[:, : d_key.shape[1]], total[:, d_key.shape[1] :])


def folds(grad):
    return paired(("ctx", "expert")) and grad.shape[0] % (64 * lax.axis_size("dp")) == 0


def fold_one(grad):
    if not folds(grad):
        return lax.psum_scatter(grad, ("dp", "ctx"), scatter_dimension=0, tiled=True)
    rows, width = grad.shape
    parts = lax.axis_size("dp")
    core = lax.axis_index("ctx") % 2
    take = partial(lax.dynamic_index_in_dim, axis=2, keepdims=False)
    grad = grad.reshape(parts, 2, 2, 2, rows // (8 * parts), width)
    return added(take(grad, core), swap(take(grad, 1 - core), "ctx", 1))


def fold_two(one, cut):
    if one.ndim == 2:
        return one, ()
    pair = lax.axis_index("ctx") // 2
    side = lax.axis_index("expert")
    take = partial(lax.dynamic_index_in_dim, keepdims=False)
    left, right = one[..., :cut], one[..., cut:]
    moved = swap(take(left, 1 - pair, 1), "ctx", 2), swap(take(right, 1 - side, 2), "expert", 1)
    return (take(left, pair, 1), take(right, side, 2)), moved


def fold_three(kept, moved):
    if not moved:
        return kept
    pair = lax.axis_index("ctx") // 2
    side = lax.axis_index("expert")
    take = partial(lax.dynamic_index_in_dim, keepdims=False)
    left, right = added(kept[0], moved[0]), added(kept[1], moved[1])
    left_sent = swap(take(left, 1 - side, 1), "expert", 1)
    right_sent = swap(take(right, 1 - pair, 1), "ctx", 2)
    whole = jnp.concatenate(
        [added(take(left, side, 1), left_sent), added(take(right, pair, 1), right_sent)], axis=-1
    )
    return whole


def scatter_parts(parts):
    size = lax.axis_size("dp")
    here = lax.axis_index("dp")
    take = partial(lax.dynamic_index_in_dim, axis=0, keepdims=False)
    total = take(parts, here).astype(jnp.float32)
    for hop in range(1, size):
        moved = lax.ppermute(
            take(parts, (here + hop) % size), "dp", [(i, (i + hop) % size) for i in range(size)]
        )
        total = total + moved.astype(jnp.float32)
    return total.astype(jnp.bfloat16)


def sum_dense(grad):
    return lax.psum(grad, "expert") if grad.ndim == 2 else scatter_parts(grad)


def finish_dense(grad, halves):
    if not halves:
        return grad.astype(jnp.float32)
    other = swap(grad, "expert", 1)
    first = lax.axis_index("expert") == 0
    return jnp.concatenate(
        [jnp.where(first, grad, other), jnp.where(first, other, grad)], axis=0
    ).astype(jnp.float32)


def per_device(
    x_prompt,
    x_cont,
    norm1_gain,
    w_query,
    key_weight,
    value_weight,
    w_out,
    norm2_gain,
    w_router,
    w_gate_up,
    w_down,
    routes_prompt,
    routes_cont,
    slot_order,
    dy_prompt,
    dy_cont,
):
    model_width = x_prompt.shape[2]
    prompt_rows = x_prompt.shape[1]
    cont_count = x_cont.shape[1]
    cont_len = x_cont.shape[2]
    cont_rows = cont_count * cont_len
    count_of_tokens = prompt_rows + cont_rows
    key_value_width = KEY_VALUE_HEADS * HEAD_SIZE
    local_experts = w_gate_up.shape[0]
    expert_groups = lax.axis_size("expert")
    expert_total = local_experts * expert_groups
    top_count = routes_prompt.shape[2]
    capacity = (count_of_tokens * top_count + expert_total - 1) // expert_total
    hidden_units = w_down.shape[1]
    prompt_total = prompt_rows * lax.axis_size("ctx")
    count_of_keys = prompt_total + cont_rows
    split = lax.axis_size("ctx") if local_experts % lax.axis_size("ctx") == 0 else 1
    own = local_experts // split
    blocks = split * expert_groups
    slots = -(-capacity // 8) * 8
    group = ("ctx", "expert") if split > 1 else ("expert",)
    block_index = lax.axis_index(group)
    own_offset = lax.axis_index("ctx") * own if split > 1 else 0
    first_expert = lax.axis_index("expert") * local_experts + own_offset
    gate_up_own = w_gate_up
    down_own = w_down
    if split > 1:
        gate_up_own = lax.dynamic_slice_in_dim(w_gate_up, own_offset, own, axis=0)
        down_own = lax.dynamic_slice_in_dim(w_down, own_offset, own, axis=0)
    routes = jnp.concatenate(
        [routes_prompt[0], routes_cont[0].reshape(cont_rows, top_count)], axis=0
    )
    codes = slot_codes(routes, slot_order[0, 0], expert_total, capacity)
    upstream_low = jnp.concatenate([dy_prompt[0], dy_cont[0].reshape(cont_rows, model_width)], axis=0)
    upstream = upstream_low.astype(jnp.float32)
    assert capacity <= 256
    fold = model_width // count_of_tokens
    code_rows = -(-expert_total // (8 * fold)) * 8
    code_table = jnp.pad(
        codes.astype(jnp.bfloat16),
        ((0, code_rows * fold - expert_total), (0, 0)),
        constant_values=-2.0,
    )
    code_table = jnp.concatenate(
        [code_table[i * code_rows : (i + 1) * code_rows] for i in range(fold)], axis=1
    )
    gain_one = norm1_gain.astype(jnp.float32)
    gain_two = norm2_gain.astype(jnp.float32)
    tokens = jnp.concatenate(
        [x_prompt[0], x_cont[0].reshape(cont_rows, model_width)], axis=0
    ).astype(jnp.float32)
    normed_one, scale_one = rms_forward(tokens, gain_one)
    h1_low = normed_one.astype(jnp.bfloat16)
    row_index = jnp.arange(count_of_tokens, dtype=jnp.int32)
    cont_offset = row_index - prompt_rows
    start = lax.axis_index("ctx") * prompt_rows
    query_pos = jnp.where(
        cont_offset >= 0, prompt_total + cont_offset % cont_len, start + row_index
    )
    key_index = jnp.arange(count_of_keys, dtype=jnp.int32)
    key_pos = jnp.where(
        key_index >= prompt_total, prompt_total + (key_index - prompt_total) % cont_len, key_index
    )
    start = start.astype(jnp.int32)[None]
    cosine, sine = signed_tables(query_pos.astype(jnp.float32))
    key_cosine, key_sine = signed_tables(key_pos.astype(jnp.float32))
    near_kv, cont_kv = project_keys(
        h1_low, key_weight, value_weight, cosine, sine, prompt_rows
    )
    near_kv, h1_late = lax.optimization_barrier((near_kv, h1_low))
    prompt_kv, q_lin = gather_keys(
        near_kv, jnp.dot(h1_late, w_query, preferred_element_type=jnp.float32)
    )
    travel = jnp.concatenate([upstream_low, code_table], axis=0)
    prompt_kv, travel = lax.optimization_barrier((prompt_kv, travel))
    upstream_all = lax.all_gather(travel, group, axis=0, tiled=False)
    codes_all = upstream_all[:, count_of_tokens:]
    codes_all = jnp.concatenate(
        [
            codes_all[:, :, i * count_of_tokens : (i + 1) * count_of_tokens] for i in range(fold)
        ],
        axis=1,
    ).astype(jnp.float32)
    own_codes = lax.dynamic_slice_in_dim(codes_all, first_expert, own, axis=1)
    own_codes = jnp.pad(own_codes, ((0, 0), (0, -own % 8), (0, 0)), constant_values=-2.0)
    d_slot_rows = dispatch(own_codes, upstream_all, own, slots)
    d_plain = jnp.einsum("ecd,efd->ecf", d_slot_rows, down_own, preferred_element_type=jnp.float32)
    query_row_block, merged_low, log_total = attend_forward(
        q_lin, prompt_kv, cont_kv, cosine, sine, start, prompt_rows, cont_len
    )
    branch = jnp.dot(merged_low, w_out, preferred_element_type=jnp.float32)
    resid = tokens + RESID * branch
    normed_two, scale_two = rms_forward(resid, gain_two)
    h2_low = normed_two.astype(jnp.bfloat16)
    rows_all = lax.all_gather(h2_low, group, axis=0, tiled=False)
    named = codes > -1.5
    logits = jnp.einsum("td,de->et", h2_low, w_router, preferred_element_type=jnp.float32)
    logits = jnp.where(named, logits, NEG)
    lifted = jnp.where(named, jnp.exp(logits - jnp.max(logits, axis=0, keepdims=True)), 0.0)
    gates = lifted / jnp.sum(lifted, axis=0, keepdims=True)
    own_gates, rows_all, d_plain = lax.optimization_barrier(
        (gather_gates(gates, group, first_expert, own), rows_all, d_plain)
    )
    slot_rows = dispatch(own_codes, rows_all, own, slots)
    slot_index = jnp.arange(slots, dtype=jnp.int32).astype(jnp.float32)
    picked = own_codes[:, :own, None, :] == slot_index[None, None, :, None]
    slot_gate = jnp.sum(jnp.where(picked, own_gates[:, :, None, :], 0.0), axis=-1)
    slot_gate = slot_gate.transpose(1, 0, 2).reshape(own, blocks * slots)
    weighted, d_both, d_slot_gate = experts(
        own_offset, slot_rows, w_gate_up, d_plain, RESID * slot_gate[:, :, None]
    )
    d_slot_gate = RESID * d_slot_gate[:, :, 0]
    grad_down = jnp.einsum(
        "ecf,ecd->efd", weighted, d_slot_rows, preferred_element_type=jnp.float32
    ).astype(jnp.bfloat16)
    d_both, _, d_slot_gate = lax.optimization_barrier(
        (d_both, grad_down, d_slot_gate)
    )
    down_part = reduce_experts(grad_down, split)
    d_gates_own = jnp.sum(
        jnp.where(
            picked,
            d_slot_gate.reshape(own, blocks, slots).transpose(1, 0, 2)[..., None],
            0.0,
        ),
        axis=2,
    )
    d_gates = return_gates(d_gates_own, group, first_expert, expert_total)
    d_slots = jnp.einsum(
        "ecf,edf->ecd", d_both, gate_up_own, preferred_element_type=jnp.float32
    ).astype(jnp.bfloat16)
    far, d_gates, slot_rows = lax.optimization_barrier(
        (far_sum(own_codes, d_slots, own, slots, group), d_gates, slot_rows)
    )
    sent = cross(far)

    def expert_gradient(slot_rows, d_part):
        return jnp.einsum(
            "ecd,ecf->edf", slot_rows, d_part, preferred_element_type=jnp.float32
        ).astype(jnp.bfloat16)

    sent, grad_gate = lax.optimization_barrier(
        (sent, expert_gradient(slot_rows, d_both[..., :hidden_units]))
    )
    gate_part = reduce_experts(grad_gate, split)
    part, weighted, slot_rows = lax.optimization_barrier(
        (scatter_one(own_codes, d_slots, own, slots, group, sent), weighted, slot_rows)
    )
    kept, moved = scatter_two(part)
    expert_out = jnp.einsum(
        "ecf,efd->ecd", weighted, down_own, preferred_element_type=jnp.float32
    ).astype(jnp.bfloat16)
    far, slot_rows = lax.optimization_barrier(
        (far_sum(own_codes, expert_out, own, slots, group), slot_rows)
    )
    moved, sent, grad_up, expert_out = lax.optimization_barrier(
        (moved, cross(far), expert_gradient(slot_rows, d_both[..., hidden_units:]), expert_out)
    )
    up_part = reduce_experts(grad_up, split)
    kept, moved = scatter_three(kept, moved)
    moved, mixed_part = lax.optimization_barrier(
        (moved, scatter_one(own_codes, expert_out, own, slots, group, sent))
    )
    d_rows = scatter_end(kept, moved)
    d_logits = (
        gates * (d_gates - jnp.sum(gates * d_gates, axis=0, keepdims=True))
    ).astype(jnp.bfloat16)
    grad_router = jnp.einsum("td,et->de", h2_low, d_logits, preferred_element_type=jnp.float32)
    d_normed_two = d_rows + jnp.einsum(
        "et,de->td", d_logits, w_router, preferred_element_type=jnp.float32
    )
    d_resid_norm, grad_norm2 = rms_backward(resid, scale_two, gain_two, d_normed_two)
    d_resid = upstream + d_resid_norm
    d_branch = (RESID * d_resid).astype(jnp.bfloat16)
    grad_out = jnp.einsum(
        "tq,td->qd", merged_low, d_branch, preferred_element_type=jnp.float32
    ).astype(jnp.bfloat16)
    out_cut = grad_out.shape[1] // 256 * 128
    grad_out = fold_one(grad_out)
    merged_gradient = jnp.einsum(
        "td,qd->tq", d_branch, w_out, preferred_element_type=jnp.float32
    ).astype(jnp.bfloat16)
    grad_out, mixed_part, down_part, merged_gradient = lax.optimization_barrier(
        (grad_out, mixed_part, down_part, merged_gradient)
    )
    mixed_kept, mixed_moved = scatter_two(mixed_part)
    out_kept, out_moved = fold_two(grad_out, out_cut)
    down_kept, down_moved = pairs_experts(down_part, split)
    d_query_low, d_key_prompt, d_value_prompt, d_key_cont, d_value_cont = attend_backward(
        query_row_block, merged_gradient, merged_low, log_total, prompt_kv, cont_kv, cosine, sine,
        key_cosine, key_sine, start, prompt_rows, cont_len,
    )
    mixed_moved, out_moved, down_moved, d_key_prompt = lax.optimization_barrier(
        (mixed_moved, out_moved, down_moved, d_key_prompt)
    )
    mixed_kept, mixed_moved = scatter_three(mixed_kept, mixed_moved)
    grad_out = fold_three(out_kept, out_moved)
    mixed = scatter_end(mixed_kept, mixed_moved)
    output = resid + mixed
    y_prompt = output[:prompt_rows].astype(jnp.bfloat16)[None]
    y_cont = output[prompt_rows:].reshape(1, cont_count, cont_len, model_width).astype(jnp.bfloat16)
    d_key_prompt, d_value_prompt = scatter_keys(d_key_prompt, d_value_prompt, prompt_rows)
    d_key_low = jnp.concatenate([d_key_prompt, d_key_cont], axis=0)
    d_value_low = jnp.concatenate([d_value_prompt, d_value_cont], axis=0)
    grad_query = jnp.einsum("td,tq->dq", h1_low, d_query_low, preferred_element_type=jnp.float32)
    grad_key = jnp.einsum("td,tq->dq", h1_low, d_key_low, preferred_element_type=jnp.float32)
    grad_value = jnp.einsum("td,tq->dq", h1_low, d_value_low, preferred_element_type=jnp.float32)
    d_normed_one = jnp.einsum("tq,dq->td", d_query_low, w_query, preferred_element_type=jnp.float32)
    d_normed_one = d_normed_one + jnp.einsum(
        "tq,dq->td", d_key_low, key_weight, preferred_element_type=jnp.float32
    )
    d_normed_one = d_normed_one + jnp.einsum(
        "tq,dq->td", d_value_low, value_weight, preferred_element_type=jnp.float32
    )
    d_tokens_norm, grad_norm1 = rms_backward(tokens, scale_one, gain_one, d_normed_one)
    d_tokens = d_resid + d_tokens_norm
    dx_prompt = d_tokens[:prompt_rows][None]
    dx_cont = d_tokens[prompt_rows:].reshape(1, cont_count, cont_len, model_width)
    small = jnp.concatenate([grad_router, grad_norm1[:, None], grad_norm2[:, None]], axis=1)
    small = jnp.pad(small, ((0, 0), (0, -small.shape[1] % 128)))
    dense = jnp.concatenate([grad_query, grad_key, grad_value, small], axis=1).astype(jnp.bfloat16)
    heads_width = QUERY_HEADS * HEAD_SIZE
    edge = heads_width + 2 * key_value_width
    dense, gate_part = lax.optimization_barrier((fold_one(dense), gate_part))
    gate_kept, gate_moved = pairs_experts(gate_part, split)
    dense = fold_three(*fold_two(dense, edge // 256 * 128))
    dense = jnp.concatenate([dense, grad_out], axis=-1)
    dense, gate_moved, up_part = lax.optimization_barrier((dense, gate_moved, up_part))
    up_kept, up_moved = pairs_experts(up_part, split)
    dense = sum_dense(dense)
    shares = lax.axis_size("dp") * lax.axis_size("ctx")
    grad_down = place_experts(
        jnp.zeros((local_experts, hidden_units // shares, model_width), jnp.float32),
        cores_experts(down_kept, down_moved, split),
        0,
    )
    grad_gate_up = place_experts(
        jnp.zeros((local_experts, model_width // shares, 2 * hidden_units), jnp.float32),
        cores_experts(gate_kept, gate_moved, split),
        0,
    )
    dense, up_moved, grad_gate_up = lax.optimization_barrier((dense, up_moved, grad_gate_up))
    grad_gate_up = place_experts(
        grad_gate_up, cores_experts(up_kept, up_moved, split), hidden_units
    )
    dense = finish_dense(dense, dense.shape[0] < w_query.shape[0] // shares)
    tail = edge + small.shape[1]
    return (
        y_prompt,
        y_cont,
        dx_prompt,
        dx_cont,
        dense[:, edge + expert_total],
        dense[:, :heads_width],
        dense[:, heads_width : heads_width + key_value_width],
        dense[:, heads_width + key_value_width : edge],
        dense[:, tail:],
        dense[:, edge + expert_total + 1],
        dense[:, edge : edge + expert_total],
        grad_gate_up,
        grad_down,
    )


def solution(mesh):
    return jax.shard_map(
        per_device,
        mesh=mesh,
        in_specs=(
            P(("dp", "expert"), "ctx", None),
            P(("dp", "expert"), "ctx", None, None),
            P(),
            P(),
            P(),
            P(),
            P(),
            P(),
            P(),
            P("expert", None, None),
            P("expert", None, None),
            P(("dp", "expert"), "ctx", None),
            P(("dp", "expert"), "ctx", None, None),
            P(("dp", "expert"), "ctx", None),
            P(("dp", "expert"), "ctx", None),
            P(("dp", "expert"), "ctx", None, None),
        ),
        out_specs=(
            P(("dp", "expert"), "ctx", None),
            P(("dp", "expert"), "ctx", None, None),
            P(("dp", "expert"), "ctx", None),
            P(("dp", "expert"), "ctx", None, None),
            P(("dp", "ctx")),
            P(("dp", "ctx"), None),
            P(("dp", "ctx"), None),
            P(("dp", "ctx"), None),
            P(("dp", "ctx"), None),
            P(("dp", "ctx")),
            P(("dp", "ctx"), None),
            P("expert", ("dp", "ctx"), None),
            P("expert", ("dp", "ctx"), None),
        ),
        check_vma=False,
    )
```

```python
from functools import partial

import jax
import jax.numpy as jnp
from jax import lax
from jax.experimental import pallas as pl
from jax.experimental.pallas import tpu as pltpu
from jax.sharding import PartitionSpec as P

QUERY_HEADS = 24
KEY_VALUE_HEADS = 8
HEAD_SIZE = 64


EPS = 1e-06
RESID = 0.22
ATT_SCALE = 0.015625
THETA = 10000.0
NEG = -1e30
LOG2E = 1.4426950408889634


def signed_tables(positions):
    lane = jnp.arange(2 * HEAD_SIZE, dtype=jnp.int32) % HEAD_SIZE
    half_dim = HEAD_SIZE // 2
    frequency = THETA ** (-((lane % half_dim).astype(jnp.float32) * 2.0 / HEAD_SIZE))
    angles = positions[:, None] * frequency[None, :]
    return (jnp.cos(angles), jnp.where(lane < half_dim, -1.0, 1.0) * jnp.sin(angles))


def rms_forward(values, norm_gain):
    inverse = lax.rsqrt(jnp.mean(values * values, axis=-1, keepdims=True) + EPS)
    return (values * inverse * norm_gain, inverse)


def rms_backward(values, inverse, norm_gain, upstream):
    normed = values * inverse
    weighted = upstream * norm_gain
    projected = jnp.mean(weighted * normed, axis=-1, keepdims=True)
    return (inverse * (weighted - normed * projected), jnp.sum(upstream * normed, axis=0))


def slot_codes(routes, visit_order, experts, capacity):
    count = routes.shape[0]
    ids = jnp.arange(count, dtype=jnp.int32)
    visit = jnp.arange(count, dtype=jnp.float32)
    place = (visit_order[:, None] == ids[None, :]).astype(jnp.float32)
    place_row = jnp.sum(place * visit[:, None], axis=0)
    place_col = jnp.sum((visit_order[None, :] == ids[:, None]).astype(jnp.float32) * visit[None, :], axis=1)
    earlier = (place_col[:, None] < place_row[None, :]).astype(jnp.bfloat16)
    named = jnp.any(
        routes.T[None, :, :] == jnp.arange(experts, dtype=jnp.int32)[:, None, None], axis=1
    )
    rank = jnp.dot(named.astype(jnp.bfloat16), earlier, preferred_element_type=jnp.float32)
    return jnp.where(named, jnp.where(rank < capacity, rank, -1.0), -2.0)


def selection(codes, own, slots):
    tokens = codes.shape[-1]
    slot_index = lax.broadcasted_iota(jnp.int32, (slots, tokens), 0).astype(jnp.float32)
    picks = [
        jnp.where(codes[e : e + 1, :] == slot_index, 1.0, 0.0).astype(jnp.bfloat16)
        for e in range(own)
    ]
    return jnp.concatenate(picks, axis=0)


def dispatch_body(own, slots, codes_ref, *refs):
    out_ref = refs[-1]
    pick = selection(codes_ref[0], own, slots)
    at = 0
    for rows_ref in refs[:-1]:
        width = rows_ref.shape[2]
        moved = jnp.dot(pick, rows_ref[0], preferred_element_type=jnp.float32).astype(jnp.bfloat16)
        for e in range(own):
            out_ref[e, :, at : at + width] = moved[e * slots : (e + 1) * slots]
        at += width


def dispatch(codes, parts, own, slots):
    blocks = parts[0].shape[0]
    tokens = codes.shape[2]
    widths = [part.shape[2] for part in parts]
    return pl.pallas_call(
        partial(dispatch_body, own, slots),
        grid=(blocks,),
        in_specs=[pl.BlockSpec((1, codes.shape[1], tokens), lambda b: (b, 0, 0))]
        + [pl.BlockSpec((1, tokens, width), lambda b: (b, 0, 0)) for width in widths],
        out_specs=pl.BlockSpec((own, slots, sum(widths)), lambda b: (0, b, 0)),
        out_shape=jax.ShapeDtypeStruct((own, blocks * slots, sum(widths)), jnp.bfloat16),
        cost_estimate=pl.CostEstimate(
            flops=2 * blocks * own * slots * tokens * sum(widths),
            transcendentals=0,
            bytes_accessed=2 * blocks * (tokens + own * slots) * sum(widths),
        ),
        name="dispatch",
    )(codes, *parts)


def experts_body(at_ref, rows_ref, gate_up_ref, plain_ref, weight_ref, out_ref, both_ref, d_weight_ref):
    total = rows_ref.shape[1]
    hidden_units = plain_ref.shape[2]
    chunk = total // 2 if total % 16 == 0 else total
    for at in range(0, total, chunk):
        rows = pl.ds(at, chunk)
        both = jnp.dot(rows_ref[0, rows], gate_up_ref[0], preferred_element_type=jnp.float32)
        gate, up = both[:, :hidden_units], both[:, hidden_units:]
        plain, weight = plain_ref[0, rows], weight_ref[0, rows]
        logistic = jax.nn.sigmoid(gate)
        silu = gate * logistic
        hidden = silu * up
        d_weight_ref[0, rows] = jnp.sum(hidden * plain, axis=1, keepdims=True)
        out_ref[0, rows] = (weight * hidden).astype(jnp.bfloat16)
        d_hidden = weight * plain
        d_gate = d_hidden * up * (logistic + silu * (1.0 - logistic))
        both_ref[0, rows, :hidden_units] = d_gate.astype(jnp.bfloat16)
        both_ref[0, rows, hidden_units:] = (d_hidden * silu).astype(jnp.bfloat16)


def experts(offset, rows, gate_up, plain, weight):
    own, total, width = rows.shape
    hidden_units = plain.shape[2]
    part = total // 2 if total % 32 == 0 else total
    tile = lambda e, r, at: (e, r, 0)
    return pl.pallas_call(
        experts_body,
        grid_spec=pltpu.PrefetchScalarGridSpec(
            num_scalar_prefetch=1,
            grid=(own, total // part),
            in_specs=[
                pl.BlockSpec((1, part, width), tile),
                pl.BlockSpec((1, width, 2 * hidden_units), lambda e, r, at: (at[0] + e, 0, 0)),
                pl.BlockSpec((1, part, hidden_units), tile),
                pl.BlockSpec((1, part, 1), tile),
            ],
            out_specs=[
                pl.BlockSpec((1, part, hidden_units), tile),
                pl.BlockSpec((1, part, 2 * hidden_units), tile),
                pl.BlockSpec((1, part, 1), tile),
            ],
        ),
        out_shape=[
            jax.ShapeDtypeStruct((own, total, hidden_units), jnp.bfloat16),
            jax.ShapeDtypeStruct((own, total, 2 * hidden_units), jnp.bfloat16),
            jax.ShapeDtypeStruct((own, total, 1), jnp.float32),
        ],
        cost_estimate=pl.CostEstimate(
            flops=4 * own * total * width * hidden_units,
            transcendentals=own * total * hidden_units,
            bytes_accessed=2 * own * (total * (width + 4 * hidden_units) + 2 * width * hidden_units),
        ),
        name="experts",
    )(jnp.asarray(offset, jnp.int32).reshape(1), rows, gate_up, plain, weight)


def combine_body(own, slots, at_ref, codes_ref, rows_ref, *refs):
    out_ref = refs[-1]
    pick = selection(codes_ref[0], own, slots)
    rows = rows_ref[...].reshape(own * slots, rows_ref.shape[-1])
    total = lax.dot_general(
        pick, rows, (((0,), (0,)), ((), ())), preferred_element_type=jnp.float32
    )
    for ref in refs[:-1]:
        total = total + ref[0].astype(jnp.float32)
    out_ref[0] = total.astype(out_ref.dtype)


def combine(at, codes, rows, own, slots, *more):
    count, tokens = at.shape[0], codes.shape[2]
    width = rows.shape[-1]
    return pl.pallas_call(
        partial(combine_body, own, slots),
        grid_spec=pltpu.PrefetchScalarGridSpec(
            num_scalar_prefetch=1,
            grid=(count,),
            in_specs=[
                pl.BlockSpec((1, codes.shape[1], tokens), lambda b, at: (at[b], 0, 0)),
                pl.BlockSpec((own, slots, width), lambda b, at: (0, at[b], 0)),
            ]
            + [pl.BlockSpec((1, tokens, width), lambda b, at: (b, 0, 0)) for _ in more],
            out_specs=pl.BlockSpec((1, tokens, width), lambda b, at: (b, 0, 0)),
        ),
        out_shape=jax.ShapeDtypeStruct((count, tokens, width), jnp.bfloat16),
        cost_estimate=pl.CostEstimate(flops=1, transcendentals=0, bytes_accessed=1),
        name="combine",
    )(at, codes, rows, *more)


def swap(values, axis, bit):
    size = lax.axis_size(axis)
    return lax.ppermute(values, axis, [(i, i ^ bit) for i in range(size)])


def exchange(values, bit, axis, stride, dim):
    take = partial(lax.dynamic_index_in_dim, axis=dim, keepdims=False)
    away = swap(take(values, 1 - bit), axis, stride)
    stay = take(values, bit)
    first = bit == 0
    return jnp.stack([jnp.where(first, stay, away), jnp.where(first, away, stay)])


def paired(group):
    return group == ("ctx", "expert") and lax.axis_size("ctx") == 4 and lax.axis_size("expert") == 2


def gather_gates(gates, group, first_expert, own):
    if not paired(group):
        whole = lax.all_gather(gates, group, axis=0, tiled=False)
        return lax.dynamic_slice_in_dim(whole, first_expert, own, axis=1)
    ctx, side = lax.axis_index("ctx"), lax.axis_index("expert")
    parts = gates.reshape(2, 2, 2, own, gates.shape[1])
    parts = exchange(parts, side, "expert", 1, 0)
    parts = exchange(parts, ctx % 2, "ctx", 1, 2)
    parts = exchange(parts, ctx // 2, "ctx", 2, 2)
    return parts.reshape(8, own, gates.shape[1])


def return_gates(values, group, first_expert, experts):
    blocks, own, tokens = values.shape
    if not paired(group):
        whole = jnp.zeros((blocks, experts, tokens), values.dtype)
        whole = lax.dynamic_update_slice_in_dim(whole, values, first_expert, axis=1)
        return lax.psum_scatter(whole, group, scatter_dimension=0)
    ctx, side = lax.axis_index("ctx"), lax.axis_index("expert")
    parts = values.reshape(2, 2, 2, own, tokens)
    parts = exchange(parts, ctx // 2, "ctx", 2, 0)
    parts = exchange(parts, ctx % 2, "ctx", 1, 1)
    parts = exchange(parts, side, "expert", 1, 2)
    return parts.transpose(0, 2, 1, 3, 4).reshape(experts, tokens)


def added(left, right):
    return (left.astype(jnp.float32) + right.astype(jnp.float32)).astype(jnp.bfloat16)


def far_sum(codes, rows, own, slots, group):
    if not paired(group):
        return jnp.zeros((), jnp.bfloat16)
    far = lax.axis_index(group).astype(jnp.int32) ^ jnp.array([2, 3, 6, 7], jnp.int32)
    return combine(far, codes, rows, own, slots)


def cross(far):
    return swap(far, "ctx", 1) if far.ndim else far


def scatter_one(codes, rows, own, slots, group, sent):
    if not paired(group):
        every = jnp.arange(codes.shape[0], dtype=jnp.int32)
        return lax.psum_scatter(
            combine(every, codes, rows, own, slots), group, scatter_dimension=0
        )
    near = lax.axis_index(group).astype(jnp.int32) ^ jnp.array([0, 1, 4, 5], jnp.int32)
    return combine(near, codes, rows, own, slots, sent)


def scatter_two(part):
    if part.ndim == 2:
        return part, ()
    half = part.shape[-1] // 2
    left, right = part[:, :, :half], part[:, :, half:]
    moved = swap(left[2:], "ctx", 2), swap(jnp.stack([right[1], right[3]]), "expert", 1)
    return (left[0], left[1], right[0], right[2]), moved


def scatter_three(kept, moved):
    if not moved:
        return kept, ()
    left, left_other, right, right_other = kept
    left_sent, right_sent = moved
    onward = (
        swap(added(left_other, left_sent[1]), "expert", 1),
        swap(added(right_other, right_sent[1]), "ctx", 2),
    )
    return (left, left_sent[0], right, right_sent[0]), onward


def scatter_end(kept, moved):
    if not moved:
        return kept.astype(jnp.float32)
    wide = lambda *pieces: sum(piece.astype(jnp.float32) for piece in pieces)
    return jnp.concatenate(
        [wide(kept[0], kept[1], moved[0]), wide(kept[2], kept[3], moved[1])], axis=1
    )


def lane_half(shape):
    return lax.broadcasted_iota(jnp.int32, shape, 1) // HEAD_SIZE


def turn(values, cosine, sine):
    half_dim = HEAD_SIZE // 2
    width = values.shape[1]
    lane = lax.broadcasted_iota(jnp.int32, values.shape, 1) % HEAD_SIZE
    partner = jnp.where(
        lane < half_dim,
        pltpu.roll(values, width - half_dim, 1),
        pltpu.roll(values, half_dim, 1),
    )
    return values * cosine + partner * sine


def to_key_half(values, swap, key_half):
    moved = jnp.where(swap, pltpu.roll(values, HEAD_SIZE, 1), values)
    return jnp.where(lane_half(values.shape) == key_half, moved, 0.0)


def project_keys_body(rows, h_ref, kw_ref, vw_ref, cos_ref, sin_ref, prompt_ref, cont_ref):
    key = jnp.dot(h_ref[...], kw_ref[...], preferred_element_type=jnp.float32)
    key = turn(key, cos_ref[...], sin_ref[...]).astype(jnp.bfloat16)
    value = jnp.dot(h_ref[...], vw_ref[...], preferred_element_type=jnp.float32)
    value = value.astype(jnp.bfloat16)
    prompt_ref[0] = key[:rows]
    prompt_ref[1] = value[:rows]
    cont_ref[0] = key[rows:]
    cont_ref[1] = value[rows:]


def project_keys(hidden, key_weight, value_weight, cosine, sine, rows):
    tokens, depth = hidden.shape
    width = key_weight.shape[1]
    whole = lambda j: (0, 0)
    column = lambda j: (0, j)
    return pl.pallas_call(
        partial(project_keys_body, rows),
        grid=(width // 128,),
        in_specs=[
            pl.BlockSpec((tokens, depth), whole),
            pl.BlockSpec((depth, 128), column),
            pl.BlockSpec((depth, 128), column),
            pl.BlockSpec((tokens, 128), whole),
            pl.BlockSpec((tokens, 128), whole),
        ],
        out_specs=[
            pl.BlockSpec((2, rows, 128), lambda j: (0, 0, j)),
            pl.BlockSpec((2, tokens - rows, 128), lambda j: (0, 0, j)),
        ],
        out_shape=[
            jax.ShapeDtypeStruct((2, rows, width), jnp.bfloat16),
            jax.ShapeDtypeStruct((2, tokens - rows, width), jnp.bfloat16),
        ],
        cost_estimate=pl.CostEstimate(
            flops=4 * tokens * depth * width,
            transcendentals=0,
            bytes_accessed=2 * (tokens * depth + 2 * depth * width + 2 * tokens * width),
        ),
        name="project_keys",
    )(hidden, key_weight, value_weight, cosine, sine)


def gather_keys(near_kv, work):
    if lax.axis_size("ctx") != 4:
        return lax.all_gather(near_kv, "ctx", axis=1, tiled=True), work
    rows = near_kv.shape[1]
    here = lax.axis_index("ctx")
    pair, side, work = lax.optimization_barrier(
        (swap(near_kv, "ctx", 2), swap(near_kv, "ctx", 1), work)
    )
    whole = jnp.zeros((2, 4 * rows, near_kv.shape[2]), near_kv.dtype)
    pieces = ((0, near_kv), (2, pair), (1, side), (3, swap(pair, "ctx", 1)))
    for step, piece in pieces:
        whole = lax.dynamic_update_slice_in_dim(whole, piece, (here ^ step) * rows, axis=1)
    return whole, work


def head_place(group):
    head = pl.program_id(0)
    key_half = (head // group) % 2
    return head, key_half, (head % 2) != key_half


def attend_forward_body(
    group, prompt_rows, cont_len, pos_ref, q_ref, cos_ref, sin_ref, kp_ref, vp_ref, kc_ref, vc_ref,
    qr_ref, out_ref, log_ref,
):
    head, key_half, swap = head_place(group)
    rotated = turn(q_ref[...], cos_ref[...], sin_ref[...]).astype(jnp.bfloat16)
    qr_ref[...] = rotated
    query = to_key_half(rotated.astype(jnp.float32), swap, key_half) * ATT_SCALE
    query = query.astype(jnp.bfloat16)
    nt = (((1,), (1,)), ((), ()))

    def finish(parts, rows):
        highest = parts[0][0].max(axis=1, keepdims=True)
        for scores, _ in parts[1:]:
            highest = jnp.maximum(highest, scores.max(axis=1, keepdims=True))
        lifted = [jnp.exp2(scores * LOG2E - highest * LOG2E) for scores, _ in parts]
        total = lifted[0].sum(axis=1, keepdims=True)
        for piece in lifted[1:]:
            total = total + piece.sum(axis=1, keepdims=True)
        inverse = 1.0 / total
        result = None
        for piece, (_, value) in zip(lifted, parts):
            term = jnp.dot(
                piece.astype(jnp.bfloat16), value, preferred_element_type=jnp.float32
            )
            result = term if result is None else result + term
        log_total = jnp.broadcast_to(highest + jnp.log(total), (total.shape[0], 128))
        log_ref[0, :, rows] = jnp.transpose(log_total)[:8]
        keep = jnp.where(lane_half(result.shape) == key_half, result * inverse, 0.0)
        keep = jnp.where(swap, pltpu.roll(keep, HEAD_SIZE, 1), keep).astype(jnp.bfloat16)

        @pl.when(head % 2 == 0)
        def _():
            out_ref[rows, :] = keep

        @pl.when(head % 2 == 1)
        def _():
            out_ref[rows, :] = out_ref[rows, :] + keep

    total_rows = q_ref.shape[0]
    first = lax.dot_general(
        query[:prompt_rows], kp_ref[...], nt, preferred_element_type=jnp.float32
    )
    row = lax.broadcasted_iota(jnp.int32, first.shape, 0) + pos_ref[0]
    first = jnp.where(lax.broadcasted_iota(jnp.int32, first.shape, 1) <= row, first, NEG)
    finish([(first, vp_ref[...])], pl.ds(0, prompt_rows))
    lower = query[prompt_rows:]
    wide = lax.dot_general(lower, kp_ref[...], nt, preferred_element_type=jnp.float32)
    near = lax.dot_general(lower, kc_ref[...], nt, preferred_element_type=jnp.float32)
    row = lax.broadcasted_iota(jnp.int32, near.shape, 0)
    col = lax.broadcasted_iota(jnp.int32, near.shape, 1)
    near = jnp.where((col <= row) & (col // cont_len == row // cont_len), near, NEG)
    finish([(wide, vp_ref[...]), (near, vc_ref[...])], pl.ds(prompt_rows, total_rows - prompt_rows))


def attend_forward(q_lin, prompt_kv, cont_kv, cosine, sine, start, rows, cont_len):
    tokens, width = q_lin.shape
    heads = width // HEAD_SIZE
    group = heads // (prompt_kv.shape[2] // HEAD_SIZE)
    keys, near = prompt_kv.shape[1], cont_kv.shape[1]
    tile = lambda h, *_: (0, h // 2)
    same = lambda h, *_: (0, 0)
    return pl.pallas_call(
        partial(attend_forward_body, group, rows, cont_len),
        grid_spec=pltpu.PrefetchScalarGridSpec(
            num_scalar_prefetch=1,
            grid=(heads,),
            in_specs=[
                pl.BlockSpec((tokens, 128), tile),
                pl.BlockSpec((tokens, 128), same),
                pl.BlockSpec((tokens, 128), same),
                pl.BlockSpec((None, keys, 128), lambda h, *_: (0, 0, h // (2 * group))),
                pl.BlockSpec((None, keys, 128), lambda h, *_: (1, 0, h // (2 * group))),
                pl.BlockSpec((None, near, 128), lambda h, *_: (0, 0, h // (2 * group))),
                pl.BlockSpec((None, near, 128), lambda h, *_: (1, 0, h // (2 * group))),
            ],
            out_specs=[
                pl.BlockSpec((tokens, 128), tile),
                pl.BlockSpec((tokens, 128), tile),
                pl.BlockSpec((1, 8, tokens), lambda h, *_: (h, 0, 0)),
            ],
        ),
        out_shape=[
            jax.ShapeDtypeStruct((tokens, width), jnp.bfloat16),
            jax.ShapeDtypeStruct((tokens, width), jnp.bfloat16),
            jax.ShapeDtypeStruct((heads, 8, tokens), jnp.float32),
        ],
        cost_estimate=pl.CostEstimate(
            flops=4 * heads * tokens * (keys + near) * 128,
            transcendentals=heads * tokens * (keys + near),
            bytes_accessed=8 * tokens * width,
        ),
        name="attend_forward",
    )(start, q_lin, cosine, sine, prompt_kv, prompt_kv, cont_kv, cont_kv)


def attend_backward_body(
    group, prompt_rows, cont_len, chunk, pos_ref, q_ref, do_ref, out_ref, log_ref, cos_ref, sin_ref,
    kcos_ref, ksin_ref, kp_ref, vp_ref, kc_ref, vc_ref,
    dq_ref, dkp_ref, dvp_ref, dkc_ref, dvc_ref, dk_acc, dv_acc,
):
    head, key_half, swap = head_place(group)
    tokens = q_ref.shape[0]
    keys = kp_ref.shape[0]
    near = kc_ref.shape[0]
    nt = (((1,), (1,)), ((), ()))
    tn = (((0,), (0,)), ((), ()))

    @pl.when(head % (2 * group) == 0)
    def _():
        dk_acc[...] = jnp.zeros_like(dk_acc)
        dv_acc[...] = jnp.zeros_like(dv_acc)

    query = to_key_half(q_ref[...].astype(jnp.float32), swap, key_half) * ATT_SCALE
    query = query.astype(jnp.bfloat16)
    d_out = to_key_half(do_ref[...].astype(jnp.float32), swap, key_half)
    result = to_key_half(out_ref[...].astype(jnp.float32), swap, key_half)
    centre = jnp.transpose(
        jnp.broadcast_to(jnp.sum(d_out * result, axis=1, keepdims=True), (tokens, 128))
    )[:1]
    d_out = d_out.astype(jnp.bfloat16)
    log_total = log_ref[0][:1]
    row = lax.broadcasted_iota(jnp.int32, (1, tokens), 1)
    limit = jnp.where(row < prompt_rows, row + pos_ref[0], keys)

    def step(key, value, query, d_out, log_total, centre, allowed, at, count):
        scores = lax.dot_general(key, query, nt, preferred_element_type=jnp.float32)
        scores = jnp.where(allowed(scores.shape), scores, NEG)
        weights = jnp.exp2(scores * LOG2E - log_total * LOG2E)
        d_weights = lax.dot_general(value, d_out, nt, preferred_element_type=jnp.float32)
        d_scores = (weights * (d_weights - centre)).astype(jnp.bfloat16)
        dv_acc[at : at + count] += jnp.dot(
            weights.astype(jnp.bfloat16), d_out, preferred_element_type=jnp.float32
        )
        dk_acc[at : at + count] += jnp.dot(d_scores, query, preferred_element_type=jnp.float32)
        return lax.dot_general(d_scores, key, tn, preferred_element_type=jnp.float32)

    d_query = jnp.zeros((tokens, 128), jnp.float32)
    for at in range(0, keys, chunk):

        def seen(shape, at=at):
            return lax.broadcasted_iota(jnp.int32, shape, 0) + at <= limit

        d_query = d_query + step(
            kp_ref[at : at + chunk], vp_ref[at : at + chunk], query, d_out, log_total, centre, seen,
            at, chunk,
        )

    def nearby(shape):
        key_at = lax.broadcasted_iota(jnp.int32, shape, 0)
        query_at = lax.broadcasted_iota(jnp.int32, shape, 1)
        return (key_at <= query_at) & (key_at // cont_len == query_at // cont_len)

    tail = step(
        kc_ref[...], vc_ref[...], query[prompt_rows:], d_out[prompt_rows:],
        log_total[:, prompt_rows:], centre[:, prompt_rows:], nearby, keys, near,
    )
    d_query = jnp.concatenate([d_query[:prompt_rows], d_query[prompt_rows:] + tail], axis=0)
    d_query = jnp.where(lane_half(d_query.shape) == key_half, d_query * ATT_SCALE, 0.0)
    d_query = jnp.where(swap, pltpu.roll(d_query, HEAD_SIZE, 1), d_query)
    d_query = turn(d_query, cos_ref[...], -sin_ref[...]).astype(jnp.bfloat16)

    @pl.when(head % 2 == 0)
    def _():
        dq_ref[...] = d_query

    @pl.when(head % 2 == 1)
    def _():
        dq_ref[...] = dq_ref[...] + d_query

    @pl.when(head % (2 * group) == 2 * group - 1)
    def _():
        dk = turn(dk_acc[...], kcos_ref[...], -ksin_ref[...]).astype(jnp.bfloat16)
        dv = dv_acc[...].astype(jnp.bfloat16)
        dkp_ref[...] = dk[:keys]
        dkc_ref[...] = dk[keys:]
        dvp_ref[...] = dv[:keys]
        dvc_ref[...] = dv[keys:]


def attend_backward(
    query, d_out, result, log_total, prompt_kv, cont_kv, cosine, sine,
    key_cosine, key_sine, start, rows, cont_len,
):
    tokens, width = query.shape
    heads = width // HEAD_SIZE
    key_width = prompt_kv.shape[2]
    group = heads // (key_width // HEAD_SIZE)
    keys, near = prompt_kv.shape[1], cont_kv.shape[1]
    chunk = min(256, keys)
    tile = lambda h, *_: (0, h // 2)
    key_tile = lambda h, *_: (0, h // (2 * group))
    same = lambda h, *_: (0, 0)
    return pl.pallas_call(
        partial(attend_backward_body, group, rows, cont_len, chunk),
        grid_spec=pltpu.PrefetchScalarGridSpec(
            num_scalar_prefetch=1,
            grid=(heads,),
            in_specs=[
                pl.BlockSpec((tokens, 128), tile),
                pl.BlockSpec((tokens, 128), tile),
                pl.BlockSpec((tokens, 128), tile),
                pl.BlockSpec((1, 8, tokens), lambda h, *_: (h, 0, 0)),
                pl.BlockSpec((tokens, 128), same),
                pl.BlockSpec((tokens, 128), same),
                pl.BlockSpec((keys + near, 128), same),
                pl.BlockSpec((keys + near, 128), same),
                pl.BlockSpec((None, keys, 128), lambda h, *_: (0, 0, h // (2 * group))),
                pl.BlockSpec((None, keys, 128), lambda h, *_: (1, 0, h // (2 * group))),
                pl.BlockSpec((None, near, 128), lambda h, *_: (0, 0, h // (2 * group))),
                pl.BlockSpec((None, near, 128), lambda h, *_: (1, 0, h // (2 * group))),
            ],
            out_specs=[
                pl.BlockSpec((tokens, 128), tile),
                pl.BlockSpec((keys, 128), key_tile),
                pl.BlockSpec((keys, 128), key_tile),
                pl.BlockSpec((near, 128), key_tile),
                pl.BlockSpec((near, 128), key_tile),
            ],
            scratch_shapes=[
                pltpu.VMEM((keys + near, 128), jnp.float32),
                pltpu.VMEM((keys + near, 128), jnp.float32),
            ],
        ),
        out_shape=[
            jax.ShapeDtypeStruct((tokens, width), jnp.bfloat16),
            jax.ShapeDtypeStruct((keys, key_width), jnp.bfloat16),
            jax.ShapeDtypeStruct((keys, key_width), jnp.bfloat16),
            jax.ShapeDtypeStruct((near, key_width), jnp.bfloat16),
            jax.ShapeDtypeStruct((near, key_width), jnp.bfloat16),
        ],
        cost_estimate=pl.CostEstimate(
            flops=10 * heads * tokens * (keys + near) * 128,
            transcendentals=heads * tokens * (keys + near),
            bytes_accessed=8 * tokens * width,
        ),
        name="attend_backward",
    )(
        start, query, d_out, result, log_total, cosine, sine, key_cosine, key_sine, prompt_kv,
        prompt_kv, cont_kv, cont_kv,
    )


def reduce_experts(grad, split):
    axes = ("dp", "ctx") if split == 1 else "dp"
    return lax.psum_scatter(grad, axes, scatter_dimension=1, tiled=True)


def send_experts(part, split):
    size = lax.axis_size("ctx")
    if split == 1:
        return (part,)
    if size & (size - 1):
        return (lax.all_to_all(part, "ctx", split_axis=1, concat_axis=0, tiled=True),)
    own, rows, width = part.shape
    here = lax.axis_index("ctx")
    part = part.reshape(own, size, rows // size, width)
    pieces = [lax.dynamic_index_in_dim(part, here ^ step, 1, keepdims=False) for step in range(size)]
    return tuple(swap(piece, "ctx", step) if step else piece for step, piece in enumerate(pieces))


def pairs_experts(part, split):
    if split != 4:
        return part, ()
    own, rows, width = part.shape
    part = part.reshape(own, 2, 2, rows // 4, width)
    pair = lax.axis_index("ctx") // 2
    take = partial(lax.dynamic_index_in_dim, axis=1, keepdims=False)
    return take(part, pair), swap(take(part, 1 - pair), "ctx", 2)


def cores_experts(kept, moved, split):
    if split != 4:
        return send_experts(kept, split)
    core = lax.axis_index("ctx") % 2
    take = partial(lax.dynamic_index_in_dim, axis=1, keepdims=False)
    crossed = swap(jnp.stack([take(kept, 1 - core), take(moved, 1 - core)]), "ctx", 1)
    return take(kept, core), crossed[0], take(moved, core), crossed[1]


def place_experts(whole, pieces, column):
    here = lax.axis_index("ctx")
    own = pieces[0].shape[0]
    for step, piece in enumerate(pieces):
        first = (here ^ step) * own if len(pieces) > 1 else 0
        whole = lax.dynamic_update_slice(whole, piece.astype(jnp.float32), (first, 0, column))
    return whole


def scatter_keys(d_key, d_value, rows):
    size = lax.axis_size("ctx")
    here = lax.axis_index("ctx")

    def share(owner):
        return jnp.concatenate(
            [
                lax.dynamic_slice_in_dim(d_key, owner * rows, rows, axis=0),
                lax.dynamic_slice_in_dim(d_value, owner * rows, rows, axis=0),
            ],
            axis=1,
        )

    total = share(here).astype(jnp.float32)
    for hop in range(1, size):
        moved = lax.ppermute(
            share((here + hop) % size), "ctx", [(i, (i + hop) % size) for i in range(size)]
        )
        total = total + moved.astype(jnp.float32)
    total = total.astype(jnp.bfloat16)
    return (total[:, : d_key.shape[1]], total[:, d_key.shape[1] :])


def folds(grad):
    return paired(("ctx", "expert")) and grad.shape[0] % (64 * lax.axis_size("dp")) == 0


def fold_one(grad):
    if not folds(grad):
        return lax.psum_scatter(grad, ("dp", "ctx"), scatter_dimension=0, tiled=True)
    rows, width = grad.shape
    parts = lax.axis_size("dp")
    core = lax.axis_index("ctx") % 2
    take = partial(lax.dynamic_index_in_dim, axis=2, keepdims=False)
    grad = grad.reshape(parts, 2, 2, 2, rows // (8 * parts), width)
    return added(take(grad, core), swap(take(grad, 1 - core), "ctx", 1))


def fold_two(one, cut):
    if one.ndim == 2:
        return one, ()
    pair = lax.axis_index("ctx") // 2
    side = lax.axis_index("expert")
    take = partial(lax.dynamic_index_in_dim, keepdims=False)
    left, right = one[..., :cut], one[..., cut:]
    moved = swap(take(left, 1 - pair, 1), "ctx", 2), swap(take(right, 1 - side, 2), "expert", 1)
    return (take(left, pair, 1), take(right, side, 2)), moved


def fold_three(kept, moved):
    if not moved:
        return kept
    pair = lax.axis_index("ctx") // 2
    side = lax.axis_index("expert")
    take = partial(lax.dynamic_index_in_dim, keepdims=False)
    left, right = added(kept[0], moved[0]), added(kept[1], moved[1])
    left_sent = swap(take(left, 1 - side, 1), "expert", 1)
    right_sent = swap(take(right, 1 - pair, 1), "ctx", 2)
    whole = jnp.concatenate(
        [added(take(left, side, 1), left_sent), added(take(right, pair, 1), right_sent)], axis=-1
    )
    return whole


def scatter_parts(parts):
    size = lax.axis_size("dp")
    here = lax.axis_index("dp")
    take = partial(lax.dynamic_index_in_dim, axis=0, keepdims=False)
    total = take(parts, here).astype(jnp.float32)
    for hop in range(1, size):
        moved = lax.ppermute(
            take(parts, (here + hop) % size), "dp", [(i, (i + hop) % size) for i in range(size)]
        )
        total = total + moved.astype(jnp.float32)
    return total.astype(jnp.bfloat16)


def sum_dense(grad):
    return lax.psum(grad, "expert") if grad.ndim == 2 else scatter_parts(grad)


def finish_dense(grad, halves):
    if not halves:
        return grad.astype(jnp.float32)
    other = swap(grad, "expert", 1)
    first = lax.axis_index("expert") == 0
    return jnp.concatenate(
        [jnp.where(first, grad, other), jnp.where(first, other, grad)], axis=0
    ).astype(jnp.float32)


def per_device(
    x_prompt,
    x_cont,
    norm1_gain,
    w_query,
    key_weight,
    value_weight,
    w_out,
    norm2_gain,
    w_router,
    w_gate_up,
    w_down,
    routes_prompt,
    routes_cont,
    slot_order,
    dy_prompt,
    dy_cont,
):
    model_width = x_prompt.shape[2]
    prompt_rows = x_prompt.shape[1]
    cont_count = x_cont.shape[1]
    cont_len = x_cont.shape[2]
    cont_rows = cont_count * cont_len
    count_of_tokens = prompt_rows + cont_rows
    key_value_width = KEY_VALUE_HEADS * HEAD_SIZE
    local_experts = w_gate_up.shape[0]
    expert_groups = lax.axis_size("expert")
    expert_total = local_experts * expert_groups
    top_count = routes_prompt.shape[2]
    capacity = (count_of_tokens * top_count + expert_total - 1) // expert_total
    hidden_units = w_down.shape[1]
    prompt_total = prompt_rows * lax.axis_size("ctx")
    count_of_keys = prompt_total + cont_rows
    split = lax.axis_size("ctx") if local_experts % lax.axis_size("ctx") == 0 else 1
    own = local_experts // split
    blocks = split * expert_groups
    slots = -(-capacity // 8) * 8
    group = ("ctx", "expert") if split > 1 else ("expert",)
    block_index = lax.axis_index(group)
    own_offset = lax.axis_index("ctx") * own if split > 1 else 0
    first_expert = lax.axis_index("expert") * local_experts + own_offset
    gate_up_own = w_gate_up
    down_own = w_down
    if split > 1:
        gate_up_own = lax.dynamic_slice_in_dim(w_gate_up, own_offset, own, axis=0)
        down_own = lax.dynamic_slice_in_dim(w_down, own_offset, own, axis=0)
    routes = jnp.concatenate(
        [routes_prompt[0], routes_cont[0].reshape(cont_rows, top_count)], axis=0
    )
    codes = slot_codes(routes, slot_order[0, 0], expert_total, capacity)
    upstream_low = jnp.concatenate([dy_prompt[0], dy_cont[0].reshape(cont_rows, model_width)], axis=0)
    upstream = upstream_low.astype(jnp.float32)
    first_width = model_width // 384 * 128
    upstream_first = lax.all_gather(upstream_low[:, :first_width], group, axis=0, tiled=False)
    assert capacity <= 256
    fold = (model_width - first_width) // count_of_tokens
    code_rows = -(-expert_total // (8 * fold)) * 8
    code_table = jnp.pad(
        codes.astype(jnp.bfloat16),
        ((0, code_rows * fold - expert_total), (0, 0)),
        constant_values=-2.0,
    )
    code_table = jnp.concatenate(
        [code_table[i * code_rows : (i + 1) * code_rows] for i in range(fold)], axis=1
    )
    gain_one = norm1_gain.astype(jnp.float32)
    gain_two = norm2_gain.astype(jnp.float32)
    tokens = jnp.concatenate(
        [x_prompt[0], x_cont[0].reshape(cont_rows, model_width)], axis=0
    ).astype(jnp.float32)
    normed_one, scale_one = rms_forward(tokens, gain_one)
    h1_low = normed_one.astype(jnp.bfloat16)
    row_index = jnp.arange(count_of_tokens, dtype=jnp.int32)
    cont_offset = row_index - prompt_rows
    start = lax.axis_index("ctx") * prompt_rows
    query_pos = jnp.where(
        cont_offset >= 0, prompt_total + cont_offset % cont_len, start + row_index
    )
    key_index = jnp.arange(count_of_keys, dtype=jnp.int32)
    key_pos = jnp.where(
        key_index >= prompt_total, prompt_total + (key_index - prompt_total) % cont_len, key_index
    )
    start = start.astype(jnp.int32)[None]
    cosine, sine = signed_tables(query_pos.astype(jnp.float32))
    key_cosine, key_sine = signed_tables(key_pos.astype(jnp.float32))
    near_kv, cont_kv = project_keys(
        h1_low, key_weight, value_weight, cosine, sine, prompt_rows
    )
    near_kv, h1_late = lax.optimization_barrier((near_kv, h1_low))
    prompt_kv, q_lin = gather_keys(
        near_kv, jnp.dot(h1_late, w_query, preferred_element_type=jnp.float32)
    )
    travel = jnp.concatenate([upstream_low[:, first_width:], code_table], axis=0)
    prompt_kv, travel, upstream_first = lax.optimization_barrier(
        (prompt_kv, travel, upstream_first)
    )
    upstream_all = lax.all_gather(travel, group, axis=0, tiled=False)
    codes_all = upstream_all[:, count_of_tokens:]
    codes_all = jnp.concatenate(
        [
            codes_all[:, :, i * count_of_tokens : (i + 1) * count_of_tokens] for i in range(fold)
        ],
        axis=1,
    ).astype(jnp.float32)
    own_codes = lax.dynamic_slice_in_dim(codes_all, first_expert, own, axis=1)
    own_codes = jnp.pad(own_codes, ((0, 0), (0, -own % 8), (0, 0)), constant_values=-2.0)
    d_slot_rows = dispatch(own_codes, (upstream_first, upstream_all), own, slots)
    d_plain = jnp.einsum("ecd,efd->ecf", d_slot_rows, down_own, preferred_element_type=jnp.float32)
    query_row_block, merged_low, log_total = attend_forward(
        q_lin, prompt_kv, cont_kv, cosine, sine, start, prompt_rows, cont_len
    )
    branch = jnp.dot(merged_low, w_out, preferred_element_type=jnp.float32)
    resid = tokens + RESID * branch
    normed_two, scale_two = rms_forward(resid, gain_two)
    h2_low = normed_two.astype(jnp.bfloat16)
    rows_all = lax.all_gather(h2_low, group, axis=0, tiled=False)
    named = codes > -1.5
    logits = jnp.einsum("td,de->et", h2_low, w_router, preferred_element_type=jnp.float32)
    logits = jnp.where(named, logits, NEG)
    lifted = jnp.where(named, jnp.exp(logits - jnp.max(logits, axis=0, keepdims=True)), 0.0)
    gates = lifted / jnp.sum(lifted, axis=0, keepdims=True)
    own_gates, rows_all, d_plain = lax.optimization_barrier(
        (gather_gates(gates, group, first_expert, own), rows_all, d_plain)
    )
    slot_rows = dispatch(own_codes, (rows_all,), own, slots)
    slot_index = jnp.arange(slots, dtype=jnp.int32).astype(jnp.float32)
    picked = own_codes[:, :own, None, :] == slot_index[None, None, :, None]
    slot_gate = jnp.sum(jnp.where(picked, own_gates[:, :, None, :], 0.0), axis=-1)
    slot_gate = slot_gate.transpose(1, 0, 2).reshape(own, blocks * slots)
    weighted, d_both, d_slot_gate = experts(
        own_offset, slot_rows, w_gate_up, d_plain, RESID * slot_gate[:, :, None]
    )
    d_slot_gate = RESID * d_slot_gate[:, :, 0]
    grad_down = jnp.einsum(
        "ecf,ecd->efd", weighted, d_slot_rows, preferred_element_type=jnp.float32
    ).astype(jnp.bfloat16)
    d_both, _, d_slot_gate = lax.optimization_barrier(
        (d_both, grad_down, d_slot_gate)
    )
    down_part = reduce_experts(grad_down, split)
    d_gates_own = jnp.sum(
        jnp.where(
            picked,
            d_slot_gate.reshape(own, blocks, slots).transpose(1, 0, 2)[..., None],
            0.0,
        ),
        axis=2,
    )
    d_gates = return_gates(d_gates_own, group, first_expert, expert_total)
    d_slots = jnp.einsum(
        "ecf,edf->ecd", d_both, gate_up_own, preferred_element_type=jnp.float32
    ).astype(jnp.bfloat16)
    far, d_gates, slot_rows = lax.optimization_barrier(
        (far_sum(own_codes, d_slots, own, slots, group), d_gates, slot_rows)
    )
    sent = cross(far)

    def expert_gradient(slot_rows, d_part):
        return jnp.einsum(
            "ecd,ecf->edf", slot_rows, d_part, preferred_element_type=jnp.float32
        ).astype(jnp.bfloat16)

    sent, grad_gate = lax.optimization_barrier(
        (sent, expert_gradient(slot_rows, d_both[..., :hidden_units]))
    )
    gate_part = reduce_experts(grad_gate, split)
    part, weighted, slot_rows = lax.optimization_barrier(
        (scatter_one(own_codes, d_slots, own, slots, group, sent), weighted, slot_rows)
    )
    kept, moved = scatter_two(part)
    expert_out = jnp.einsum(
        "ecf,efd->ecd", weighted, down_own, preferred_element_type=jnp.float32
    ).astype(jnp.bfloat16)
    far, slot_rows = lax.optimization_barrier(
        (far_sum(own_codes, expert_out, own, slots, group), slot_rows)
    )
    moved, sent, grad_up, expert_out = lax.optimization_barrier(
        (moved, cross(far), expert_gradient(slot_rows, d_both[..., hidden_units:]), expert_out)
    )
    up_part = reduce_experts(grad_up, split)
    kept, moved = scatter_three(kept, moved)
    moved, mixed_part = lax.optimization_barrier(
        (moved, scatter_one(own_codes, expert_out, own, slots, group, sent))
    )
    d_rows = scatter_end(kept, moved)
    d_logits = (
        gates * (d_gates - jnp.sum(gates * d_gates, axis=0, keepdims=True))
    ).astype(jnp.bfloat16)
    grad_router = jnp.einsum("td,et->de", h2_low, d_logits, preferred_element_type=jnp.float32)
    d_normed_two = d_rows + jnp.einsum(
        "et,de->td", d_logits, w_router, preferred_element_type=jnp.float32
    )
    d_resid_norm, grad_norm2 = rms_backward(resid, scale_two, gain_two, d_normed_two)
    d_resid = upstream + d_resid_norm
    d_branch = (RESID * d_resid).astype(jnp.bfloat16)
    grad_out = jnp.einsum(
        "tq,td->qd", merged_low, d_branch, preferred_element_type=jnp.float32
    ).astype(jnp.bfloat16)
    out_cut = grad_out.shape[1] // 256 * 128
    grad_out = fold_one(grad_out)
    merged_gradient = jnp.einsum(
        "td,qd->tq", d_branch, w_out, preferred_element_type=jnp.float32
    ).astype(jnp.bfloat16)
    grad_out, mixed_part, down_part, merged_gradient = lax.optimization_barrier(
        (grad_out, mixed_part, down_part, merged_gradient)
    )
    mixed_kept, mixed_moved = scatter_two(mixed_part)
    out_kept, out_moved = fold_two(grad_out, out_cut)
    down_kept, down_moved = pairs_experts(down_part, split)
    d_query_low, d_key_prompt, d_value_prompt, d_key_cont, d_value_cont = attend_backward(
        query_row_block, merged_gradient, merged_low, log_total, prompt_kv, cont_kv, cosine, sine,
        key_cosine, key_sine, start, prompt_rows, cont_len,
    )
    mixed_moved, out_moved, down_moved, d_key_prompt = lax.optimization_barrier(
        (mixed_moved, out_moved, down_moved, d_key_prompt)
    )
    mixed_kept, mixed_moved = scatter_three(mixed_kept, mixed_moved)
    grad_out = fold_three(out_kept, out_moved)
    mixed = scatter_end(mixed_kept, mixed_moved)
    output = resid + mixed
    y_prompt = output[:prompt_rows].astype(jnp.bfloat16)[None]
    y_cont = output[prompt_rows:].reshape(1, cont_count, cont_len, model_width).astype(jnp.bfloat16)
    d_key_prompt, d_value_prompt = scatter_keys(d_key_prompt, d_value_prompt, prompt_rows)
    d_key_low = jnp.concatenate([d_key_prompt, d_key_cont], axis=0)
    d_value_low = jnp.concatenate([d_value_prompt, d_value_cont], axis=0)
    grad_query = jnp.einsum("td,tq->dq", h1_low, d_query_low, preferred_element_type=jnp.float32)
    grad_key = jnp.einsum("td,tq->dq", h1_low, d_key_low, preferred_element_type=jnp.float32)
    grad_value = jnp.einsum("td,tq->dq", h1_low, d_value_low, preferred_element_type=jnp.float32)
    d_normed_one = jnp.einsum("tq,dq->td", d_query_low, w_query, preferred_element_type=jnp.float32)
    d_normed_one = d_normed_one + jnp.einsum(
        "tq,dq->td", d_key_low, key_weight, preferred_element_type=jnp.float32
    )
    d_normed_one = d_normed_one + jnp.einsum(
        "tq,dq->td", d_value_low, value_weight, preferred_element_type=jnp.float32
    )
    d_tokens_norm, grad_norm1 = rms_backward(tokens, scale_one, gain_one, d_normed_one)
    d_tokens = d_resid + d_tokens_norm
    dx_prompt = d_tokens[:prompt_rows][None]
    dx_cont = d_tokens[prompt_rows:].reshape(1, cont_count, cont_len, model_width)
    small = jnp.concatenate([grad_router, grad_norm1[:, None], grad_norm2[:, None]], axis=1)
    small = jnp.pad(small, ((0, 0), (0, -small.shape[1] % 128)))
    dense = jnp.concatenate([grad_query, grad_key, grad_value, small], axis=1).astype(jnp.bfloat16)
    heads_width = QUERY_HEADS * HEAD_SIZE
    edge = heads_width + 2 * key_value_width
    dense, gate_part = lax.optimization_barrier((fold_one(dense), gate_part))
    gate_kept, gate_moved = pairs_experts(gate_part, split)
    dense = fold_three(*fold_two(dense, edge // 256 * 128))
    dense = jnp.concatenate([dense, grad_out], axis=-1)
    dense, gate_moved, up_part = lax.optimization_barrier((dense, gate_moved, up_part))
    up_kept, up_moved = pairs_experts(up_part, split)
    dense = sum_dense(dense)
    shares = lax.axis_size("dp") * lax.axis_size("ctx")
    grad_down = place_experts(
        jnp.zeros((local_experts, hidden_units // shares, model_width), jnp.float32),
        cores_experts(down_kept, down_moved, split),
        0,
    )
    grad_gate_up = place_experts(
        jnp.zeros((local_experts, model_width // shares, 2 * hidden_units), jnp.float32),
        cores_experts(gate_kept, gate_moved, split),
        0,
    )
    dense, up_moved, grad_gate_up = lax.optimization_barrier((dense, up_moved, grad_gate_up))
    grad_gate_up = place_experts(
        grad_gate_up, cores_experts(up_kept, up_moved, split), hidden_units
    )
    dense = finish_dense(dense, dense.shape[0] < w_query.shape[0] // shares)
    tail = edge + small.shape[1]
    return (
        y_prompt,
        y_cont,
        dx_prompt,
        dx_cont,
        dense[:, edge + expert_total],
        dense[:, :heads_width],
        dense[:, heads_width : heads_width + key_value_width],
        dense[:, heads_width + key_value_width : edge],
        dense[:, tail:],
        dense[:, edge + expert_total + 1],
        dense[:, edge : edge + expert_total],
        grad_gate_up,
        grad_down,
    )


def solution(mesh):
    return jax.shard_map(
        per_device,
        mesh=mesh,
        in_specs=(
            P(("dp", "expert"), "ctx", None),
            P(("dp", "expert"), "ctx", None, None),
            P(),
            P(),
            P(),
            P(),
            P(),
            P(),
            P(),
            P("expert", None, None),
            P("expert", None, None),
            P(("dp", "expert"), "ctx", None),
            P(("dp", "expert"), "ctx", None, None),
            P(("dp", "expert"), "ctx", None),
            P(("dp", "expert"), "ctx", None),
            P(("dp", "expert"), "ctx", None, None),
        ),
        out_specs=(
            P(("dp", "expert"), "ctx", None),
            P(("dp", "expert"), "ctx", None, None),
            P(("dp", "expert"), "ctx", None),
            P(("dp", "expert"), "ctx", None, None),
            P(("dp", "ctx")),
            P(("dp", "ctx"), None),
            P(("dp", "ctx"), None),
            P(("dp", "ctx"), None),
            P(("dp", "ctx"), None),
            P(("dp", "ctx")),
            P(("dp", "ctx"), None),
            P("expert", ("dp", "ctx"), None),
            P("expert", ("dp", "ctx"), None),
        ),
        check_vma=False,
    )
```
